32 devices in a mesh: slab: 8 (over y, x, core), grid: 4 (over z).
Axes of the slice: x: 2, y: 2, z: 4, core: 2. Of those that a mesh axis runs over, the one named last changes fastest.
Arguments:
- blocks: bfloat16 [8, 4, 16, 64, 4096], P('slab', 'grid')
- coords: int32 [8, 4, 16, 3], P('slab', 'grid'), may hold values from 0 to 15, as said below
- counts: int32 [8, 4], P('slab', 'grid'), may hold values from 2 to 16, as said below
- b_init: float32 [4096, 256], P(('slab', 'grid'))
- c_init: float32 [256, 256], replicated
Outputs:
- factor_a: float32 [8192, 256], P(('slab', 'grid'))
- factor_b: float32 [4096, 256], P(('slab', 'grid'))
- factor_c: float32 [256, 256], replicated
The draws below stay inside these ranges and needn't reach their ends.
Inputs may be any that keep to these rules, and one draw needn't show every extreme that they name: `coords`: column 0 is below 16, column 1 below 16, column 2 below 4; the 16 slots of one device name different blocks. Slots 0 to counts - 1 of a device hold its blocks and the other slots are padding; at least one device uses all 16 slots.
All inputs are finite; a program needn't handle non-finite values.
Results may differ from the reference program's by a relative error of at most 0.0007.
The reference program's roundings to bfloat16 on the way count: a program that leaves them out, or rounds other values in their place, can miss the bound.
Values may be sent and summed in bfloat16 or wider, within the bound.
No kernel may reach another device: no remote copies, remote signals or barrier semaphores. Data moves between devices by JAX's collectives and lax.ppermute only.
A program may use at most 64 MiB of HBM per device.

```python
import math
import jax
import jax.numpy as jnp
from jax import lax

W = 64
R = 256
KB = 4
IBP = 16
JBP = 16
NBD = 16
DOC_ROWS = 1024
TERM_ROWS = 1024
TERM_PIECE = 128
DOCS = 8192
TERMS = 4096
MONTHS = 256
N_SLAB = 8
N_GRID = 4


def draw_blocks(key, part):
    noise_key = jax.random.fold_in(key, 11)
    scale_key = jax.random.fold_in(key, 12)
    shape = (N_SLAB, N_GRID, NBD, W, W * W)
    device_total = N_SLAB * N_GRID
    ramp = 1.0 + 2.0 * jnp.arange(device_total, dtype=jnp.float32).reshape(N_SLAB, N_GRID, 1, 1, 1) / (device_total - 1)
    row_scale = jnp.exp(jax.random.uniform(scale_key, (N_SLAB, N_GRID, NBD, W, 1), dtype=jnp.float32) * math.log(10.0)) / 4.0
    values = jnp.clip(jax.random.normal(noise_key, shape, dtype=jnp.float32), -6.0, 6.0)
    return (values * row_scale * ramp).astype(jnp.bfloat16)


def factor_draw(key, rows):
    noise_key = jax.random.fold_in(key, 21)
    shared_key = jax.random.fold_in(key, 22)
    shared = jnp.clip(jax.random.normal(shared_key, (rows, 1), dtype=jnp.float32), -6.0, 6.0)
    values = jnp.clip(jax.random.normal(noise_key, (rows, R), dtype=jnp.float32), -6.0, 6.0)
    return values + 0.7 * shared


def draw_b_init(key, part):
    return factor_draw(key, TERMS).astype(jnp.float32)


def draw_c_init(key, part):
    return factor_draw(key, MONTHS).astype(jnp.float32)


def pick_positions(device_key):
    return jax.random.permutation(device_key, IBP * JBP * KB)[:NBD]


def draw_coords(key, part):
    device_keys = jax.random.split(jax.random.fold_in(key, 31), N_SLAB * N_GRID)
    picks = jax.vmap(pick_positions)(device_keys).astype(jnp.int32)
    doc_block = picks // (JBP * KB)
    term_block = picks // KB % JBP
    month_block = picks % KB
    stacked = jnp.stack([doc_block, term_block, month_block], axis=-1)
    return stacked.reshape(N_SLAB, N_GRID, NBD, 3).astype(jnp.int32)


def draw_counts(key, part):
    device_total = N_SLAB * N_GRID
    base = jax.random.randint(jax.random.fold_in(key, 41), (device_total,), 2, NBD // 2 + 2, dtype=jnp.int32)
    chosen = jax.random.randint(jax.random.fold_in(key, 42), (), 0, device_total, dtype=jnp.int32)
    filled = jnp.where(jnp.arange(device_total, dtype=jnp.int32) == chosen, NBD, base)
    return filled.reshape(N_SLAB, N_GRID).astype(jnp.int32)


def setup_inputs(seed: int = 0) -> dict:
    splits = jax.random.split(jax.random.key(seed), 6)
    return {
        "blocks": draw_blocks(jax.random.fold_in(splits[5], 71), 0),
        "coords": draw_coords(jax.random.fold_in(splits[5], 71), 0),
        "counts": draw_counts(jax.random.fold_in(splits[5], 71), 0),
        "b_init": draw_b_init(jax.random.fold_in(splits[5], 71), 0),
        "c_init": draw_c_init(jax.random.fold_in(splits[5], 71), 0),
    }


HIGH = lax.Precision.HIGHEST
EPS = 1e-05

def kr_rows(first_rows, second_rows):
    product = first_rows.astype(jnp.float32)[:, None, :] * second_rows.astype(jnp.float32)[None, :, :]
    return product.astype(jnp.bfloat16)

def fetch_panel(panels, panel_index, start):
    return lax.dynamic_slice(panels, (panel_index, start, jnp.int32(0)), (1, W, R))[0]

def fetch_months(month_rows, start):
    return lax.dynamic_slice(month_rows, (start, jnp.int32(0)), (W, R))

def all_moments(target_mode, blocks, coords, counts, doc_panels, term_panels, month_rows, out_shape):
    device_total = N_SLAB * N_GRID
    flat_blocks = blocks.reshape(device_total * NBD, W, W * W)
    flat_coords = coords.reshape(device_total * NBD, 3).astype(jnp.int32)
    order = jnp.arange(device_total * NBD, dtype=jnp.int32)
    device_ids = order // NBD
    live_mask = order % NBD < counts.reshape(-1).astype(jnp.int32)[device_ids]

    def visit(totals, item):
        single, offsets, device, live = item
        slab_at = device // N_GRID
        grid_at = device % N_GRID
        starts = offsets * W

        def compute():
            if target_mode == 0:
                outer = kr_rows(fetch_panel(term_panels, grid_at, starts[1]), fetch_months(month_rows, starts[2]))
                return jnp.dot(single.astype(jnp.float32), outer.reshape(W * W, R).astype(jnp.float32), precision=HIGH, preferred_element_type=jnp.float32)
            volume = single.astype(jnp.float32).reshape(W, W, W)
            if target_mode == 1:
                outer = kr_rows(fetch_panel(doc_panels, slab_at, starts[0]), fetch_months(month_rows, starts[2]))
                return jnp.einsum('ijk,ikr->jr', volume, outer.astype(jnp.float32), precision=HIGH)
            outer = kr_rows(fetch_panel(doc_panels, slab_at, starts[0]), fetch_panel(term_panels, grid_at, starts[1]))
            return jnp.einsum('ijk,ijr->kr', volume, outer.astype(jnp.float32), precision=HIGH)

        def nothing():
            return jnp.zeros((W, R), jnp.float32)
        contrib = lax.cond(live, compute, nothing)
        if target_mode == 2:
            index = (starts[2], jnp.int32(0))
            current = lax.dynamic_slice(totals, index, (W, R))
            totals = lax.dynamic_update_slice(totals, current + contrib, index)
        else:
            if target_mode == 0:
                index = (slab_at, starts[0], jnp.int32(0))
            else:
                index = (grid_at, starts[1], jnp.int32(0))
            current = lax.dynamic_slice(totals, index, (1, W, R))
            totals = lax.dynamic_update_slice(totals, current + contrib[None], index)
        return (totals, None)
    totals, unused = lax.scan(visit, jnp.zeros(out_shape, jnp.float32), (flat_blocks, flat_coords, device_ids, live_mask))
    return totals

def gram_of(factor):
    return jnp.dot(factor.T.astype(jnp.float32), factor.astype(jnp.float32), precision=HIGH, preferred_element_type=jnp.float32)

def solve_rows(moments, system):
    lower = jnp.linalg.cholesky(system)
    return jax.scipy.linalg.cho_solve((lower, True), moments.T).T

def unit_columns(raw_rows):
    column_scale = jnp.sqrt(lax.optimization_barrier(jnp.mean(raw_rows * raw_rows, axis=0)) + EPS)
    return raw_rows / column_scale

def to_term_panels(factor):
    shaped = factor.astype(jnp.bfloat16).reshape(N_SLAB, N_GRID, TERM_PIECE, R)
    return jnp.transpose(shaped, (1, 0, 2, 3)).reshape(N_GRID, TERM_ROWS, R)

def from_term_panels(panels):
    shaped = panels.reshape(N_GRID, N_SLAB, TERM_PIECE, R)
    return jnp.transpose(shaped, (1, 0, 2, 3)).reshape(TERMS, R)

def reference(blocks, coords, counts, b_init, c_init):
    gram_b = gram_of(b_init) / TERMS
    gram_c = gram_of(c_init) / MONTHS
    month_bf = c_init.astype(jnp.bfloat16)
    term_panels = to_term_panels(b_init)
    moments_a = all_moments(0, blocks, coords, counts, None, term_panels, month_bf, (N_SLAB, DOC_ROWS, R)).reshape(DOCS, R)
    factor_a = unit_columns(solve_rows(moments_a, gram_b * gram_c))
    gram_a = gram_of(factor_a) / DOCS
    doc_panels = factor_a.astype(jnp.bfloat16).reshape(N_SLAB, DOC_ROWS, R)
    moments_b = from_term_panels(all_moments(1, blocks, coords, counts, doc_panels, None, month_bf, (N_GRID, TERM_ROWS, R)))
    factor_b = unit_columns(solve_rows(moments_b, gram_a * gram_c))
    gram_bn = gram_of(factor_b) / TERMS
    moments_c = all_moments(2, blocks, coords, counts, doc_panels, to_term_panels(factor_b), None, (MONTHS, R))
    factor_c = unit_columns(solve_rows(moments_c, gram_a * gram_bn))
    return (factor_a, factor_b, factor_c)
```

```python
import functools

import jax
import jax.numpy as jnp
from jax import lax
from jax.experimental import pallas as pl
from jax.experimental.pallas import tpu as pltpu
from jax.sharding import PartitionSpec as P

W = 64
IBP = 16
JBP = 16
LANES = 128
GROUP = 4

HIGH = lax.Precision.HIGHEST
EPS = 1e-05
BOTH = ("slab", "grid")
F32 = jnp.float32
BF16 = jnp.bfloat16


def product_rows(first, second, start):
    rank = first.shape[1]
    pieces = []
    for row in range(start, start + GROUP):
        spread = jnp.broadcast_to(first[row : row + 1, :], (16, rank)).astype(BF16)
        pieces.append((second * spread[None]).reshape(W, rank))
    return jnp.concatenate(pieces, 0)


def slot_rows(coords_ref, slot, mode):
    return pl.multiple_of(coords_ref[slot * 3 + mode] * W, W)


def moments_kernel(mode, count_ref, coords_ref, blocks_ref, first_ref, second_ref, out_ref, *scratch):
    slot = pl.program_id(0)
    rank = out_ref.shape[1]

    @pl.when(slot == 0)
    def _():
        out_ref[...] = jnp.zeros_like(out_ref)

    spread_mode, tile_mode = ((1, 2), (0, 2), (1, 0))[mode]

    @pl.when(slot < count_ref[0])
    def _():
        first = first_ref[pl.ds(slot_rows(coords_ref, slot, spread_mode), W), :].astype(F32)
        second = second_ref[pl.ds(slot_rows(coords_ref, slot, tile_mode), W), :].reshape(4, 16, rank)
        target = slot_rows(coords_ref, slot, mode)
        total = jnp.zeros((W, rank), F32)
        if mode == 1:
            lanes_ref, order_ref = scratch
            columns = W * W // LANES
            for column in range(columns):
                lanes_ref[pl.ds(column, W, stride=columns), :] = blocks_ref[
                    0, :, column * LANES : (column + 1) * LANES
                ].astype(F32)
            low = lax.broadcasted_iota(jnp.int32, (columns, LANES), 1) < W
        for step in range(W // GROUP):
            right = product_rows(first, second, step * GROUP)
            if mode == 0:
                left = blocks_ref[0, :, step * GROUP * W : (step + 1) * GROUP * W]
            elif mode == 1:
                parts = []
                for pair in range(GROUP // 2):
                    row = step * GROUP + 2 * pair
                    one = lanes_ref[row * columns : (row + 1) * columns, :]
                    two = lanes_ref[(row + 1) * columns : (row + 2) * columns, :]
                    even = jnp.where(low, one, pltpu.roll(two, W, 1)).astype(BF16)
                    odd = jnp.where(low, pltpu.roll(one, W, 1), two).astype(BF16)
                    parts.append(jnp.concatenate([even, odd], 0))
                left = jnp.concatenate(parts, 1)
            else:
                parts = []
                for pair in range(GROUP // 2):
                    column = step * GROUP // 2 + pair
                    turned = blocks_ref[0, :, column * LANES : (column + 1) * LANES].T
                    parts += [turned[:W], turned[W:]]
                left = jnp.concatenate(parts, 1)
            total = total + jnp.dot(left, right, preferred_element_type=F32)
        if mode == 1:
            halves = []
            for part in range(rank // LANES):
                for parity in range(2):
                    order_ref[part, pl.ds(parity, W // 2, stride=2), :] = total[
                        parity * W // 2 : (parity + 1) * W // 2, part * LANES : (part + 1) * LANES
                    ]
                halves.append(order_ref[part])
            total = jnp.concatenate(halves, 1)
        out_ref[pl.ds(target, W), :] += total


def block_moments(mode, blocks, coords, count, first, second, out_rows):
    slots = blocks.shape[0]
    rank = first.shape[1]
    scratch = []
    if mode == 1:
        scratch = [
            pltpu.VMEM((W * W * W // LANES, LANES), F32),
            pltpu.VMEM((rank // LANES, W, LANES), F32),
        ]
    whole = lambda slot, count_ref, coords_ref: (0, 0)
    spec = pltpu.PrefetchScalarGridSpec(
        num_scalar_prefetch=2,
        grid=(slots,),
        in_specs=[
            pl.BlockSpec(
                (1, W, W * W),
                lambda slot, count_ref, coords_ref: (jnp.minimum(slot, count_ref[0] - 1), 0, 0),
            ),
            pl.BlockSpec(first.shape, whole),
            pl.BlockSpec(second.shape, whole),
        ],
        out_specs=pl.BlockSpec((out_rows, rank), whole),
        scratch_shapes=scratch,
    )
    return pl.pallas_call(
        functools.partial(moments_kernel, mode),
        grid_spec=spec,
        out_shape=jax.ShapeDtypeStruct((out_rows, rank), F32),
        compiler_params=pltpu.CompilerParams(vmem_limit_bytes=40 << 20),
        cost_estimate=pl.CostEstimate(
            flops=2 * slots * W**3 * rank, bytes_accessed=blocks.size * 2, transcendentals=0
        ),
    )(count, coords, blocks, first, second)


def scatter_sum(rows, axes):
    parts = lax.all_to_all(rows, axes, split_axis=0, concat_axis=0, tiled=True)
    devices = lax.axis_size(axes)
    return jnp.sum(parts.reshape(devices, rows.shape[0] // devices, rows.shape[1]), axis=0)


def spread_rows(rows, axes):
    devices = lax.axis_size(axes)
    return lax.all_to_all(jnp.tile(rows, (devices, 1)), axes, split_axis=0, concat_axis=0, tiled=True)


def total_sum(square):
    return spread_rows(scatter_sum(square, BOTH), BOTH)


def gram_local(factor):
    return jnp.dot(factor.T, factor, precision=HIGH, preferred_element_type=F32)


def solve_rows(moments, system):
    lower = jnp.linalg.cholesky(system)
    return jax.scipy.linalg.cho_solve((lower, True), moments.T).T


def scale_and_gram(gram_raw, row_total):
    mean_gram = gram_raw / row_total
    column_scale = jnp.sqrt(jnp.diagonal(mean_gram) + EPS)
    return column_scale, mean_gram / (column_scale[:, None] * column_scale[None, :])


def on_device(blocks, coords, counts, b_init, c_init):
    slab_count = lax.axis_size("slab")
    grid_count = lax.axis_size("grid")
    local_blocks = blocks[0, 0]
    local_coords = coords.reshape(-1)
    filled = counts.reshape(-1)
    doc_rows = IBP * W
    term_rows = JBP * W
    doc_total = doc_rows * slab_count
    term_total = term_rows * grid_count
    month_total = c_init.shape[0]
    month_bf = c_init.astype(BF16)
    gram_c = gram_local(c_init) / month_total
    gram_b = total_sum(gram_local(b_init)) / term_total
    term_panel = lax.all_gather(b_init.astype(BF16), "slab", axis=0, tiled=True)
    moments_a = block_moments(0, local_blocks, local_coords, filled, term_panel, month_bf, doc_rows)
    own_a = scatter_sum(moments_a, "grid")
    raw_a = solve_rows(own_a, gram_b * gram_c)
    scale_a, gram_a = scale_and_gram(total_sum(gram_local(raw_a)), doc_total)
    factor_a = raw_a / scale_a
    doc_panel = lax.all_gather(factor_a.astype(BF16), "grid", axis=0, tiled=True)
    moments_b = block_moments(1, local_blocks, local_coords, filled, doc_panel, month_bf, term_rows)
    own_b = scatter_sum(moments_b, "slab")
    raw_b = solve_rows(own_b, gram_a * gram_c)
    scale_b, gram_bn = scale_and_gram(total_sum(gram_local(raw_b)), term_total)
    factor_b = raw_b / scale_b
    term_panel_new = lax.all_gather(factor_b.astype(BF16), "slab", axis=0, tiled=True)
    moments_c = block_moments(
        2, local_blocks, local_coords, filled, term_panel_new, doc_panel, month_total
    )
    raw_c = solve_rows(total_sum(moments_c), gram_a * gram_bn)
    column_scale = jnp.sqrt(jnp.mean(raw_c * raw_c, axis=0) + EPS)
    return (factor_a, factor_b, raw_c / column_scale)


def solution(mesh):
    in_specs = (
        P("slab", "grid", None, None, None),
        P("slab", "grid", None, None),
        P("slab", "grid"),
        P(("slab", "grid"), None),
        P(),
    )
    out_specs = (P(("slab", "grid"), None), P(("slab", "grid"), None), P())
    return jax.shard_map(
        on_device, mesh=mesh, in_specs=in_specs, out_specs=out_specs, check_vma=False
    )
```

```python
import functools

import jax
import jax.numpy as jnp
from jax import lax
from jax.experimental import pallas as pl
from jax.experimental.pallas import tpu as pltpu
from jax.sharding import PartitionSpec as P

W = 64
IBP = 16
JBP = 16
LANES = 128
PANEL = 128
GROUP = 4

HIGH = lax.Precision.HIGHEST
EPS = 1e-05
BOTH = ("slab", "grid")
F32 = jnp.float32
BF16 = jnp.bfloat16


def product_rows(first, second, start):
    rank = first.shape[1]
    pieces = []
    for row in range(start, start + GROUP):
        spread = jnp.broadcast_to(first[row : row + 1, :], (16, rank)).astype(BF16)
        pieces.append((second * spread[None]).reshape(W, rank))
    return jnp.concatenate(pieces, 0)


def slot_rows(coords_ref, slot, mode):
    return pl.multiple_of(coords_ref[slot * 3 + mode] * W, W)


def moments_kernel(mode, count_ref, coords_ref, blocks_ref, first_ref, second_ref, out_ref, *scratch):
    slot = pl.program_id(0)
    rank = out_ref.shape[1]

    @pl.when(slot == 0)
    def _():
        out_ref[...] = jnp.zeros_like(out_ref)

    spread_mode, tile_mode = ((1, 2), (0, 2), (1, 0))[mode]

    @pl.when(slot < count_ref[0])
    def _():
        first = first_ref[pl.ds(slot_rows(coords_ref, slot, spread_mode), W), :].astype(F32)
        second = second_ref[pl.ds(slot_rows(coords_ref, slot, tile_mode), W), :].reshape(4, 16, rank)
        target = slot_rows(coords_ref, slot, mode)
        total = jnp.zeros((W, rank), F32)
        if mode == 1:
            lanes_ref, order_ref = scratch
            columns = W * W // LANES
            for column in range(columns):
                lanes_ref[pl.ds(column, W, stride=columns), :] = blocks_ref[
                    0, :, column * LANES : (column + 1) * LANES
                ].astype(F32)
            low = lax.broadcasted_iota(jnp.int32, (columns, LANES), 1) < W
        for step in range(W // GROUP):
            right = product_rows(first, second, step * GROUP)
            if mode == 0:
                left = blocks_ref[0, :, step * GROUP * W : (step + 1) * GROUP * W]
            elif mode == 1:
                parts = []
                for pair in range(GROUP // 2):
                    row = step * GROUP + 2 * pair
                    one = lanes_ref[row * columns : (row + 1) * columns, :]
                    two = lanes_ref[(row + 1) * columns : (row + 2) * columns, :]
                    even = jnp.where(low, one, pltpu.roll(two, W, 1)).astype(BF16)
                    odd = jnp.where(low, pltpu.roll(one, W, 1), two).astype(BF16)
                    parts.append(jnp.concatenate([even, odd], 0))
                left = jnp.concatenate(parts, 1)
            else:
                parts = []
                for pair in range(GROUP // 2):
                    column = step * GROUP // 2 + pair
                    turned = blocks_ref[0, :, column * LANES : (column + 1) * LANES].T
                    parts += [turned[:W], turned[W:]]
                left = jnp.concatenate(parts, 1)
            total = total + jnp.dot(left, right, preferred_element_type=F32)
        if mode == 1:
            halves = []
            for part in range(rank // LANES):
                for parity in range(2):
                    order_ref[part, pl.ds(parity, W // 2, stride=2), :] = total[
                        parity * W // 2 : (parity + 1) * W // 2, part * LANES : (part + 1) * LANES
                    ]
                halves.append(order_ref[part])
            total = jnp.concatenate(halves, 1)
        out_ref[pl.ds(target, W), :] += total


def block_moments(mode, blocks, coords, count, first, second, out_rows):
    slots = blocks.shape[0]
    rank = first.shape[1]
    scratch = []
    if mode == 1:
        scratch = [
            pltpu.VMEM((W * W * W // LANES, LANES), F32),
            pltpu.VMEM((rank // LANES, W, LANES), F32),
        ]
    whole = lambda slot, count_ref, coords_ref: (0, 0)
    spec = pltpu.PrefetchScalarGridSpec(
        num_scalar_prefetch=2,
        grid=(slots,),
        in_specs=[
            pl.BlockSpec(
                (1, W, W * W),
                lambda slot, count_ref, coords_ref: (jnp.minimum(slot, count_ref[0] - 1), 0, 0),
            ),
            pl.BlockSpec(first.shape, whole),
            pl.BlockSpec(second.shape, whole),
        ],
        out_specs=pl.BlockSpec((out_rows, rank), whole),
        scratch_shapes=scratch,
    )
    return pl.pallas_call(
        functools.partial(moments_kernel, mode),
        grid_spec=spec,
        out_shape=jax.ShapeDtypeStruct((out_rows, rank), F32),
        compiler_params=pltpu.CompilerParams(vmem_limit_bytes=40 << 20),
        cost_estimate=pl.CostEstimate(
            flops=2 * slots * W**3 * rank, bytes_accessed=blocks.size * 2, transcendentals=0
        ),
    )(count, coords, blocks, first, second)


def exchange(rows, axes):
    devices = lax.axis_size(axes)
    parts = lax.all_to_all(rows, axes, split_axis=0, concat_axis=0, tiled=True)
    return parts.reshape(devices, rows.shape[0] // devices, rows.shape[1])


def spread_rows(rows, axes):
    devices = lax.axis_size(axes)
    return lax.all_to_all(jnp.tile(rows, (devices, 1)), axes, split_axis=0, concat_axis=0, tiled=True)


def total_sum(square):
    return spread_rows(jnp.sum(exchange(square, BOTH), axis=0), BOTH)


def gram_local(factor):
    return jnp.dot(factor.T, factor, precision=HIGH, preferred_element_type=F32)


def exact_dot(left, right, contract):
    return lax.dot_general(left, right, (contract, ((), ())), precision=HIGH, preferred_element_type=F32)


def across_lanes(tile, lane):
    return jnp.broadcast_to(tile[:, lane : lane + 1], tile.shape)


def across_rows(tile, row):
    return jnp.broadcast_to(tile[row : row + 1, :], tile.shape)


def tree_sum(terms):
    while len(terms) > 1:
        terms = [a + b for a, b in zip(terms[::2], terms[1::2])]
    return terms[0]


def sweep_corner(entries):
    for k in range(0, 8, 2):
        at = lambda i, j: entries[(min(i, j), max(i, j))]
        a, o, d = at(k, k), at(k, k + 1), at(k + 1, k + 1)
        inverse = 1.0 / (a * d - o * o)
        w00, w01, w11 = d * inverse, -(o * inverse), a * inverse
        rest = [j for j in range(8) if j not in (k, k + 1)]
        top = {j: w00 * at(k, j) + w01 * at(k + 1, j) for j in rest}
        low = {j: w01 * at(k, j) + w11 * at(k + 1, j) for j in rest}
        swept = {(k, k): -w00, (k, k + 1): -w01, (k + 1, k + 1): -w11}
        for i in rest:
            swept[(min(k, i), max(k, i))] = top[i]
            swept[(min(k + 1, i), max(k + 1, i))] = low[i]
            for j in rest:
                if i <= j:
                    swept[(i, j)] = at(i, j) - (at(k, i) * top[j] + at(k + 1, i) * low[j])
        entries = swept
    return entries


def panel_inverse(tiles):
    shape = tiles[0].shape
    lane = lax.broadcasted_iota(jnp.int32, shape, 1)
    row = lax.broadcasted_iota(jnp.int32, shape, 0)
    for pivot in range(len(tiles)):
        tile = tiles[pivot]
        first = 8 * pivot
        columns = [across_lanes(tile, first + j) for j in range(8)]
        corner = sweep_corner({(i, j): across_rows(columns[j], i) for j in range(8) for i in range(j + 1)})
        here = (lane >= first) & (lane < first + 8)
        turned = jnp.where(here, jnp.where(lane - first == row, 1.0, 0.0), -tile)
        rows = [across_rows(turned, i) for i in range(8)]
        scaled = [tree_sum([corner[(min(i, j), max(i, j))] * rows[j] for j in range(8)]) for i in range(8)]
        swept = []
        for other, held in enumerate(tiles):
            if other == pivot:
                mine = scaled[0]
                for i in range(1, 8):
                    mine = jnp.where(row == i, scaled[i], mine)
            else:
                change = tree_sum([across_lanes(held, first + j) * scaled[j] for j in range(8)])
                mine = jnp.where(here, 0.0, held) - change
            swept.append(mine)
        tiles = swept
    return -jnp.concatenate(tiles, 0)


def inverse_kernel(one_ref, two_ref, out_ref, held_ref):
    size = held_ref.shape[0]
    system = one_ref[...] * two_ref[...]
    shape = (size, size)
    on_diagonal = lax.broadcasted_iota(jnp.int32, shape, 0) == lax.broadcasted_iota(jnp.int32, shape, 1)
    diagonal = jnp.where(on_diagonal, system, 0.0)
    across = lax.rsqrt(jnp.sum(diagonal, 0, keepdims=True))
    down = lax.rsqrt(jnp.sum(diagonal, 1, keepdims=True))
    held_ref[...] = system * across * down
    here = lax.broadcasted_iota(jnp.int32, (1, size), 1) < PANEL
    rest = size - PANEL

    def eliminate(step, carry):
        pivot = panel_inverse([held_ref[8 * g : 8 * g + 8, :PANEL] for g in range(PANEL // 8)])
        rows = held_ref[:PANEL, :]
        scaled = exact_dot(pivot, rows, ((1,), (0,)))
        minus = jnp.concatenate([-pivot, jnp.zeros((PANEL, rest), F32)], 1)
        scaled = jnp.where(here, minus, scaled)
        others = jnp.where(here, 0.0, held_ref[PANEL:, :]) - exact_dot(
            rows[:, PANEL:], scaled, ((0,), (0,))
        )
        held_ref[:rest, :] = pltpu.roll(others, rest, 1)
        held_ref[rest:, :] = pltpu.roll(scaled, rest, 1)
        return carry

    lax.fori_loop(0, size // PANEL, eliminate, 0)
    out_ref[...] = -held_ref[...] * across * down


def product_inverse(one, two):
    return pl.pallas_call(
        inverse_kernel,
        out_shape=jax.ShapeDtypeStruct(one.shape, F32),
        scratch_shapes=[pltpu.VMEM(one.shape, F32)],
        compiler_params=pltpu.CompilerParams(vmem_limit_bytes=16 << 20),
        cost_estimate=pl.CostEstimate(flops=6 * one.shape[0] ** 3 * 40, bytes_accessed=3 * one.size * 4, transcendentals=0),
    )(one, two)


def solve_kernel(parts_ref, inverse_ref, raw_ref, *gram_ref):
    moments = parts_ref[0]
    for part in range(1, parts_ref.shape[0]):
        moments = moments + parts_ref[part]
    raw = exact_dot(moments, inverse_ref[...], ((1,), (0,)))
    raw_ref[...] = raw
    if gram_ref:
        gram_ref[0][...] = exact_dot(raw, raw, ((0,), (0,)))


def solve_rows(parts, inverse, with_gram):
    rows, rank = parts.shape[1:]
    out_shape = [jax.ShapeDtypeStruct((rows, rank), F32)]
    if with_gram:
        out_shape.append(jax.ShapeDtypeStruct((rank, rank), F32))
    return pl.pallas_call(
        solve_kernel,
        out_shape=out_shape,
        compiler_params=pltpu.CompilerParams(vmem_limit_bytes=16 << 20),
    )(parts, inverse)


def scale_kernel(row_total, total_ref, raw_ref, factor_ref, rounded_ref, gram_ref):
    mean = total_ref[...] / row_total
    shape = mean.shape
    on_diagonal = lax.broadcasted_iota(jnp.int32, shape, 0) == lax.broadcasted_iota(jnp.int32, shape, 1)
    diagonal = jnp.where(on_diagonal, mean, 0.0)
    across = jnp.sqrt(jnp.sum(diagonal, 0, keepdims=True) + EPS)
    down = jnp.sqrt(jnp.sum(diagonal, 1, keepdims=True) + EPS)
    gram_ref[...] = mean / across / down
    factor = raw_ref[...] / across
    factor_ref[...] = factor
    rounded_ref[...] = factor.astype(BF16)


def scale_rows(gram_total, raw, row_total):
    return pl.pallas_call(
        functools.partial(scale_kernel, row_total),
        out_shape=[
            jax.ShapeDtypeStruct(raw.shape, F32),
            jax.ShapeDtypeStruct(raw.shape, BF16),
            jax.ShapeDtypeStruct(gram_total.shape, F32),
        ],
        compiler_params=pltpu.CompilerParams(vmem_limit_bytes=16 << 20),
    )(gram_total, raw)


def on_device(blocks, coords, counts, b_init, c_init):
    slab_count = lax.axis_size("slab")
    grid_count = lax.axis_size("grid")
    local_blocks = blocks[0, 0]
    local_coords = coords.reshape(-1)
    filled = counts.reshape(-1)
    doc_rows = IBP * W
    term_rows = JBP * W
    doc_total = doc_rows * slab_count
    term_total = term_rows * grid_count
    month_total = c_init.shape[0]
    month_bf = c_init.astype(BF16)
    gram_c = gram_local(c_init) / month_total
    gram_b = total_sum(gram_local(b_init)) / term_total
    term_panel = lax.all_gather(b_init.astype(BF16), "slab", axis=0, tiled=True)
    moments_a = block_moments(0, local_blocks, local_coords, filled, term_panel, month_bf, doc_rows)
    parts_a = exchange(moments_a, "grid")
    inverse_a = product_inverse(gram_b, gram_c)
    raw_a, own_gram_a = solve_rows(parts_a, inverse_a, True)
    factor_a, rounded_a, gram_a = scale_rows(total_sum(own_gram_a), raw_a, doc_total)
    doc_panel = lax.all_gather(rounded_a, "grid", axis=0, tiled=True)
    moments_b = block_moments(1, local_blocks, local_coords, filled, doc_panel, month_bf, term_rows)
    parts_b = exchange(moments_b, "slab")
    inverse_b = product_inverse(gram_a, gram_c)
    raw_b, own_gram_b = solve_rows(parts_b, inverse_b, True)
    factor_b, rounded_b, gram_bn = scale_rows(total_sum(own_gram_b), raw_b, term_total)
    term_panel_new = lax.all_gather(rounded_b, "slab", axis=0, tiled=True)
    moments_c = block_moments(
        2, local_blocks, local_coords, filled, term_panel_new, doc_panel, month_total
    )
    parts_c = exchange(moments_c, BOTH)
    inverse_c = product_inverse(gram_a, gram_bn)
    (raw_own,) = solve_rows(parts_c, inverse_c, False)
    raw_c = spread_rows(raw_own, BOTH)
    column_scale = jnp.sqrt(jnp.mean(raw_c * raw_c, axis=0) + EPS)
    return (factor_a, factor_b, raw_c / column_scale)


def solution(mesh):
    in_specs = (
        P("slab", "grid", None, None, None),
        P("slab", "grid", None, None),
        P("slab", "grid"),
        P(("slab", "grid"), None),
        P(),
    )
    out_specs = (P(("slab", "grid"), None), P(("slab", "grid"), None), P())
    return jax.shard_map(
        on_device, mesh=mesh, in_specs=in_specs, out_specs=out_specs, check_vma=False
    )
```

```python
import functools

import jax
import jax.numpy as jnp
from jax import lax
from jax.experimental import pallas as pl
from jax.experimental.pallas import tpu as pltpu
from jax.sharding import PartitionSpec as P

W = 64
IBP = 16
JBP = 16
LANES = 128
PANEL = 128
GROUP = 4

HIGH = lax.Precision.HIGHEST
EPS = 1e-05
BOTH = ("slab", "grid")
F32 = jnp.float32
BF16 = jnp.bfloat16


def product_rows(first, second, start):
    rank = first.shape[1]
    pieces = []
    for row in range(start, start + GROUP):
        spread = jnp.broadcast_to(first[row : row + 1, :], (16, rank)).astype(BF16)
        pieces.append((second * spread[None]).reshape(W, rank))
    return jnp.concatenate(pieces, 0)


def slot_rows(coords_ref, slot, mode, order):
    block = coords_ref[slot * 3 + mode]
    if order is not None:
        each = IBP // lax.axis_size(order)
        block = ((block // each) ^ lax.axis_index(order)) * each + block % each
    return pl.multiple_of(block * W, W)


def moments_kernel(mode, orders, count_ref, coords_ref, blocks_ref, first_ref, second_ref, out_ref, *scratch):
    slot = pl.program_id(0)
    rank = out_ref.shape[1]

    @pl.when(slot == 0)
    def _():
        out_ref[...] = jnp.zeros_like(out_ref)

    spread_mode, tile_mode = ((1, 2), (0, 2), (1, 0))[mode]

    @pl.when(slot < count_ref[0])
    def _():
        first = first_ref[pl.ds(slot_rows(coords_ref, slot, spread_mode, orders[0]), W), :].astype(F32)
        second = second_ref[pl.ds(slot_rows(coords_ref, slot, tile_mode, orders[1]), W), :].reshape(4, 16, rank)
        target = slot_rows(coords_ref, slot, mode, orders[2])
        total = jnp.zeros((W, rank), F32)
        if mode == 1:
            lanes_ref, order_ref = scratch
            columns = W * W // LANES
            for column in range(columns):
                lanes_ref[pl.ds(column, W, stride=columns), :] = blocks_ref[
                    0, :, column * LANES : (column + 1) * LANES
                ].astype(F32)
            low = lax.broadcasted_iota(jnp.int32, (columns, LANES), 1) < W
        for step in range(W // GROUP):
            right = product_rows(first, second, step * GROUP)
            if mode == 0:
                left = blocks_ref[0, :, step * GROUP * W : (step + 1) * GROUP * W]
            elif mode == 1:
                parts = []
                for pair in range(GROUP // 2):
                    row = step * GROUP + 2 * pair
                    one = lanes_ref[row * columns : (row + 1) * columns, :]
                    two = lanes_ref[(row + 1) * columns : (row + 2) * columns, :]
                    even = jnp.where(low, one, pltpu.roll(two, W, 1)).astype(BF16)
                    odd = jnp.where(low, pltpu.roll(one, W, 1), two).astype(BF16)
                    parts.append(jnp.concatenate([even, odd], 0))
                left = jnp.concatenate(parts, 1)
            else:
                parts = []
                for pair in range(GROUP // 2):
                    column = step * GROUP // 2 + pair
                    turned = blocks_ref[0, :, column * LANES : (column + 1) * LANES].T
                    parts += [turned[:W], turned[W:]]
                left = jnp.concatenate(parts, 1)
            total = total + jnp.dot(left, right, preferred_element_type=F32)
        if mode == 1:
            halves = []
            for part in range(rank // LANES):
                for parity in range(2):
                    order_ref[part, pl.ds(parity, W // 2, stride=2), :] = total[
                        parity * W // 2 : (parity + 1) * W // 2, part * LANES : (part + 1) * LANES
                    ]
                halves.append(order_ref[part])
            total = jnp.concatenate(halves, 1)
        out_ref[pl.ds(target, W), :] += total


def block_moments(mode, orders, blocks, coords, count, first, second, out_rows):
    slots = blocks.shape[0]
    rank = first.shape[1]
    scratch = []
    if mode == 1:
        scratch = [
            pltpu.VMEM((W * W * W // LANES, LANES), F32),
            pltpu.VMEM((rank // LANES, W, LANES), F32),
        ]
    whole = lambda slot, count_ref, coords_ref: (0, 0)
    spec = pltpu.PrefetchScalarGridSpec(
        num_scalar_prefetch=2,
        grid=(slots,),
        in_specs=[
            pl.BlockSpec(
                (1, W, W * W),
                lambda slot, count_ref, coords_ref: (jnp.minimum(slot, count_ref[0] - 1), 0, 0),
            ),
            pl.BlockSpec(first.shape, whole),
            pl.BlockSpec(second.shape, whole),
        ],
        out_specs=pl.BlockSpec((out_rows, rank), whole),
        scratch_shapes=scratch,
    )
    return pl.pallas_call(
        functools.partial(moments_kernel, mode, orders),
        grid_spec=spec,
        out_shape=jax.ShapeDtypeStruct((out_rows, rank), F32),
        compiler_params=pltpu.CompilerParams(vmem_limit_bytes=14 << 20),
        cost_estimate=pl.CostEstimate(
            flops=2 * slots * W**3 * rank, bytes_accessed=blocks.size * 2, transcendentals=0
        ),
    )(count, coords, blocks, first, second)


def exchange(rows, axes):
    devices = lax.axis_size(axes)
    parts = lax.all_to_all(rows, axes, split_axis=0, concat_axis=0, tiled=True)
    return parts.reshape(devices, rows.shape[0] // devices, rows.shape[1])


def spread_rows(rows, axes):
    devices = lax.axis_size(axes)
    return lax.all_to_all(jnp.tile(rows, (devices, 1)), axes, split_axis=0, concat_axis=0, tiled=True)


def total_sum(square):
    return spread_rows(jnp.sum(exchange(square, BOTH), axis=0), BOTH)


def swap(rows, axis, step):
    return lax.ppermute(rows, axis, [(i, i ^ step) for i in range(lax.axis_size(axis))])


def swap_pieces(rows, axis):
    devices = lax.axis_size(axis)
    each = rows.shape[0] // devices
    return [swap(rows[k * each : (k + 1) * each], axis, k) for k in range(1, devices)]


def swap_gather(rows, axis):
    return jnp.concatenate([rows] + [swap(rows, axis, k) for k in range(1, lax.axis_size(axis))], 0)


def gram_local(factor):
    return jnp.dot(factor.T, factor, precision=HIGH, preferred_element_type=F32)


def exact_dot(left, right, contract):
    return lax.dot_general(left, right, (contract, ((), ())), precision=HIGH, preferred_element_type=F32)


def across_lanes(tile, lane):
    return jnp.broadcast_to(tile[:, lane : lane + 1], tile.shape)


def across_rows(tile, row):
    return jnp.broadcast_to(tile[row : row + 1, :], tile.shape)


def tree_sum(terms):
    while len(terms) > 1:
        terms = [a + b for a, b in zip(terms[::2], terms[1::2])]
    return terms[0]


def sweep_corner(entries):
    for k in range(0, 8, 2):
        at = lambda i, j: entries[(min(i, j), max(i, j))]
        a, o, d = at(k, k), at(k, k + 1), at(k + 1, k + 1)
        inverse = 1.0 / (a * d - o * o)
        w00, w01, w11 = d * inverse, -(o * inverse), a * inverse
        rest = [j for j in range(8) if j not in (k, k + 1)]
        top = {j: w00 * at(k, j) + w01 * at(k + 1, j) for j in rest}
        low = {j: w01 * at(k, j) + w11 * at(k + 1, j) for j in rest}
        swept = {(k, k): -w00, (k, k + 1): -w01, (k + 1, k + 1): -w11}
        for i in rest:
            swept[(min(k, i), max(k, i))] = top[i]
            swept[(min(k + 1, i), max(k + 1, i))] = low[i]
            for j in rest:
                if i <= j:
                    swept[(i, j)] = at(i, j) - (at(k, i) * top[j] + at(k + 1, i) * low[j])
        entries = swept
    return entries


def panel_inverse(tiles):
    shape = tiles[0].shape
    lane = lax.broadcasted_iota(jnp.int32, shape, 1)
    row = lax.broadcasted_iota(jnp.int32, shape, 0)
    for pivot in range(len(tiles)):
        tile = tiles[pivot]
        first = 8 * pivot
        columns = [across_lanes(tile, first + j) for j in range(8)]
        corner = sweep_corner({(i, j): across_rows(columns[j], i) for j in range(8) for i in range(j + 1)})
        here = (lane >= first) & (lane < first + 8)
        turned = jnp.where(here, jnp.where(lane - first == row, 1.0, 0.0), -tile)
        rows = [across_rows(turned, i) for i in range(8)]
        scaled = [tree_sum([corner[(min(i, j), max(i, j))] * rows[j] for j in range(8)]) for i in range(8)]
        swept = []
        for other, held in enumerate(tiles):
            if other == pivot:
                mine = scaled[0]
                for i in range(1, 8):
                    mine = jnp.where(row == i, scaled[i], mine)
            else:
                change = tree_sum([across_lanes(held, first + j) * scaled[j] for j in range(8)])
                mine = jnp.where(here, 0.0, held) - change
            swept.append(mine)
        tiles = swept
    return -jnp.concatenate(tiles, 0)


def on_diagonal(size):
    shape = (size, size)
    return lax.broadcasted_iota(jnp.int32, shape, 0) == lax.broadcasted_iota(jnp.int32, shape, 1)


def turned_down(across, diagonal):
    return jnp.sum(jnp.where(diagonal, across, 0.0), 1, keepdims=True)


def inverse_kernel(totals, one_ref, one_scale_ref, two_ref, two_scale_ref, out_ref, held_ref):
    size = held_ref.shape[0]
    diagonal = on_diagonal(size)
    system = None
    for total, gram_ref, scale_ref in zip(totals, (one_ref, two_ref), (one_scale_ref, two_scale_ref)):
        inverse_scale = 1.0 / scale_ref[...]
        gram = gram_ref[...] * (inverse_scale / total) * turned_down(inverse_scale, diagonal)
        system = gram if system is None else system * gram
    across = lax.rsqrt(jnp.sum(jnp.where(diagonal, system, 0.0), 0, keepdims=True))
    down = turned_down(across, diagonal)
    held_ref[...] = system * across * down
    here = lax.broadcasted_iota(jnp.int32, (1, size), 1) < PANEL
    rest = size - PANEL

    def eliminate(step, carry):
        pivot = panel_inverse([held_ref[8 * g : 8 * g + 8, :PANEL] for g in range(PANEL // 8)])
        rows = held_ref[:PANEL, :]
        scaled = exact_dot(pivot, rows, ((1,), (0,)))
        minus = jnp.concatenate([-pivot, jnp.zeros((PANEL, rest), F32)], 1)
        scaled = jnp.where(here, minus, scaled)
        others = jnp.where(here, 0.0, held_ref[PANEL:, :]) - exact_dot(
            rows[:, PANEL:], scaled, ((0,), (0,))
        )
        held_ref[:rest, :] = pltpu.roll(others, rest, 1)
        held_ref[rest:, :] = pltpu.roll(scaled, rest, 1)
        return carry

    lax.fori_loop(0, size // PANEL, eliminate, 0)
    out_ref[...] = -held_ref[...] * across * down


def product_inverse(one, two):
    shape = one[0].shape
    return pl.pallas_call(
        functools.partial(inverse_kernel, (one[1], two[1])),
        out_shape=jax.ShapeDtypeStruct(shape, F32),
        scratch_shapes=[pltpu.VMEM(shape, F32)],
        compiler_params=pltpu.CompilerParams(vmem_limit_bytes=10 << 20),
        cost_estimate=pl.CostEstimate(flops=10**10, bytes_accessed=3 << 18, transcendentals=0),
    )(one[0], one[2], two[0], two[2])


def solve_kernel(stacked, parts, *refs):
    inverse_ref, outs = refs[parts], refs[parts + 1 :]
    if stacked:
        terms = [refs[0][part] for part in range(refs[0].shape[0])]
    else:
        terms = [ref[...] for ref in refs[:parts]]
    raw = exact_dot(functools.reduce(jnp.add, terms), inverse_ref[...], ((1,), (0,)))
    outs[0][...] = raw
    if len(outs) > 1:
        outs[1][...] = exact_dot(raw, raw, ((0,), (0,)))
        outs[2][...] = jnp.broadcast_to(jnp.sum(raw * raw, 0, keepdims=True), outs[2].shape)


def solve_swapped(own, others, inverse, devices):
    rows, rank = others[0].shape
    whole = pl.BlockSpec((rows, rank), lambda step: (0, 0))
    square = pl.BlockSpec((rank, rank), lambda step: (0, 0))
    return pl.pallas_call(
        functools.partial(solve_kernel, False, 1 + len(others)),
        grid=(1,),
        in_specs=[whole] * (1 + len(others)) + [square],
        out_specs=[whole, square, pl.BlockSpec((devices, rank), lambda step: (0, 0))],
        out_shape=[
            jax.ShapeDtypeStruct((rows, rank), F32),
            jax.ShapeDtypeStruct((rank, rank), F32),
            jax.ShapeDtypeStruct((devices, rank), F32),
        ],
        compiler_params=pltpu.CompilerParams(vmem_limit_bytes=10 << 20),
    )(own, *others, inverse)


def solve_stacked(parts, inverse):
    return pl.pallas_call(
        functools.partial(solve_kernel, True, 1),
        out_shape=[jax.ShapeDtypeStruct(parts.shape[1:], F32)],
        compiler_params=pltpu.CompilerParams(vmem_limit_bytes=10 << 20),
    )(parts, inverse)[0]


def scale_kernel(row_total, squares_ref, raw_ref, factor_ref, rounded_ref, scale_ref):
    scale = jnp.sqrt(jnp.sum(squares_ref[...], 0, keepdims=True) / row_total + EPS)
    scale_ref[...] = scale
    factor = raw_ref[...] / scale
    factor_ref[...] = factor
    rounded_ref[...] = factor.astype(BF16)


def scale_rows(squares, raw, row_total):
    return pl.pallas_call(
        functools.partial(scale_kernel, row_total),
        out_shape=[
            jax.ShapeDtypeStruct(raw.shape, F32),
            jax.ShapeDtypeStruct(raw.shape, BF16),
            jax.ShapeDtypeStruct((1, raw.shape[1]), F32),
        ],
        compiler_params=pltpu.CompilerParams(vmem_limit_bytes=10 << 20),
    )(squares, raw)


def on_device(blocks, coords, counts, b_init, c_init):
    slab_count = lax.axis_size("slab")
    grid_count = lax.axis_size("grid")
    local_blocks = blocks[0, 0]
    local_coords = coords.reshape(-1)
    filled = counts.reshape(-1)
    doc_rows = IBP * W
    term_rows = JBP * W
    doc_total = doc_rows * slab_count
    term_total = term_rows * grid_count
    month_total = c_init.shape[0]
    month_bf = c_init.astype(BF16)
    devices = slab_count * grid_count
    ones = jnp.ones((1, c_init.shape[1]), F32)
    term_panel = lax.all_gather(b_init.astype(BF16), "slab", axis=0, tiled=True)
    term_panel, b_held = lax.optimization_barrier((term_panel, b_init))
    gram_c = (gram_local(c_init), month_total, ones)
    gram_b = (total_sum(gram_local(b_held)), term_total, ones)

    moments_a = block_moments(
        0, (None, None, "grid"), local_blocks, local_coords, filled, term_panel, month_bf, doc_rows
    )
    others_a = swap_pieces(moments_a, "grid")
    inverse_a = product_inverse(gram_b, gram_c)
    raw_a, own_gram_a, squares_a = solve_swapped(moments_a, others_a, inverse_a, devices)
    all_squares_a = exchange(squares_a, BOTH)[:, 0]
    factor_a, rounded_a, scale_a = scale_rows(all_squares_a, raw_a, doc_total)
    doc_panel = swap_gather(rounded_a, "grid")
    own_gram_a, rounded_a = lax.optimization_barrier((own_gram_a, rounded_a))
    gram_a = (total_sum(own_gram_a), doc_total, scale_a)

    moments_b = block_moments(
        1, ("grid", None, "slab"), local_blocks, local_coords, filled, doc_panel, month_bf, term_rows
    )
    others_b = swap_pieces(moments_b, "slab")
    inverse_b = product_inverse(gram_a, gram_c)
    raw_b, own_gram_b, squares_b = solve_swapped(moments_b, others_b, inverse_b, devices)
    all_squares_b = exchange(squares_b, BOTH)[:, 0]
    factor_b, rounded_b, scale_b = scale_rows(all_squares_b, raw_b, term_total)
    term_panel_new = lax.all_gather(rounded_b, "slab", axis=0, tiled=True)
    own_gram_b, rounded_b = lax.optimization_barrier((own_gram_b, rounded_b))
    gram_bn = (total_sum(own_gram_b), term_total, scale_b)

    moments_c = block_moments(
        2, (None, "grid", None), local_blocks, local_coords, filled, term_panel_new, doc_panel, month_total
    )
    parts_c = exchange(moments_c, BOTH)
    inverse_c = product_inverse(gram_a, gram_bn)
    raw_c = spread_rows(solve_stacked(parts_c, inverse_c), BOTH)
    column_scale = jnp.sqrt(jnp.mean(raw_c * raw_c, axis=0) + EPS)
    return (factor_a, factor_b, raw_c / column_scale)


def solution(mesh):
    in_specs = (
        P("slab", "grid", None, None, None),
        P("slab", "grid", None, None),
        P("slab", "grid"),
        P(("slab", "grid"), None),
        P(),
    )
    out_specs = (P(("slab", "grid"), None), P(("slab", "grid"), None), P())
    return jax.shard_map(
        on_device, mesh=mesh, in_specs=in_specs, out_specs=out_specs, check_vma=False
    )
```

```python
import functools

import jax
import jax.numpy as jnp
from jax import lax
from jax.experimental import pallas as pl
from jax.experimental.pallas import tpu as pltpu
from jax.sharding import PartitionSpec as P

W = 64
IBP = 16
JBP = 16
LANES = 128
PANEL = 128
GROUP = 4

HIGH = lax.Precision.HIGHEST
EPS = 1e-05
BOTH = ("slab", "grid")
F32 = jnp.float32
BF16 = jnp.bfloat16


def product_rows(first, second, start):
    rank = first.shape[1]
    pieces = []
    for row in range(start, start + GROUP):
        spread = jnp.broadcast_to(first[row : row + 1, :], (16, rank)).astype(BF16)
        pieces.append((second * spread[None]).reshape(W, rank))
    return jnp.concatenate(pieces, 0)


def slot_rows(coords_ref, slot, mode, order):
    block = coords_ref[slot * 3 + mode]
    if order is not None:
        each = IBP // lax.axis_size(order)
        block = ((block // each) ^ lax.axis_index(order)) * each + block % each
    return pl.multiple_of(block * W, W)


def moments_kernel(mode, orders, count_ref, coords_ref, blocks_ref, first_ref, second_ref, out_ref, *scratch):
    slot = pl.program_id(0)
    rank = out_ref.shape[1]

    @pl.when(slot == 0)
    def _():
        out_ref[...] = jnp.zeros_like(out_ref)

    spread_mode, tile_mode = ((1, 2), (0, 2), (1, 0))[mode]

    @pl.when(slot < count_ref[0])
    def _():
        first = first_ref[pl.ds(slot_rows(coords_ref, slot, spread_mode, orders[0]), W), :].astype(F32)
        second = second_ref[pl.ds(slot_rows(coords_ref, slot, tile_mode, orders[1]), W), :].reshape(4, 16, rank)
        target = slot_rows(coords_ref, slot, mode, orders[2])
        total = jnp.zeros((W, rank), F32)
        if mode == 1:
            lanes_ref, order_ref = scratch
            columns = W * W // LANES
            for column in range(columns):
                lanes_ref[pl.ds(column, W, stride=columns), :] = blocks_ref[
                    0, :, column * LANES : (column + 1) * LANES
                ].astype(F32)
            low = lax.broadcasted_iota(jnp.int32, (columns, LANES), 1) < W
        for step in range(W // GROUP):
            right = product_rows(first, second, step * GROUP)
            if mode == 0:
                left = blocks_ref[0, :, step * GROUP * W : (step + 1) * GROUP * W]
            elif mode == 1:
                parts = []
                for pair in range(GROUP // 2):
                    row = step * GROUP + 2 * pair
                    one = lanes_ref[row * columns : (row + 1) * columns, :]
                    two = lanes_ref[(row + 1) * columns : (row + 2) * columns, :]
                    even = jnp.where(low, one, pltpu.roll(two, W, 1)).astype(BF16)
                    odd = jnp.where(low, pltpu.roll(one, W, 1), two).astype(BF16)
                    parts.append(jnp.concatenate([even, odd], 0))
                left = jnp.concatenate(parts, 1)
            else:
                parts = []
                for pair in range(GROUP // 2):
                    column = step * GROUP // 2 + pair
                    turned = blocks_ref[0, :, column * LANES : (column + 1) * LANES].T
                    parts += [turned[:W], turned[W:]]
                left = jnp.concatenate(parts, 1)
            total = total + jnp.dot(left, right, preferred_element_type=F32)
        if mode == 1:
            halves = []
            for part in range(rank // LANES):
                for parity in range(2):
                    order_ref[part, pl.ds(parity, W // 2, stride=2), :] = total[
                        parity * W // 2 : (parity + 1) * W // 2, part * LANES : (part + 1) * LANES
                    ]
                halves.append(order_ref[part])
            total = jnp.concatenate(halves, 1)
        out_ref[pl.ds(target, W), :] += total


def block_moments(mode, orders, blocks, coords, count, first, second, out_rows):
    slots = blocks.shape[0]
    rank = first.shape[1]
    scratch = []
    if mode == 1:
        scratch = [
            pltpu.VMEM((W * W * W // LANES, LANES), F32),
            pltpu.VMEM((rank // LANES, W, LANES), F32),
        ]
    whole = lambda slot, count_ref, coords_ref: (0, 0)
    spec = pltpu.PrefetchScalarGridSpec(
        num_scalar_prefetch=2,
        grid=(slots,),
        in_specs=[
            pl.BlockSpec(
                (1, W, W * W),
                lambda slot, count_ref, coords_ref: (jnp.minimum(slot, count_ref[0] - 1), 0, 0),
            ),
            pl.BlockSpec(first.shape, whole),
            pl.BlockSpec(second.shape, whole),
        ],
        out_specs=pl.BlockSpec((out_rows, rank), whole),
        scratch_shapes=scratch,
    )
    return pl.pallas_call(
        functools.partial(moments_kernel, mode, orders),
        grid_spec=spec,
        out_shape=jax.ShapeDtypeStruct((out_rows, rank), F32),
        compiler_params=pltpu.CompilerParams(vmem_limit_bytes=14 << 20),
        cost_estimate=pl.CostEstimate(
            flops=2 * slots * W**3 * rank, bytes_accessed=blocks.size * 2, transcendentals=0
        ),
    )(count, coords, blocks, first, second)


def exchange(rows, axes):
    devices = lax.axis_size(axes)
    parts = lax.all_to_all(rows, axes, split_axis=0, concat_axis=0, tiled=True)
    return parts.reshape(devices, rows.shape[0] // devices, rows.shape[1])


def spread_rows(rows, axes):
    devices = lax.axis_size(axes)
    return lax.all_to_all(jnp.tile(rows, (devices, 1)), axes, split_axis=0, concat_axis=0, tiled=True)


def swap(rows, axis, step):
    return lax.ppermute(rows, axis, [(i, i ^ step) for i in range(lax.axis_size(axis))])


def swap_pieces(rows, axis):
    devices = lax.axis_size(axis)
    each = rows.shape[0] // devices
    return [swap(rows[k * each : (k + 1) * each], axis, k) for k in range(1, devices)]


def swap_gather(rows, axis):
    return jnp.concatenate([rows] + [swap(rows, axis, k) for k in range(1, lax.axis_size(axis))], 0)


def gram_local(factor):
    return jnp.dot(factor.T, factor, precision=HIGH, preferred_element_type=F32)


def exact_dot(left, right, contract):
    return lax.dot_general(left, right, (contract, ((), ())), precision=HIGH, preferred_element_type=F32)


def across_lanes(tile, lane):
    return jnp.broadcast_to(tile[:, lane : lane + 1], tile.shape)


def across_rows(tile, row):
    return jnp.broadcast_to(tile[row : row + 1, :], tile.shape)


def tree_sum(terms):
    while len(terms) > 1:
        terms = [a + b for a, b in zip(terms[::2], terms[1::2])]
    return terms[0]


def sweep_corner(entries):
    for k in range(0, 8, 2):
        at = lambda i, j: entries[(min(i, j), max(i, j))]
        a, o, d = at(k, k), at(k, k + 1), at(k + 1, k + 1)
        inverse = 1.0 / (a * d - o * o)
        w00, w01, w11 = d * inverse, -(o * inverse), a * inverse
        rest = [j for j in range(8) if j not in (k, k + 1)]
        top = {j: w00 * at(k, j) + w01 * at(k + 1, j) for j in rest}
        low = {j: w01 * at(k, j) + w11 * at(k + 1, j) for j in rest}
        swept = {(k, k): -w00, (k, k + 1): -w01, (k + 1, k + 1): -w11}
        for i in rest:
            swept[(min(k, i), max(k, i))] = top[i]
            swept[(min(k + 1, i), max(k + 1, i))] = low[i]
            for j in rest:
                if i <= j:
                    swept[(i, j)] = at(i, j) - (at(k, i) * top[j] + at(k + 1, i) * low[j])
        entries = swept
    return entries


def panel_inverse(tiles):
    shape = tiles[0].shape
    lane = lax.broadcasted_iota(jnp.int32, shape, 1)
    row = lax.broadcasted_iota(jnp.int32, shape, 0)
    for pivot in range(len(tiles)):
        tile = tiles[pivot]
        first = 8 * pivot
        columns = [across_lanes(tile, first + j) for j in range(8)]
        corner = sweep_corner({(i, j): across_rows(columns[j], i) for j in range(8) for i in range(j + 1)})
        here = (lane >= first) & (lane < first + 8)
        turned = jnp.where(here, jnp.where(lane - first == row, 1.0, 0.0), -tile)
        rows = [across_rows(turned, i) for i in range(8)]
        scaled = [tree_sum([corner[(min(i, j), max(i, j))] * rows[j] for j in range(8)]) for i in range(8)]
        swept = []
        for other, held in enumerate(tiles):
            if other == pivot:
                mine = scaled[0]
                for i in range(1, 8):
                    mine = jnp.where(row == i, scaled[i], mine)
            else:
                change = tree_sum([across_lanes(held, first + j) * scaled[j] for j in range(8)])
                mine = jnp.where(here, 0.0, held) - change
            swept.append(mine)
        tiles = swept
    return -jnp.concatenate(tiles, 0)


def on_diagonal(size):
    shape = (size, size)
    return lax.broadcasted_iota(jnp.int32, shape, 0) == lax.broadcasted_iota(jnp.int32, shape, 1)


def turned_down(across, diagonal):
    return jnp.sum(jnp.where(diagonal, across, 0.0), 1, keepdims=True)


def message_rows(devices):
    own = -(-3 * LANES // devices)
    return own, -(-(own + 2) // 8) * 8


def pack_gram(message_ref, gram, squares, devices):
    own, rows = message_rows(devices)
    packed = jnp.concatenate([gram[:LANES, :LANES], gram[:LANES, LANES:], gram[LANES:, LANES:]], 0)
    if devices * own > 3 * LANES or rows > own + 2:
        message_ref[...] = jnp.zeros_like(message_ref)
    for e in range(own):
        held = min(devices, 3 * LANES - devices * e)
        message_ref[pl.ds(e, held, stride=rows), :] = packed[devices * e : devices * e + held]
    for half in range(2):
        part = squares[:, half * LANES : (half + 1) * LANES]
        message_ref[pl.ds(own + half, devices, stride=rows), :] = jnp.broadcast_to(part, (devices, LANES))


def fold_messages(parts_ref, spread_ref, devices):
    own, rows = message_rows(devices)
    terms = [parts_ref[rows * d : rows * (d + 1), :] for d in range(devices)]
    total = functools.reduce(jnp.add, terms)
    for d in range(devices):
        spread_ref[rows * d : rows * (d + 1), :] = total
    return jnp.concatenate([total[own : own + 1], total[own + 1 : own + 2]], 1)


def unpack_gram(ref, devices):
    if ref.shape[1] != LANES:
        return ref[...]
    own, rows = message_rows(devices)
    pieces = []
    for e in range(own):
        held = min(devices, 3 * LANES - devices * e)
        pieces.append(ref[pl.ds(e, held, stride=rows), :])
    packed = jnp.concatenate(pieces, 0)
    first, corner, last = packed[:LANES], packed[LANES : 2 * LANES], packed[2 * LANES :]
    return jnp.concatenate(
        [jnp.concatenate([first, corner], 1), jnp.concatenate([corner.T, last], 1)], 0
    )


def swap_all(messages):
    return lax.all_to_all(messages, BOTH, split_axis=0, concat_axis=0, tiled=True)


def gram_message_kernel(devices, factor_ref, message_ref):
    factor = factor_ref[...]
    squares = jnp.sum(factor * factor, 0, keepdims=True)
    pack_gram(message_ref, exact_dot(factor, factor, ((0,), (0,))), squares, devices)


def fold_kernel(devices, parts_ref, spread_ref):
    fold_messages(parts_ref, spread_ref, devices)


def message_shape(devices):
    return jax.ShapeDtypeStruct((devices * message_rows(devices)[1], LANES), F32)


def gram_message(factor, devices):
    return pl.pallas_call(
        functools.partial(gram_message_kernel, devices),
        out_shape=message_shape(devices),
        compiler_params=pltpu.CompilerParams(vmem_limit_bytes=10 << 20),
    )(factor)


def fold(parts, devices):
    return pl.pallas_call(
        functools.partial(fold_kernel, devices),
        out_shape=message_shape(devices),
        compiler_params=pltpu.CompilerParams(vmem_limit_bytes=10 << 20),
    )(parts)


def on_diagonal(size):
    shape = (size, size)
    return lax.broadcasted_iota(jnp.int32, shape, 0) == lax.broadcasted_iota(jnp.int32, shape, 1)


def turned_down(across, diagonal):
    return jnp.sum(jnp.where(diagonal, across, 0.0), 1, keepdims=True)


def inverse_kernel(devices, totals, one_ref, one_scale_ref, two_ref, two_scale_ref, out_ref, held_ref):
    size = held_ref.shape[0]
    diagonal = on_diagonal(size)
    system = None
    for total, gram_ref, scale_ref in zip(totals, (one_ref, two_ref), (one_scale_ref, two_scale_ref)):
        inverse_scale = 1.0 / scale_ref[...]
        gram = unpack_gram(gram_ref, devices) * (inverse_scale / total) * turned_down(inverse_scale, diagonal)
        system = gram if system is None else system * gram
    across = lax.rsqrt(jnp.sum(jnp.where(diagonal, system, 0.0), 0, keepdims=True))
    down = turned_down(across, diagonal)
    held_ref[...] = system * across * down
    here = lax.broadcasted_iota(jnp.int32, (1, size), 1) < PANEL
    rest = size - PANEL

    def eliminate(step, carry):
        pivot = panel_inverse([held_ref[8 * g : 8 * g + 8, :PANEL] for g in range(PANEL // 8)])
        rows = held_ref[:PANEL, :]
        scaled = exact_dot(pivot, rows, ((1,), (0,)))
        minus = jnp.concatenate([-pivot, jnp.zeros((PANEL, rest), F32)], 1)
        scaled = jnp.where(here, minus, scaled)
        others = jnp.where(here, 0.0, held_ref[PANEL:, :]) - exact_dot(
            rows[:, PANEL:], scaled, ((0,), (0,))
        )
        held_ref[:rest, :] = pltpu.roll(others, rest, 1)
        held_ref[rest:, :] = pltpu.roll(scaled, rest, 1)
        return carry

    lax.fori_loop(0, size // PANEL, eliminate, 0)
    out_ref[...] = -held_ref[...] * across * down


def product_inverse(one, two, devices):
    rank = one[2].shape[1]
    return pl.pallas_call(
        functools.partial(inverse_kernel, devices, (one[1], two[1])),
        out_shape=jax.ShapeDtypeStruct((rank, rank), F32),
        scratch_shapes=[pltpu.VMEM((rank, rank), F32)],
        compiler_params=pltpu.CompilerParams(vmem_limit_bytes=10 << 20),
        cost_estimate=pl.CostEstimate(flops=10**10, bytes_accessed=3 << 18, transcendentals=0),
    )(one[0], one[2], two[0], two[2])


def solve_kernel(devices, stacked, parts, *refs):
    inverse_ref, outs = refs[parts], refs[parts + 1 :]
    if stacked:
        terms = [refs[0][part] for part in range(refs[0].shape[0])]
    else:
        terms = [ref[...] for ref in refs[:parts]]
    raw = exact_dot(functools.reduce(jnp.add, terms), inverse_ref[...], ((1,), (0,)))
    outs[0][...] = raw
    if len(outs) > 1:
        squares = jnp.sum(raw * raw, 0, keepdims=True)
        pack_gram(outs[1], exact_dot(raw, raw, ((0,), (0,))), squares, devices)


def solve_swapped(own, others, inverse, devices):
    rows, rank = others[0].shape
    whole = pl.BlockSpec((rows, rank), lambda step: (0, 0))
    square = pl.BlockSpec((rank, rank), lambda step: (0, 0))
    messages = message_shape(devices)
    return pl.pallas_call(
        functools.partial(solve_kernel, devices, False, 1 + len(others)),
        grid=(1,),
        in_specs=[whole] * (1 + len(others)) + [square],
        out_specs=[whole, pl.BlockSpec(messages.shape, lambda step: (0, 0))],
        out_shape=[jax.ShapeDtypeStruct((rows, rank), F32), messages],
        compiler_params=pltpu.CompilerParams(vmem_limit_bytes=12 << 20),
    )(own, *others, inverse)


def solve_stacked(parts, inverse, devices, with_gram):
    out_shape = [jax.ShapeDtypeStruct(parts.shape[1:], F32)]
    if with_gram:
        out_shape.append(message_shape(devices))
    return pl.pallas_call(
        functools.partial(solve_kernel, devices, True, 1),
        out_shape=out_shape,
        compiler_params=pltpu.CompilerParams(vmem_limit_bytes=10 << 20),
    )(parts, inverse)


def scale_kernel(devices, row_total, parts_ref, raw_ref, factor_ref, rounded_ref, scale_ref, spread_ref):
    squares = fold_messages(parts_ref, spread_ref, devices)
    scale = jnp.sqrt(squares / row_total + EPS)
    scale_ref[...] = scale
    factor = raw_ref[...] / scale
    factor_ref[...] = factor
    rounded_ref[...] = factor.astype(BF16)


def scale_rows(messages, raw, row_total, devices):
    return pl.pallas_call(
        functools.partial(scale_kernel, devices, row_total),
        out_shape=[
            jax.ShapeDtypeStruct(raw.shape, F32),
            jax.ShapeDtypeStruct(raw.shape, BF16),
            jax.ShapeDtypeStruct((1, raw.shape[1]), F32),
            message_shape(devices),
        ],
        compiler_params=pltpu.CompilerParams(vmem_limit_bytes=10 << 20),
    )(messages, raw)


def on_device(blocks, coords, counts, b_init, c_init):
    slab_count = lax.axis_size("slab")
    grid_count = lax.axis_size("grid")
    local_blocks = blocks[0, 0]
    local_coords = coords.reshape(-1)
    filled = counts.reshape(-1)
    doc_rows = IBP * W
    term_rows = JBP * W
    doc_total = doc_rows * slab_count
    term_total = term_rows * grid_count
    month_total = c_init.shape[0]
    month_bf = c_init.astype(BF16)
    devices = slab_count * grid_count
    ones = jnp.ones((1, c_init.shape[1]), F32)
    local_blocks = pltpu.with_memory_space_constraint(local_blocks, pltpu.HBM)
    term_panel = lax.all_gather(b_init.astype(BF16), "slab", axis=0, tiled=True)
    term_panel, b_held = lax.optimization_barrier((term_panel, b_init))
    messages_b = swap_all(gram_message(b_held, devices))
    moments_a = block_moments(
        0, (None, None, "grid"), local_blocks, local_coords, filled, term_panel, month_bf, doc_rows
    )
    others_a = swap_pieces(moments_a, "grid")
    messages_b, _ = lax.optimization_barrier((messages_b, moments_a))
    gram_b = (swap_all(fold(messages_b, devices)), term_total, ones)
    gram_c = (gram_local(c_init), month_total, ones)
    inverse_a = product_inverse(gram_b, gram_c, devices)
    raw_a, messages_a = solve_swapped(moments_a, others_a, inverse_a, devices)
    factor_a, rounded_a, scale_a, spread_a = scale_rows(swap_all(messages_a), raw_a, doc_total, devices)
    doc_panel = swap_gather(rounded_a, "grid")
    doc_panel, spread_a = lax.optimization_barrier((doc_panel, spread_a))
    gram_a = (swap_all(spread_a), doc_total, scale_a)

    moments_b = block_moments(
        1, ("grid", None, None), local_blocks, local_coords, filled, doc_panel, month_bf, term_rows
    )
    parts_b = exchange(moments_b, "slab")
    inverse_b = product_inverse(gram_a, gram_c, devices)
    raw_b, messages_n = solve_stacked(parts_b, inverse_b, devices, True)
    factor_b, rounded_b, scale_b, spread_b = scale_rows(swap_all(messages_n), raw_b, term_total, devices)
    term_panel_new = lax.all_gather(rounded_b, "slab", axis=0, tiled=True)
    gram_bn = (swap_all(spread_b), term_total, scale_b)

    moments_c = block_moments(
        2, (None, "grid", None), local_blocks, local_coords, filled, term_panel_new, doc_panel, month_total
    )
    parts_c = exchange(moments_c, BOTH)
    inverse_c = product_inverse(gram_a, gram_bn, devices)
    (raw_own,) = solve_stacked(parts_c, inverse_c, devices, False)
    raw_c = spread_rows(raw_own, BOTH)
    column_scale = jnp.sqrt(jnp.mean(raw_c * raw_c, axis=0) + EPS)
    return (factor_a, factor_b, raw_c / column_scale)


def solution(mesh):
    in_specs = (
        P("slab", "grid", None, None, None),
        P("slab", "grid", None, None),
        P("slab", "grid"),
        P(("slab", "grid"), None),
        P(),
    )
    out_specs = (P(("slab", "grid"), None), P(("slab", "grid"), None), P())
    return jax.shard_map(
        on_device, mesh=mesh, in_specs=in_specs, out_specs=out_specs, check_vma=False
    )
```

```python
import functools

import jax
import jax.numpy as jnp
from jax import lax
from jax.experimental import pallas as pl
from jax.experimental.pallas import tpu as pltpu
from jax.sharding import PartitionSpec as P

W = 64
IBP = 16
JBP = 16
LANES = 128
PANEL = 128
GROUP = 4

HIGH = lax.Precision.HIGHEST
EPS = 1e-05
BOTH = ("slab", "grid")
F32 = jnp.float32
BF16 = jnp.bfloat16


def product_rows(first, second, start):
    rank = first.shape[1]
    pieces = []
    for row in range(start, start + GROUP):
        spread = jnp.broadcast_to(first[row : row + 1, :], (16, rank)).astype(BF16)
        pieces.append((second * spread[None]).reshape(W, rank))
    return jnp.concatenate(pieces, 0)


def slot_rows(coords_ref, slot, mode, order):
    block = coords_ref[slot * 3 + mode]
    if order is not None:
        each = IBP // lax.axis_size(order)
        block = ((block // each) ^ lax.axis_index(order)) * each + block % each
    return pl.multiple_of(block * W, W)


def fetch(blocks_ref, held_ref, sems, slot):
    return pltpu.make_async_copy(blocks_ref.at[slot], held_ref.at[slot], sems.at[slot])


def fetch_all(count, blocks_ref, held_ref, sems):
    for slot in range(blocks_ref.shape[0]):

        @pl.when(slot < count)
        def _():
            fetch(blocks_ref, held_ref, sems, slot).start()


def moments_kernel(
    mode, orders, count_ref, coords_ref, blocks_ref, first_ref, second_ref, out_ref, held_ref, sems, order_ref
):
    rank = out_ref.shape[1]
    count = count_ref[0]
    fetch_all(count, blocks_ref, held_ref, sems)
    out_ref[...] = jnp.zeros_like(out_ref)
    spread_mode, tile_mode = ((1, 2), (0, 2), (1, 0))[mode]

    def add_block(slot, carry):
        first = first_ref[pl.ds(slot_rows(coords_ref, slot, spread_mode, orders[0]), W), :].astype(F32)
        second = second_ref[pl.ds(slot_rows(coords_ref, slot, tile_mode, orders[1]), W), :].reshape(4, 16, rank)
        target = slot_rows(coords_ref, slot, mode, orders[2])
        fetch(blocks_ref, held_ref, sems, slot).wait()
        total = jnp.zeros((W, rank), F32)
        for step in range(W // GROUP):
            left = held_ref[slot, :, step * GROUP * W : (step + 1) * GROUP * W]
            right = product_rows(first, second, step * GROUP)
            total = total + jnp.dot(left, right, preferred_element_type=F32)
        if mode == 1:
            halves = []
            for part in range(rank // LANES):
                for parity in range(2):
                    order_ref[part, pl.ds(parity, W // 2, stride=2), :] = total[
                        parity * W // 2 : (parity + 1) * W // 2, part * LANES : (part + 1) * LANES
                    ]
                halves.append(order_ref[part])
            total = jnp.concatenate(halves, 1)
        out_ref[pl.ds(target, W), :] += total
        return carry

    lax.fori_loop(0, count, add_block, 0)


SMEM_SPEC = pl.BlockSpec(memory_space=pltpu.SMEM)
HBM_SPEC = pl.BlockSpec(memory_space=pltpu.HBM)
VMEM_SPEC = pl.BlockSpec(memory_space=pltpu.VMEM)


def block_moments(mode, orders, blocks, coords, count, first, second, out_rows):
    slots = blocks.shape[0]
    rank = first.shape[1]
    return pl.pallas_call(
        functools.partial(moments_kernel, mode, orders),
        in_specs=[SMEM_SPEC, SMEM_SPEC, HBM_SPEC, VMEM_SPEC, VMEM_SPEC],
        out_specs=VMEM_SPEC,
        out_shape=jax.ShapeDtypeStruct((out_rows, rank), F32),
        scratch_shapes=[
            pltpu.VMEM(blocks.shape, BF16),
            pltpu.SemaphoreType.DMA((slots,)),
            pltpu.VMEM((rank // LANES, W, LANES), F32),
        ],
        compiler_params=pltpu.CompilerParams(vmem_limit_bytes=18 << 20),
        cost_estimate=pl.CostEstimate(
            flops=2 * slots * W**3 * rank, bytes_accessed=blocks.size * 2, transcendentals=0
        ),
    )(count, coords, pltpu.with_memory_space_constraint(blocks, pltpu.HBM), first, second)


def turn_kernel(mode, count_ref, blocks_ref, out_ref, held_ref, turned_ref, in_sems, out_sems, lanes_ref):
    count = count_ref[0]
    fetch_all(count, blocks_ref, held_ref, in_sems)
    columns = W * W // LANES

    def turn(slot, carry):
        fetch(blocks_ref, held_ref, in_sems, slot).wait()
        if mode == 1:
            for column in range(columns):
                lanes_ref[pl.ds(column, W, stride=columns), :] = held_ref[
                    slot, :, column * LANES : (column + 1) * LANES
                ].astype(F32)
            low = lax.broadcasted_iota(jnp.int32, (columns, LANES), 1) < W
            for pair in range(W // 2):
                one = lanes_ref[2 * pair * columns : (2 * pair + 1) * columns, :]
                two = lanes_ref[(2 * pair + 1) * columns : (2 * pair + 2) * columns, :]
                even = jnp.where(low, one, pltpu.roll(two, W, 1)).astype(BF16)
                odd = jnp.where(low, pltpu.roll(one, W, 1), two).astype(BF16)
                turned_ref[slot, :, pair * LANES : (pair + 1) * LANES] = jnp.concatenate([even, odd], 0)
        else:
            for pair in range(W // 2):
                turned = held_ref[slot, :, pair * LANES : (pair + 1) * LANES].T
                turned_ref[slot, :, pair * LANES : (pair + 1) * LANES] = jnp.concatenate(
                    [turned[:W], turned[W:]], 1
                )
        fetch(turned_ref, out_ref, out_sems, slot).start()
        return carry

    lax.fori_loop(0, count, turn, 0)

    def finish(slot, carry):
        fetch(turned_ref, out_ref, out_sems, slot).wait()
        return carry

    lax.fori_loop(0, count, finish, 0)


def turned_blocks(mode, blocks, count):
    slots = blocks.shape[0]
    return pl.pallas_call(
        functools.partial(turn_kernel, mode),
        in_specs=[SMEM_SPEC, HBM_SPEC],
        out_specs=HBM_SPEC,
        out_shape=pltpu.HBM(blocks.shape, blocks.dtype),
        scratch_shapes=[
            pltpu.VMEM(blocks.shape, BF16),
            pltpu.VMEM(blocks.shape, BF16),
            pltpu.SemaphoreType.DMA((slots,)),
            pltpu.SemaphoreType.DMA((slots,)),
            pltpu.VMEM((W * W * W // LANES, LANES), F32),
        ],
        compiler_params=pltpu.CompilerParams(vmem_limit_bytes=24 << 20),
        cost_estimate=pl.CostEstimate(flops=0, bytes_accessed=blocks.size * 8, transcendentals=0),
    )(count, pltpu.with_memory_space_constraint(blocks, pltpu.HBM))


def exchange(rows, axes):
    devices = lax.axis_size(axes)
    parts = lax.all_to_all(rows, axes, split_axis=0, concat_axis=0, tiled=True)
    return parts.reshape(devices, rows.shape[0] // devices, rows.shape[1])


def spread_rows(rows, axes):
    devices = lax.axis_size(axes)
    return lax.all_to_all(jnp.tile(rows, (devices, 1)), axes, split_axis=0, concat_axis=0, tiled=True)


def swap(rows, axis, step):
    return lax.ppermute(rows, axis, [(i, i ^ step) for i in range(lax.axis_size(axis))])


def swap_pieces(rows, axis):
    devices = lax.axis_size(axis)
    each = rows.shape[0] // devices
    return [swap(rows[k * each : (k + 1) * each], axis, k) for k in range(1, devices)]


def swap_gather(rows, axis):
    return jnp.concatenate([rows] + [swap(rows, axis, k) for k in range(1, lax.axis_size(axis))], 0)


def gram_local(factor):
    return jnp.dot(factor.T, factor, precision=HIGH, preferred_element_type=F32)


def exact_dot(left, right, contract):
    return lax.dot_general(left, right, (contract, ((), ())), precision=HIGH, preferred_element_type=F32)


def across_lanes(tile, lane):
    return jnp.broadcast_to(tile[:, lane : lane + 1], tile.shape)


def across_rows(tile, row):
    return jnp.broadcast_to(tile[row : row + 1, :], tile.shape)


def tree_sum(terms):
    while len(terms) > 1:
        terms = [a + b for a, b in zip(terms[::2], terms[1::2])]
    return terms[0]


def sweep_corner(entries):
    for k in range(0, 8, 2):
        at = lambda i, j: entries[(min(i, j), max(i, j))]
        a, o, d = at(k, k), at(k, k + 1), at(k + 1, k + 1)
        inverse = 1.0 / (a * d - o * o)
        w00, w01, w11 = d * inverse, -(o * inverse), a * inverse
        rest = [j for j in range(8) if j not in (k, k + 1)]
        top = {j: w00 * at(k, j) + w01 * at(k + 1, j) for j in rest}
        low = {j: w01 * at(k, j) + w11 * at(k + 1, j) for j in rest}
        swept = {(k, k): -w00, (k, k + 1): -w01, (k + 1, k + 1): -w11}
        for i in rest:
            swept[(min(k, i), max(k, i))] = top[i]
            swept[(min(k + 1, i), max(k + 1, i))] = low[i]
            for j in rest:
                if i <= j:
                    swept[(i, j)] = at(i, j) - (at(k, i) * top[j] + at(k + 1, i) * low[j])
        entries = swept
    return entries


def panel_inverse(tiles):
    shape = tiles[0].shape
    lane = lax.broadcasted_iota(jnp.int32, shape, 1)
    row = lax.broadcasted_iota(jnp.int32, shape, 0)
    for pivot in range(len(tiles)):
        tile = tiles[pivot]
        first = 8 * pivot
        columns = [across_lanes(tile, first + j) for j in range(8)]
        corner = sweep_corner({(i, j): across_rows(columns[j], i) for j in range(8) for i in range(j + 1)})
        here = (lane >= first) & (lane < first + 8)
        turned = jnp.where(here, jnp.where(lane - first == row, 1.0, 0.0), -tile)
        rows = [across_rows(turned, i) for i in range(8)]
        scaled = [tree_sum([corner[(min(i, j), max(i, j))] * rows[j] for j in range(8)]) for i in range(8)]
        swept = []
        for other, held in enumerate(tiles):
            if other == pivot:
                mine = scaled[0]
                for i in range(1, 8):
                    mine = jnp.where(row == i, scaled[i], mine)
            else:
                change = tree_sum([across_lanes(held, first + j) * scaled[j] for j in range(8)])
                mine = jnp.where(here, 0.0, held) - change
            swept.append(mine)
        tiles = swept
    return -jnp.concatenate(tiles, 0)


def on_diagonal(size):
    shape = (size, size)
    return lax.broadcasted_iota(jnp.int32, shape, 0) == lax.broadcasted_iota(jnp.int32, shape, 1)


def turned_down(across, diagonal):
    return jnp.sum(jnp.where(diagonal, across, 0.0), 1, keepdims=True)


def message_rows(devices):
    own = -(-3 * LANES // devices)
    return own, -(-(own + 2) // 8) * 8


def pack_gram(message_ref, gram, squares, devices):
    own, rows = message_rows(devices)
    packed = jnp.concatenate([gram[:LANES, :LANES], gram[:LANES, LANES:], gram[LANES:, LANES:]], 0)
    if devices * own > 3 * LANES or rows > own + 2:
        message_ref[...] = jnp.zeros_like(message_ref)
    for e in range(own):
        held = min(devices, 3 * LANES - devices * e)
        message_ref[pl.ds(e, held, stride=rows), :] = packed[devices * e : devices * e + held]
    for half in range(2):
        part = squares[:, half * LANES : (half + 1) * LANES]
        message_ref[pl.ds(own + half, devices, stride=rows), :] = jnp.broadcast_to(part, (devices, LANES))


def fold_messages(parts_ref, spread_ref, devices):
    own, rows = message_rows(devices)
    terms = [parts_ref[rows * d : rows * (d + 1), :] for d in range(devices)]
    total = functools.reduce(jnp.add, terms)
    for d in range(devices):
        spread_ref[rows * d : rows * (d + 1), :] = total
    return jnp.concatenate([total[own : own + 1], total[own + 1 : own + 2]], 1)


def unpack_gram(ref, devices):
    if ref.shape[1] != LANES:
        return ref[...]
    own, rows = message_rows(devices)
    pieces = []
    for e in range(own):
        held = min(devices, 3 * LANES - devices * e)
        pieces.append(ref[pl.ds(e, held, stride=rows), :])
    packed = jnp.concatenate(pieces, 0)
    first, corner, last = packed[:LANES], packed[LANES : 2 * LANES], packed[2 * LANES :]
    return jnp.concatenate(
        [jnp.concatenate([first, corner], 1), jnp.concatenate([corner.T, last], 1)], 0
    )


def swap_all(messages):
    return lax.all_to_all(messages, BOTH, split_axis=0, concat_axis=0, tiled=True)


def gram_message_kernel(devices, factor_ref, message_ref):
    factor = factor_ref[...]
    squares = jnp.sum(factor * factor, 0, keepdims=True)
    pack_gram(message_ref, exact_dot(factor, factor, ((0,), (0,))), squares, devices)


def fold_kernel(devices, parts_ref, spread_ref):
    fold_messages(parts_ref, spread_ref, devices)


def message_shape(devices):
    return jax.ShapeDtypeStruct((devices * message_rows(devices)[1], LANES), F32)


def gram_message(factor, devices):
    return pl.pallas_call(
        functools.partial(gram_message_kernel, devices),
        out_shape=message_shape(devices),
        compiler_params=pltpu.CompilerParams(vmem_limit_bytes=10 << 20),
    )(factor)


def fold(parts, devices):
    return pl.pallas_call(
        functools.partial(fold_kernel, devices),
        out_shape=message_shape(devices),
        compiler_params=pltpu.CompilerParams(vmem_limit_bytes=10 << 20),
    )(parts)


def on_diagonal(size):
    shape = (size, size)
    return lax.broadcasted_iota(jnp.int32, shape, 0) == lax.broadcasted_iota(jnp.int32, shape, 1)


def turned_down(across, diagonal):
    return jnp.sum(jnp.where(diagonal, across, 0.0), 1, keepdims=True)


def inverse_kernel(devices, totals, one_ref, one_scale_ref, two_ref, two_scale_ref, out_ref, held_ref):
    size = held_ref.shape[0]
    diagonal = on_diagonal(size)
    system = None
    for total, gram_ref, scale_ref in zip(totals, (one_ref, two_ref), (one_scale_ref, two_scale_ref)):
        inverse_scale = 1.0 / scale_ref[...]
        gram = unpack_gram(gram_ref, devices) * (inverse_scale / total) * turned_down(inverse_scale, diagonal)
        system = gram if system is None else system * gram
    across = lax.rsqrt(jnp.sum(jnp.where(diagonal, system, 0.0), 0, keepdims=True))
    down = turned_down(across, diagonal)
    held_ref[...] = system * across * down
    here = lax.broadcasted_iota(jnp.int32, (1, size), 1) < PANEL
    rest = size - PANEL

    def eliminate(step, carry):
        pivot = panel_inverse([held_ref[8 * g : 8 * g + 8, :PANEL] for g in range(PANEL // 8)])
        rows = held_ref[:PANEL, :]
        scaled = exact_dot(pivot, rows, ((1,), (0,)))
        minus = jnp.concatenate([-pivot, jnp.zeros((PANEL, rest), F32)], 1)
        scaled = jnp.where(here, minus, scaled)
        others = jnp.where(here, 0.0, held_ref[PANEL:, :]) - exact_dot(
            rows[:, PANEL:], scaled, ((0,), (0,))
        )
        held_ref[:rest, :] = pltpu.roll(others, rest, 1)
        held_ref[rest:, :] = pltpu.roll(scaled, rest, 1)
        return carry

    lax.fori_loop(0, size // PANEL, eliminate, 0)
    out_ref[...] = -held_ref[...] * across * down


def product_inverse(one, two, devices):
    rank = one[2].shape[1]
    return pl.pallas_call(
        functools.partial(inverse_kernel, devices, (one[1], two[1])),
        out_shape=jax.ShapeDtypeStruct((rank, rank), F32),
        scratch_shapes=[pltpu.VMEM((rank, rank), F32)],
        compiler_params=pltpu.CompilerParams(vmem_limit_bytes=10 << 20),
        cost_estimate=pl.CostEstimate(flops=10**10, bytes_accessed=3 << 18, transcendentals=0),
    )(one[0], one[2], two[0], two[2])


def solve_kernel(devices, stacked, parts, *refs):
    inverse_ref, outs = refs[parts], refs[parts + 1 :]
    if stacked:
        terms = [refs[0][part] for part in range(refs[0].shape[0])]
    else:
        terms = [ref[...] for ref in refs[:parts]]
    raw = exact_dot(functools.reduce(jnp.add, terms), inverse_ref[...], ((1,), (0,)))
    outs[0][...] = raw
    if len(outs) > 1:
        squares = jnp.sum(raw * raw, 0, keepdims=True)
        pack_gram(outs[1], exact_dot(raw, raw, ((0,), (0,))), squares, devices)


def solve_swapped(own, others, inverse, devices):
    rows, rank = others[0].shape
    whole = pl.BlockSpec((rows, rank), lambda step: (0, 0))
    square = pl.BlockSpec((rank, rank), lambda step: (0, 0))
    messages = message_shape(devices)
    return pl.pallas_call(
        functools.partial(solve_kernel, devices, False, 1 + len(others)),
        grid=(1,),
        in_specs=[whole] * (1 + len(others)) + [square],
        out_specs=[whole, pl.BlockSpec(messages.shape, lambda step: (0, 0))],
        out_shape=[jax.ShapeDtypeStruct((rows, rank), F32), messages],
        compiler_params=pltpu.CompilerParams(vmem_limit_bytes=12 << 20),
    )(own, *others, inverse)


def solve_stacked(parts, inverse, devices, with_gram):
    out_shape = [jax.ShapeDtypeStruct(parts.shape[1:], F32)]
    if with_gram:
        out_shape.append(message_shape(devices))
    return pl.pallas_call(
        functools.partial(solve_kernel, devices, True, 1),
        out_shape=out_shape,
        compiler_params=pltpu.CompilerParams(vmem_limit_bytes=10 << 20),
    )(parts, inverse)


def scale_kernel(devices, row_total, parts_ref, raw_ref, factor_ref, rounded_ref, scale_ref, spread_ref):
    squares = fold_messages(parts_ref, spread_ref, devices)
    scale = jnp.sqrt(squares / row_total + EPS)
    scale_ref[...] = scale
    factor = raw_ref[...] / scale
    factor_ref[...] = factor
    rounded_ref[...] = factor.astype(BF16)


def scale_rows(messages, raw, row_total, devices):
    return pl.pallas_call(
        functools.partial(scale_kernel, devices, row_total),
        out_shape=[
            jax.ShapeDtypeStruct(raw.shape, F32),
            jax.ShapeDtypeStruct(raw.shape, BF16),
            jax.ShapeDtypeStruct((1, raw.shape[1]), F32),
            message_shape(devices),
        ],
        compiler_params=pltpu.CompilerParams(vmem_limit_bytes=10 << 20),
    )(messages, raw)


def on_device(blocks, coords, counts, b_init, c_init):
    slab_count = lax.axis_size("slab")
    grid_count = lax.axis_size("grid")
    local_blocks = blocks[0, 0]
    local_coords = coords.reshape(-1)
    filled = counts.reshape(-1)
    doc_rows = IBP * W
    term_rows = JBP * W
    doc_total = doc_rows * slab_count
    term_total = term_rows * grid_count
    month_total = c_init.shape[0]
    month_bf = c_init.astype(BF16)
    devices = slab_count * grid_count
    ones = jnp.ones((1, c_init.shape[1]), F32)
    messages_b = gram_message(b_init, devices)
    messages_b, b_rounded = lax.optimization_barrier((messages_b, b_init.astype(BF16)))
    term_panel = lax.all_gather(b_rounded, "slab", axis=0, tiled=True)
    messages_b, term_panel = lax.optimization_barrier((swap_all(messages_b), term_panel))
    spread_b = fold(messages_b, devices)
    spread_b, term_panel = lax.optimization_barrier((spread_b, term_panel))
    gram_b = (swap_all(spread_b), term_total, ones)
    moments_a = block_moments(
        0, (None, None, "grid"), local_blocks, local_coords, filled, term_panel, month_bf, doc_rows
    )
    others_a = swap_pieces(moments_a, "grid")
    blocks_b, _ = lax.optimization_barrier((local_blocks, moments_a))
    blocks_b = turned_blocks(1, blocks_b, filled)
    gram_c = (gram_local(c_init), month_total, ones)
    inverse_a = product_inverse(gram_b, gram_c, devices)
    inverse_a, blocks_b = lax.optimization_barrier((inverse_a, blocks_b))
    raw_a, messages_a = solve_swapped(moments_a, others_a, inverse_a, devices)
    factor_a, rounded_a, scale_a, spread_a = scale_rows(swap_all(messages_a), raw_a, doc_total, devices)
    doc_panel = swap_gather(rounded_a, "grid")
    blocks_c, _ = lax.optimization_barrier((local_blocks, rounded_a))
    blocks_c = turned_blocks(2, blocks_c, filled)
    doc_panel, spread_a, blocks_c = lax.optimization_barrier((doc_panel, spread_a, blocks_c))
    gram_a = (swap_all(spread_a), doc_total, scale_a)

    moments_b = block_moments(
        1, ("grid", None, None), blocks_b, local_coords, filled, doc_panel, month_bf, term_rows
    )
    parts_b = exchange(moments_b, "slab")
    inverse_b = product_inverse(gram_a, gram_c, devices)
    raw_b, messages_n = solve_stacked(parts_b, inverse_b, devices, True)
    factor_b, rounded_b, scale_b, spread_b = scale_rows(swap_all(messages_n), raw_b, term_total, devices)
    term_panel_new = lax.all_gather(rounded_b, "slab", axis=0, tiled=True)
    gram_bn = (swap_all(spread_b), term_total, scale_b)

    moments_c = block_moments(
        2, (None, "grid", None), blocks_c, local_coords, filled, term_panel_new, doc_panel, month_total
    )
    parts_c = exchange(moments_c, BOTH)
    inverse_c = product_inverse(gram_a, gram_bn, devices)
    (raw_own,) = solve_stacked(parts_c, inverse_c, devices, False)
    raw_c = spread_rows(raw_own, BOTH)
    column_scale = jnp.sqrt(jnp.mean(raw_c * raw_c, axis=0) + EPS)
    return (factor_a, factor_b, raw_c / column_scale)


def solution(mesh):
    in_specs = (
        P("slab", "grid", None, None, None),
        P("slab", "grid", None, None),
        P("slab", "grid"),
        P(("slab", "grid"), None),
        P(),
    )
    out_specs = (P(("slab", "grid"), None), P(("slab", "grid"), None), P())
    return jax.shard_map(
        on_device, mesh=mesh, in_specs=in_specs, out_specs=out_specs, check_vma=False
    )
```

```python
import functools

import jax
import jax.numpy as jnp
from jax import lax
from jax.experimental import pallas as pl
from jax.experimental.pallas import tpu as pltpu
from jax.sharding import PartitionSpec as P

W = 64
IBP = 16
JBP = 16
LANES = 128
STRIDE = 40
PANEL = 128
GROUP = 4

HIGH = lax.Precision.HIGHEST
EPS = 1e-05
BOTH = ("slab", "grid")
TERM_ORDER, DOC_ORDER = ("slab", True), ("grid", False)
F32 = jnp.float32
BF16 = jnp.bfloat16


def product_rows(first, second, start):
    rank = first.shape[1]
    pieces = []
    for row in range(start, start + GROUP):
        spread = jnp.broadcast_to(first[row : row + 1, :], (16, rank)).astype(BF16)
        pieces.append((second * spread[None]).reshape(W, rank))
    return jnp.concatenate(pieces, 0)


def slot_rows(coords_ref, slot, mode, order):
    block = coords_ref[0, 0, slot, mode]
    if order is not None:
        axis, paired = order
        devices = lax.axis_size(axis)
        each = IBP // devices
        place = (block // each) ^ lax.axis_index(axis)
        if paired:
            place = place // 2 + place % 2 * (devices // 2)
        block = place * each + block % each
    return pl.multiple_of(block * W, W)


def fetch(blocks_ref, held_ref, sems, slot):
    return pltpu.make_async_copy(blocks_ref.at[slot], held_ref.at[slot], sems.at[slot])


def fetch_all(count, blocks_ref, held_ref, sems):
    for slot in range(blocks_ref.shape[0]):

        @pl.when(slot < count)
        def _():
            fetch(blocks_ref, held_ref, sems, slot).start()


def moments_kernel(
    mode, orders, count_ref, coords_ref, blocks_ref, first_ref, second_ref, out_ref, held_ref, sems, order_ref
):
    rank = out_ref.shape[1]
    count = count_ref[0, 0]
    fetch_all(count, blocks_ref, held_ref, sems)
    out_ref[...] = jnp.zeros_like(out_ref)
    spread_mode, tile_mode = ((1, 2), (0, 2), (1, 0))[mode]

    def add_block(slot, carry):
        first = first_ref[pl.ds(slot_rows(coords_ref, slot, spread_mode, orders[0]), W), :].astype(F32)
        second = second_ref[pl.ds(slot_rows(coords_ref, slot, tile_mode, orders[1]), W), :].astype(BF16).reshape(4, 16, rank)
        target = slot_rows(coords_ref, slot, mode, orders[2])
        fetch(blocks_ref, held_ref, sems, slot).wait()
        total = jnp.zeros((W, rank), F32)
        for step in range(W // GROUP):
            left = held_ref[slot, :, step * GROUP * W : (step + 1) * GROUP * W]
            right = product_rows(first, second, step * GROUP)
            total = total + jnp.dot(left, right, preferred_element_type=F32)
        if mode == 1:
            halves = []
            for part in range(rank // LANES):
                for parity in range(2):
                    order_ref[part, pl.ds(parity, W // 2, stride=2), :] = total[
                        parity * W // 2 : (parity + 1) * W // 2, part * LANES : (part + 1) * LANES
                    ]
                halves.append(order_ref[part])
            total = jnp.concatenate(halves, 1)
        out_ref[pl.ds(target, W), :] += total
        return carry

    lax.fori_loop(0, count, add_block, 0)


SMEM_SPEC = pl.BlockSpec(memory_space=pltpu.SMEM)
HBM_SPEC = pl.BlockSpec(memory_space=pltpu.HBM)
VMEM_SPEC = pl.BlockSpec(memory_space=pltpu.VMEM)


def block_moments(mode, orders, blocks, coords, count, first, second, out_rows):
    slots = blocks.shape[0]
    rank = first.shape[1]
    return pl.pallas_call(
        functools.partial(moments_kernel, mode, orders),
        in_specs=[SMEM_SPEC, SMEM_SPEC, HBM_SPEC, VMEM_SPEC, VMEM_SPEC],
        out_specs=VMEM_SPEC,
        out_shape=jax.ShapeDtypeStruct((out_rows, rank), F32),
        scratch_shapes=[
            pltpu.VMEM(blocks.shape, BF16),
            pltpu.SemaphoreType.DMA((slots,)),
            pltpu.VMEM((rank // LANES, W, LANES), F32),
        ],
        compiler_params=pltpu.CompilerParams(vmem_limit_bytes=18 << 20),
        cost_estimate=pl.CostEstimate(
            flops=2 * slots * W**3 * rank, bytes_accessed=blocks.size * 2, transcendentals=0
        ),
    )(count, coords, pltpu.with_memory_space_constraint(blocks, pltpu.HBM), first, second)


def turn_kernel(mode, count_ref, blocks_ref, out_ref, held_ref, turned_ref, in_sems, out_sems, lanes_ref):
    count = count_ref[0, 0]
    fetch_all(count, blocks_ref, held_ref, in_sems)
    columns = W * W // LANES

    def turn(slot, carry):
        fetch(blocks_ref, held_ref, in_sems, slot).wait()
        if mode == 1:
            for column in range(columns):
                lanes_ref[pl.ds(column, W, stride=STRIDE), :] = held_ref[
                    slot, :, column * LANES : (column + 1) * LANES
                ].astype(F32)
            low = lax.broadcasted_iota(jnp.int32, (columns, LANES), 1) < W
            for pair in range(W // 2):
                one = lanes_ref[2 * pair * STRIDE : 2 * pair * STRIDE + columns, :]
                two = lanes_ref[(2 * pair + 1) * STRIDE : (2 * pair + 1) * STRIDE + columns, :]
                even = jnp.where(low, one, pltpu.roll(two, W, 1)).astype(BF16)
                odd = jnp.where(low, pltpu.roll(one, W, 1), two).astype(BF16)
                turned_ref[slot, :, pair * LANES : (pair + 1) * LANES] = jnp.concatenate([even, odd], 0)
        else:
            for pair in range(W // 2):
                turned = held_ref[slot, :, pair * LANES : (pair + 1) * LANES].T
                turned_ref[slot, :, pair * LANES : (pair + 1) * LANES] = jnp.concatenate(
                    [turned[:W], turned[W:]], 1
                )
        fetch(turned_ref, out_ref, out_sems, slot).start()
        return carry

    lax.fori_loop(0, count, turn, 0)

    def finish(slot, carry):
        fetch(turned_ref, out_ref, out_sems, slot).wait()
        return carry

    lax.fori_loop(0, count, finish, 0)


def turned_blocks(mode, blocks, count):
    slots = blocks.shape[0]
    return pl.pallas_call(
        functools.partial(turn_kernel, mode),
        in_specs=[SMEM_SPEC, HBM_SPEC],
        out_specs=HBM_SPEC,
        out_shape=pltpu.HBM(blocks.shape, blocks.dtype),
        scratch_shapes=[
            pltpu.VMEM(blocks.shape, BF16),
            pltpu.VMEM(blocks.shape, BF16),
            pltpu.SemaphoreType.DMA((slots,)),
            pltpu.SemaphoreType.DMA((slots,)),
            pltpu.VMEM((W * STRIDE, LANES), F32),
        ],
        compiler_params=pltpu.CompilerParams(vmem_limit_bytes=24 << 20),
        cost_estimate=pl.CostEstimate(flops=0, bytes_accessed=blocks.size * 8, transcendentals=0),
    )(count, pltpu.with_memory_space_constraint(blocks, pltpu.HBM))


def exchange(rows, axes):
    devices = lax.axis_size(axes)
    parts = lax.all_to_all(rows, axes, split_axis=0, concat_axis=0, tiled=True)
    return parts.reshape(devices, rows.shape[0] // devices, rows.shape[1])


def spread_rows(rows, axes):
    devices = lax.axis_size(axes)
    return lax.all_to_all(jnp.tile(rows, (devices, 1)), axes, split_axis=0, concat_axis=0, tiled=True)


def swap(rows, axis, step):
    return lax.ppermute(rows, axis, [(i, i ^ step) for i in range(lax.axis_size(axis))])


def swap_pieces(rows, axis):
    devices = lax.axis_size(axis)
    each = rows.shape[0] // devices
    return [swap(rows[k * each : (k + 1) * each], axis, k) for k in range(1, devices)]


def swap_gather(rows, axis):
    even = [rows] + [swap(rows, axis, k) for k in range(2, lax.axis_size(axis), 2)]
    rows = jnp.concatenate(even, 0)
    return jnp.concatenate([rows, swap(rows, axis, 1)], 0)


def gram_local(factor):
    return jnp.dot(factor.T, factor, precision=HIGH, preferred_element_type=F32)


def exact_dot(left, right, contract):
    return lax.dot_general(left, right, (contract, ((), ())), precision=HIGH, preferred_element_type=F32)


def across_lanes(tile, lane):
    return jnp.broadcast_to(tile[:, lane : lane + 1], tile.shape)


def across_rows(tile, row):
    return jnp.broadcast_to(tile[row : row + 1, :], tile.shape)


def tree_sum(terms):
    while len(terms) > 1:
        terms = [a + b for a, b in zip(terms[::2], terms[1::2])]
    return terms[0]


def sweep_corner(entries):
    for k in range(0, 8, 2):
        at = lambda i, j: entries[(min(i, j), max(i, j))]
        a, o, d = at(k, k), at(k, k + 1), at(k + 1, k + 1)
        inverse = 1.0 / (a * d - o * o)
        w00, w01, w11 = d * inverse, -(o * inverse), a * inverse
        rest = [j for j in range(8) if j not in (k, k + 1)]
        top = {j: w00 * at(k, j) + w01 * at(k + 1, j) for j in rest}
        low = {j: w01 * at(k, j) + w11 * at(k + 1, j) for j in rest}
        swept = {(k, k): -w00, (k, k + 1): -w01, (k + 1, k + 1): -w11}
        for i in rest:
            swept[(min(k, i), max(k, i))] = top[i]
            swept[(min(k + 1, i), max(k + 1, i))] = low[i]
            for j in rest:
                if i <= j:
                    swept[(i, j)] = at(i, j) - (at(k, i) * top[j] + at(k + 1, i) * low[j])
        entries = swept
    return entries


def panel_inverse(tiles):
    shape = tiles[0].shape
    lane = lax.broadcasted_iota(jnp.int32, shape, 1)
    row = lax.broadcasted_iota(jnp.int32, shape, 0)
    for pivot in range(len(tiles)):
        tile = tiles[pivot]
        first = 8 * pivot
        columns = [across_lanes(tile, first + j) for j in range(8)]
        corner = sweep_corner({(i, j): across_rows(columns[j], i) for j in range(8) for i in range(j + 1)})
        here = (lane >= first) & (lane < first + 8)
        turned = jnp.where(here, jnp.where(lane - first == row, 1.0, 0.0), -tile)
        rows = [across_rows(turned, i) for i in range(8)]
        scaled = [tree_sum([corner[(min(i, j), max(i, j))] * rows[j] for j in range(8)]) for i in range(8)]
        swept = []
        for other, held in enumerate(tiles):
            if other == pivot:
                mine = scaled[0]
                for i in range(1, 8):
                    mine = jnp.where(row == i, scaled[i], mine)
            else:
                change = tree_sum([across_lanes(held, first + j) * scaled[j] for j in range(8)])
                mine = jnp.where(here, 0.0, held) - change
            swept.append(mine)
        tiles = swept
    return -jnp.concatenate(tiles, 0)


def on_diagonal(size):
    shape = (size, size)
    return lax.broadcasted_iota(jnp.int32, shape, 0) == lax.broadcasted_iota(jnp.int32, shape, 1)


def turned_down(across, diagonal):
    return jnp.sum(jnp.where(diagonal, across, 0.0), 1, keepdims=True)


def message_rows(devices):
    own = -(-3 * LANES // devices)
    return own, -(-(own + 2) // 8) * 8


def pack_gram(message_ref, gram, squares, devices):
    own, rows = message_rows(devices)
    packed = jnp.concatenate([gram[:LANES, :LANES], gram[:LANES, LANES:], gram[LANES:, LANES:]], 0)
    if devices * own > 3 * LANES or rows > own + 2:
        message_ref[...] = jnp.zeros_like(message_ref)
    for e in range(own):
        held = min(devices, 3 * LANES - devices * e)
        message_ref[pl.ds(e, held, stride=rows), :] = packed[devices * e : devices * e + held]
    for half in range(2):
        part = squares[:, half * LANES : (half + 1) * LANES]
        message_ref[pl.ds(own + half, devices, stride=rows), :] = jnp.broadcast_to(part, (devices, LANES))


def fold_messages(parts_ref, spread_ref, devices):
    rows = message_rows(devices)[1]
    terms = [parts_ref[rows * d : rows * (d + 1), :] for d in range(devices)]
    total = functools.reduce(jnp.add, terms)
    for d in range(devices):
        spread_ref[rows * d : rows * (d + 1), :] = total


def unpack_gram(ref, devices):
    if ref.shape[1] != LANES:
        return ref[...]
    own, rows = message_rows(devices)
    pieces = []
    for e in range(own):
        held = min(devices, 3 * LANES - devices * e)
        pieces.append(ref[pl.ds(e, held, stride=rows), :])
    packed = jnp.concatenate(pieces, 0)
    first, corner, last = packed[:LANES], packed[LANES : 2 * LANES], packed[2 * LANES :]
    return jnp.concatenate(
        [jnp.concatenate([first, corner], 1), jnp.concatenate([corner.T, last], 1)], 0
    )


def swap_all(messages):
    return lax.all_to_all(messages, BOTH, split_axis=0, concat_axis=0, tiled=True)


def gram_message_kernel(devices, factor_ref, message_ref):
    factor = factor_ref[...]
    squares = jnp.sum(factor * factor, 0, keepdims=True)
    pack_gram(message_ref, exact_dot(factor, factor, ((0,), (0,))), squares, devices)


def fold_kernel(devices, parts_ref, spread_ref):
    fold_messages(parts_ref, spread_ref, devices)


def message_shape(devices):
    return jax.ShapeDtypeStruct((devices * message_rows(devices)[1], LANES), F32)


def gram_message(factor, devices):
    return pl.pallas_call(
        functools.partial(gram_message_kernel, devices),
        out_shape=message_shape(devices),
        compiler_params=pltpu.CompilerParams(vmem_limit_bytes=10 << 20),
    )(factor)


def fold(parts, devices):
    return pl.pallas_call(
        functools.partial(fold_kernel, devices),
        out_shape=message_shape(devices),
        compiler_params=pltpu.CompilerParams(vmem_limit_bytes=10 << 20),
    )(parts)


def on_diagonal(size):
    shape = (size, size)
    return lax.broadcasted_iota(jnp.int32, shape, 0) == lax.broadcasted_iota(jnp.int32, shape, 1)


def turned_down(across, diagonal):
    return jnp.sum(jnp.where(diagonal, across, 0.0), 1, keepdims=True)


def inverse_kernel(devices, totals, one_ref, one_scale_ref, two_ref, two_scale_ref, out_ref, held_ref):
    size = held_ref.shape[0]
    diagonal = on_diagonal(size)
    system = None
    for total, gram_ref, scale_ref in zip(totals, (one_ref, two_ref), (one_scale_ref, two_scale_ref)):
        inverse_scale = 1.0 / scale_ref[...]
        gram = unpack_gram(gram_ref, devices) * (inverse_scale / total) * turned_down(inverse_scale, diagonal)
        system = gram if system is None else system * gram
    across = lax.rsqrt(jnp.sum(jnp.where(diagonal, system, 0.0), 0, keepdims=True))
    down = turned_down(across, diagonal)
    held_ref[...] = system * across * down
    here = lax.broadcasted_iota(jnp.int32, (1, size), 1) < PANEL
    rest = size - PANEL

    def eliminate(step, carry):
        pivot = panel_inverse([held_ref[8 * g : 8 * g + 8, :PANEL] for g in range(PANEL // 8)])
        rows = held_ref[:PANEL, :]
        scaled = exact_dot(pivot, rows, ((1,), (0,)))
        minus = jnp.concatenate([-pivot, jnp.zeros((PANEL, rest), F32)], 1)
        scaled = jnp.where(here, minus, scaled)
        others = jnp.where(here, 0.0, held_ref[PANEL:, :]) - exact_dot(
            rows[:, PANEL:], scaled, ((0,), (0,))
        )
        held_ref[:rest, :] = pltpu.roll(others, rest, 1)
        held_ref[rest:, :] = pltpu.roll(scaled, rest, 1)
        return carry

    lax.fori_loop(0, size // PANEL, eliminate, 0)
    out_ref[...] = -held_ref[...] * across * down


def product_inverse(one, two, devices):
    rank = one[2].shape[1]
    return pl.pallas_call(
        functools.partial(inverse_kernel, devices, (one[1], two[1])),
        out_shape=jax.ShapeDtypeStruct((rank, rank), F32),
        scratch_shapes=[pltpu.VMEM((rank, rank), F32)],
        compiler_params=pltpu.CompilerParams(vmem_limit_bytes=10 << 20),
        cost_estimate=pl.CostEstimate(flops=10**10, bytes_accessed=3 << 18, transcendentals=0),
    )(one[0], one[2], two[0], two[2])


def solve_kernel(devices, stacked, parts, *refs):
    inverse_ref, outs = refs[parts], refs[parts + 1 :]
    if stacked:
        terms = [refs[0][part] for part in range(refs[0].shape[0])]
    else:
        terms = [ref[...] for ref in refs[:parts]]
    raw = exact_dot(functools.reduce(jnp.add, terms), inverse_ref[...], ((1,), (0,)))
    outs[0][...] = raw
    if len(outs) > 1:
        squares = jnp.sum(raw * raw, 0, keepdims=True)
        pack_gram(outs[1], exact_dot(raw, raw, ((0,), (0,))), squares, devices)


def solve_swapped(own, others, inverse, devices):
    rows, rank = others[0].shape
    whole = pl.BlockSpec((rows, rank), lambda step: (0, 0))
    square = pl.BlockSpec((rank, rank), lambda step: (0, 0))
    messages = message_shape(devices)
    return pl.pallas_call(
        functools.partial(solve_kernel, devices, False, 1 + len(others)),
        grid=(1,),
        in_specs=[whole] * (1 + len(others)) + [square],
        out_specs=[whole, pl.BlockSpec(messages.shape, lambda step: (0, 0))],
        out_shape=[jax.ShapeDtypeStruct((rows, rank), F32), messages],
        compiler_params=pltpu.CompilerParams(vmem_limit_bytes=12 << 20),
    )(own, *others, inverse)


def solve_stacked(parts, inverse, devices, with_gram):
    out_shape = [jax.ShapeDtypeStruct(parts.shape[1:], F32)]
    if with_gram:
        out_shape.append(message_shape(devices))
    return pl.pallas_call(
        functools.partial(solve_kernel, devices, True, 1),
        out_shape=out_shape,
        compiler_params=pltpu.CompilerParams(vmem_limit_bytes=10 << 20),
    )(parts, inverse)


def scale_kernel(devices, row_total, parts_ref, raw_ref, factor_ref, rounded_ref, scale_ref):
    own, rows = message_rows(devices)
    total = functools.reduce(jnp.add, [parts_ref[rows * d + own : rows * d + own + 2, :] for d in range(devices)])
    squares = jnp.concatenate([total[:1], total[1:2]], 1)
    scale = jnp.sqrt(squares / row_total + EPS)
    scale_ref[...] = scale
    factor = raw_ref[...] / scale
    factor_ref[...] = factor
    rounded_ref[...] = factor.astype(BF16)


def scale_rows(messages, raw, row_total, devices):
    return pl.pallas_call(
        functools.partial(scale_kernel, devices, row_total),
        out_shape=[
            jax.ShapeDtypeStruct(raw.shape, F32),
            jax.ShapeDtypeStruct(raw.shape, BF16),
            jax.ShapeDtypeStruct((1, raw.shape[1]), F32),
        ],
        compiler_params=pltpu.CompilerParams(vmem_limit_bytes=10 << 20),
    )(messages, raw)


def on_device(blocks, coords, counts, b_init, c_init):
    slab_count = lax.axis_size("slab")
    grid_count = lax.axis_size("grid")
    local_blocks = blocks[0, 0]
    doc_rows = IBP * W
    term_rows = JBP * W
    doc_total = doc_rows * slab_count
    term_total = term_rows * grid_count
    month_total = c_init.shape[0]
    devices = slab_count * grid_count
    ones = jnp.ones((1, c_init.shape[1]), F32)
    b_rounded, b_held = lax.optimization_barrier((b_init.astype(BF16), b_init))
    term_panel = swap_gather(b_rounded, "slab")
    messages_b = swap_all(gram_message(b_held, devices))
    spread_b, term_panel = lax.optimization_barrier((fold(messages_b, devices), term_panel))
    gram_b = (swap_all(spread_b), term_total, ones)
    moments_a = block_moments(
        0, (TERM_ORDER, None, DOC_ORDER), local_blocks, coords, counts, term_panel, c_init, doc_rows
    )
    others_a = swap_pieces(moments_a, "grid")
    c_held, _ = lax.optimization_barrier((c_init, moments_a))
    gram_c = (gram_local(c_held), month_total, ones)
    inverse_a = product_inverse(gram_b, gram_c, devices)
    blocks_b, inverse_a = lax.optimization_barrier((local_blocks, inverse_a))
    blocks_b = turned_blocks(1, blocks_b, counts)
    inverse_a, blocks_b = lax.optimization_barrier((inverse_a, blocks_b))
    raw_a, messages_a = solve_swapped(moments_a, others_a, inverse_a, devices)
    blocks_c, messages_a = lax.optimization_barrier((local_blocks, messages_a))
    blocks_c = turned_blocks(2, blocks_c, counts)
    messages_a, blocks_c = lax.optimization_barrier((swap_all(messages_a), blocks_c))
    factor_a, rounded_a, scale_a = scale_rows(messages_a, raw_a, doc_total, devices)
    pieces = [rounded_a] + [swap(rounded_a, "grid", k) for k in range(1, grid_count)]
    messages_a, pieces[1] = lax.optimization_barrier((messages_a, pieces[1]))
    doc_panel = jnp.concatenate(pieces, 0)
    spread_a = fold(messages_a, devices)
    gram_a = (swap_all(spread_a), doc_total, scale_a)

    moments_b = block_moments(
        1, (DOC_ORDER, None, None), blocks_b, coords, counts, doc_panel, c_init, term_rows
    )
    parts_b = exchange(moments_b, "slab")
    inverse_b = product_inverse(gram_a, gram_c, devices)
    raw_b, messages_n = solve_stacked(parts_b, inverse_b, devices, True)
    messages_n = swap_all(messages_n)
    factor_b, rounded_b, scale_b = scale_rows(messages_n, raw_b, term_total, devices)
    term_panel_new = swap_gather(rounded_b, "slab")
    messages_n, _ = lax.optimization_barrier((messages_n, rounded_b))
    spread_n = fold(messages_n, devices)
    gram_bn = (swap_all(spread_n), term_total, scale_b)

    moments_c = block_moments(
        2, (TERM_ORDER, DOC_ORDER, None), blocks_c, coords, counts, term_panel_new, doc_panel, month_total
    )
    parts_c = exchange(moments_c, BOTH)
    inverse_c = product_inverse(gram_a, gram_bn, devices)
    (raw_own,) = solve_stacked(parts_c, inverse_c, devices, False)
    raw_c = spread_rows(raw_own, BOTH)
    column_scale = jnp.sqrt(jnp.mean(raw_c * raw_c, axis=0) + EPS)
    return (factor_a, factor_b, raw_c / column_scale)


def solution(mesh):
    in_specs = (
        P("slab", "grid", None, None, None),
        P("slab", "grid", None, None),
        P("slab", "grid"),
        P(("slab", "grid"), None),
        P(),
    )
    out_specs = (P(("slab", "grid"), None), P(("slab", "grid"), None), P())
    return jax.shard_map(
        on_device, mesh=mesh, in_specs=in_specs, out_specs=out_specs, check_vma=False
    )
```

```python
import functools

import jax
import jax.numpy as jnp
from jax import lax
from jax.experimental import pallas as pl
from jax.experimental.pallas import tpu as pltpu
from jax.sharding import PartitionSpec as P

W = 64
IBP = 16
JBP = 16
LANES = 128
STRIDE = 40
PANEL = 128
GROUP = 4

HIGH = lax.Precision.HIGHEST
EPS = 1e-05
BOTH = ("slab", "grid")
TERM_ORDER, DOC_ORDER = ("slab", True), ("grid", False)
F32 = jnp.float32
BF16 = jnp.bfloat16


def product_rows(first, second, start):
    rank = first.shape[1]
    pieces = []
    for row in range(start, start + GROUP):
        spread = jnp.broadcast_to(first[row : row + 1, :], (16, rank)).astype(BF16)
        pieces.append((second * spread[None]).reshape(W, rank))
    return jnp.concatenate(pieces, 0)


def slot_rows(coords_ref, slot, mode, order):
    block = coords_ref[0, 0, slot, mode]
    if order is not None:
        axis, paired = order
        devices = lax.axis_size(axis)
        each = IBP // devices
        place = (block // each) ^ lax.axis_index(axis)
        if paired:
            place = place // 2 + place % 2 * (devices // 2)
        block = place * each + block % each
    return pl.multiple_of(block * W, W)


def fetch(source_ref, source, held_ref, sems, slot):
    return pltpu.make_async_copy(source_ref.at[source], held_ref.at[slot], sems.at[slot])


def fetch_all(count, block_refs, first, held_ref, sems):
    each = block_refs[0].shape[0]
    for slot in range(held_ref.shape[0]):

        @pl.when(slot < count)
        def _():
            fetch(block_refs[slot // each], first + slot % each, held_ref, sems, slot).start()


def moments_kernel(mode, orders, arrays, count_ref, coords_ref, *refs):
    block_refs, refs = refs[:arrays], refs[arrays:]
    first_ref, second_ref, out_ref, held_ref, sems, order_ref = refs[:6]
    rank = out_ref.shape[1]
    count = count_ref[0, 0]
    if len(refs) > 6:
        months_ref, month_sem = refs[6:]
        months = pltpu.make_async_copy(second_ref, months_ref, month_sem)
        months.start()
        second_ref = months_ref
    fetch_all(count, block_refs, 0, held_ref, sems)
    out_ref[...] = jnp.zeros_like(out_ref)
    if len(refs) > 6:
        months.wait()
    spread_mode, tile_mode = ((1, 2), (0, 2), (1, 0))[mode]

    def add_block(slot, carry):
        first = first_ref[pl.ds(slot_rows(coords_ref, slot, spread_mode, orders[0]), W), :].astype(F32)
        second = second_ref[pl.ds(slot_rows(coords_ref, slot, tile_mode, orders[1]), W), :].astype(BF16).reshape(4, 16, rank)
        target = slot_rows(coords_ref, slot, mode, orders[2])
        fetch(block_refs[0], 0, held_ref, sems, slot).wait()
        total = jnp.zeros((W, rank), F32)
        for step in range(W // GROUP):
            left = held_ref[slot, :, step * GROUP * W : (step + 1) * GROUP * W]
            right = product_rows(first, second, step * GROUP)
            total = total + jnp.dot(left, right, preferred_element_type=F32)
        if mode == 1:
            halves = []
            for part in range(rank // LANES):
                for parity in range(2):
                    order_ref[part, pl.ds(parity, W // 2, stride=2), :] = total[
                        parity * W // 2 : (parity + 1) * W // 2, part * LANES : (part + 1) * LANES
                    ]
                halves.append(order_ref[part])
            total = jnp.concatenate(halves, 1)
        out_ref[pl.ds(target, W), :] += total
        return carry

    lax.fori_loop(0, count, add_block, 0)


SMEM_SPEC = pl.BlockSpec(memory_space=pltpu.SMEM)
HBM_SPEC = pl.BlockSpec(memory_space=pltpu.HBM)
VMEM_SPEC = pl.BlockSpec(memory_space=pltpu.VMEM)


def block_moments(mode, orders, blocks, coords, count, first, second, out_rows):
    slots = sum(part.shape[0] for part in blocks)
    shape = (slots, *blocks[0].shape[1:])
    rank = first.shape[1]
    in_hbm = lambda array: pltpu.with_memory_space_constraint(array, pltpu.HBM)
    scratch = [
        pltpu.VMEM(shape, BF16),
        pltpu.SemaphoreType.DMA((slots,)),
        pltpu.VMEM((rank // LANES, W, LANES), F32),
    ]
    second_spec = VMEM_SPEC
    if mode < 2:
        second, second_spec = in_hbm(second), HBM_SPEC
        scratch += [pltpu.VMEM(second.shape, second.dtype), pltpu.SemaphoreType.DMA]
    return pl.pallas_call(
        functools.partial(moments_kernel, mode, orders, len(blocks)),
        in_specs=[SMEM_SPEC, SMEM_SPEC] + [HBM_SPEC] * len(blocks) + [VMEM_SPEC, second_spec],
        out_specs=VMEM_SPEC,
        out_shape=jax.ShapeDtypeStruct((out_rows, rank), F32),
        scratch_shapes=scratch,
        compiler_params=pltpu.CompilerParams(vmem_limit_bytes=18 << 20),
        cost_estimate=pl.CostEstimate(
            flops=2 * slots * W**3 * rank, bytes_accessed=slots * W**3 * 2, transcendentals=0
        ),
    )(count, coords, *[in_hbm(part) for part in blocks], first, second)


def turn_kernel(mode, first, count_ref, blocks_ref, out_ref, held_ref, turned_ref, in_sems, out_sems, lanes_ref):
    count = jnp.clip(count_ref[0, 0] - first, 0, held_ref.shape[0])
    fetch_all(count, [blocks_ref], first, held_ref, in_sems)
    columns = W * W // LANES

    def turn(slot, carry):
        fetch(blocks_ref, 0, held_ref, in_sems, slot).wait()
        if mode == 1:
            for column in range(columns):
                lanes_ref[pl.ds(column, W, stride=STRIDE), :] = held_ref[
                    slot, :, column * LANES : (column + 1) * LANES
                ].astype(F32)
            low = lax.broadcasted_iota(jnp.int32, (columns, LANES), 1) < W
            for pair in range(W // 2):
                one = lanes_ref[2 * pair * STRIDE : 2 * pair * STRIDE + columns, :]
                two = lanes_ref[(2 * pair + 1) * STRIDE : (2 * pair + 1) * STRIDE + columns, :]
                even = jnp.where(low, one, pltpu.roll(two, W, 1)).astype(BF16)
                odd = jnp.where(low, pltpu.roll(one, W, 1), two).astype(BF16)
                turned_ref[slot, :, pair * LANES : (pair + 1) * LANES] = jnp.concatenate([even, odd], 0)
        else:
            for pair in range(W // 2):
                turned = held_ref[slot, :, pair * LANES : (pair + 1) * LANES].T
                turned_ref[slot, :, pair * LANES : (pair + 1) * LANES] = jnp.concatenate(
                    [turned[:W], turned[W:]], 1
                )
        fetch(turned_ref, slot, out_ref, out_sems, slot).start()
        return carry

    lax.fori_loop(0, count, turn, 0)

    def finish(slot, carry):
        fetch(turned_ref, slot, out_ref, out_sems, slot).wait()
        return carry

    lax.fori_loop(0, count, finish, 0)


def turned_blocks(mode, blocks, count, half):
    slots = blocks.shape[0] // 2
    shape = (slots, *blocks.shape[1:])
    return pl.pallas_call(
        functools.partial(turn_kernel, mode, half * slots),
        in_specs=[SMEM_SPEC, HBM_SPEC],
        out_specs=HBM_SPEC,
        out_shape=pltpu.HBM(shape, blocks.dtype),
        scratch_shapes=[
            pltpu.VMEM(shape, BF16),
            pltpu.VMEM(shape, BF16),
            pltpu.SemaphoreType.DMA((slots,)),
            pltpu.SemaphoreType.DMA((slots,)),
            pltpu.VMEM((W * STRIDE, LANES), F32),
        ],
        compiler_params=pltpu.CompilerParams(vmem_limit_bytes=14 << 20),
        cost_estimate=pl.CostEstimate(flops=0, bytes_accessed=blocks.size * 4, transcendentals=0),
    )(count, pltpu.with_memory_space_constraint(blocks, pltpu.HBM))


def exchange(rows, axes):
    devices = lax.axis_size(axes)
    parts = lax.all_to_all(rows, axes, split_axis=0, concat_axis=0, tiled=True)
    return parts.reshape(devices, rows.shape[0] // devices, rows.shape[1])


def spread_rows(rows, axes):
    devices = lax.axis_size(axes)
    return lax.all_to_all(jnp.tile(rows, (devices, 1)), axes, split_axis=0, concat_axis=0, tiled=True)


def swap(rows, axis, step):
    return lax.ppermute(rows, axis, [(i, i ^ step) for i in range(lax.axis_size(axis))])


def swap_pieces(rows, axis):
    devices = lax.axis_size(axis)
    each = rows.shape[0] // devices
    return [swap(rows[k * each : (k + 1) * each], axis, k) for k in range(1, devices)]


def swap_gather(rows, axis):
    even = [rows] + [swap(rows, axis, k) for k in range(2, lax.axis_size(axis), 2)]
    rows = jnp.concatenate(even, 0)
    return jnp.concatenate([rows, swap(rows, axis, 1)], 0)


def gram_local(factor):
    return jnp.dot(factor.T, factor, precision=HIGH, preferred_element_type=F32)


def exact_dot(left, right, contract):
    return lax.dot_general(left, right, (contract, ((), ())), precision=HIGH, preferred_element_type=F32)


def across_lanes(tile, lane):
    return jnp.broadcast_to(tile[:, lane : lane + 1], tile.shape)


def across_rows(tile, row):
    return jnp.broadcast_to(tile[row : row + 1, :], tile.shape)


def tree_sum(terms):
    while len(terms) > 1:
        terms = [a + b for a, b in zip(terms[::2], terms[1::2])]
    return terms[0]


def sweep_corner(entries):
    for k in range(0, 8, 2):
        at = lambda i, j: entries[(min(i, j), max(i, j))]
        a, o, d = at(k, k), at(k, k + 1), at(k + 1, k + 1)
        inverse = 1.0 / (a * d - o * o)
        w00, w01, w11 = d * inverse, -(o * inverse), a * inverse
        rest = [j for j in range(8) if j not in (k, k + 1)]
        top = {j: w00 * at(k, j) + w01 * at(k + 1, j) for j in rest}
        low = {j: w01 * at(k, j) + w11 * at(k + 1, j) for j in rest}
        swept = {(k, k): -w00, (k, k + 1): -w01, (k + 1, k + 1): -w11}
        for i in rest:
            swept[(min(k, i), max(k, i))] = top[i]
            swept[(min(k + 1, i), max(k + 1, i))] = low[i]
            for j in rest:
                if i <= j:
                    swept[(i, j)] = at(i, j) - (at(k, i) * top[j] + at(k + 1, i) * low[j])
        entries = swept
    return entries


def panel_inverse(tiles):
    shape = tiles[0].shape
    lane = lax.broadcasted_iota(jnp.int32, shape, 1)
    row = lax.broadcasted_iota(jnp.int32, shape, 0)
    for pivot in range(len(tiles)):
        tile = tiles[pivot]
        first = 8 * pivot
        columns = [across_lanes(tile, first + j) for j in range(8)]
        corner = sweep_corner({(i, j): across_rows(columns[j], i) for j in range(8) for i in range(j + 1)})
        here = (lane >= first) & (lane < first + 8)
        turned = jnp.where(here, jnp.where(lane - first == row, 1.0, 0.0), -tile)
        rows = [across_rows(turned, i) for i in range(8)]
        scaled = [tree_sum([corner[(min(i, j), max(i, j))] * rows[j] for j in range(8)]) for i in range(8)]
        swept = []
        for other, held in enumerate(tiles):
            if other == pivot:
                mine = scaled[0]
                for i in range(1, 8):
                    mine = jnp.where(row == i, scaled[i], mine)
            else:
                change = tree_sum([across_lanes(held, first + j) * scaled[j] for j in range(8)])
                mine = jnp.where(here, 0.0, held) - change
            swept.append(mine)
        tiles = swept
    return -jnp.concatenate(tiles, 0)


def on_diagonal(size):
    shape = (size, size)
    return lax.broadcasted_iota(jnp.int32, shape, 0) == lax.broadcasted_iota(jnp.int32, shape, 1)


def turned_down(across, diagonal):
    return jnp.sum(jnp.where(diagonal, across, 0.0), 1, keepdims=True)


def message_rows(devices):
    own = -(-3 * LANES // devices)
    return own, -(-(own + 2) // 8) * 8


def pack_gram(message_ref, gram, squares, devices):
    own, rows = message_rows(devices)
    packed = jnp.concatenate([gram[:LANES, :LANES], gram[:LANES, LANES:], gram[LANES:, LANES:]], 0)
    if devices * own > 3 * LANES or rows > own + 2:
        message_ref[...] = jnp.zeros_like(message_ref)
    for e in range(own):
        held = min(devices, 3 * LANES - devices * e)
        message_ref[pl.ds(e, held, stride=rows), :] = packed[devices * e : devices * e + held]
    for half in range(2):
        part = squares[:, half * LANES : (half + 1) * LANES]
        message_ref[pl.ds(own + half, devices, stride=rows), :] = jnp.broadcast_to(part, (devices, LANES))


def fold_messages(parts_ref, spread_ref, devices):
    rows = message_rows(devices)[1]
    terms = [parts_ref[rows * d : rows * (d + 1), :] for d in range(devices)]
    total = functools.reduce(jnp.add, terms)
    for d in range(devices):
        spread_ref[rows * d : rows * (d + 1), :] = total


def unpack_gram(ref, devices):
    if ref.shape[1] != LANES:
        return ref[...]
    own, rows = message_rows(devices)
    pieces = []
    for e in range(own):
        held = min(devices, 3 * LANES - devices * e)
        pieces.append(ref[pl.ds(e, held, stride=rows), :])
    packed = jnp.concatenate(pieces, 0)
    first, corner, last = packed[:LANES], packed[LANES : 2 * LANES], packed[2 * LANES :]
    return jnp.concatenate(
        [jnp.concatenate([first, corner], 1), jnp.concatenate([corner.T, last], 1)], 0
    )


def swap_all(messages):
    return lax.all_to_all(messages, BOTH, split_axis=0, concat_axis=0, tiled=True)


def gram_message_kernel(devices, factor_ref, message_ref):
    factor = factor_ref[...]
    squares = jnp.sum(factor * factor, 0, keepdims=True)
    pack_gram(message_ref, exact_dot(factor, factor, ((0,), (0,))), squares, devices)


def fold_kernel(devices, parts_ref, spread_ref):
    fold_messages(parts_ref, spread_ref, devices)


def message_shape(devices):
    return jax.ShapeDtypeStruct((devices * message_rows(devices)[1], LANES), F32)


def gram_message(factor, devices):
    return pl.pallas_call(
        functools.partial(gram_message_kernel, devices),
        out_shape=message_shape(devices),
        compiler_params=pltpu.CompilerParams(vmem_limit_bytes=10 << 20),
    )(factor)


def fold(parts, devices):
    return pl.pallas_call(
        functools.partial(fold_kernel, devices),
        out_shape=message_shape(devices),
        compiler_params=pltpu.CompilerParams(vmem_limit_bytes=10 << 20),
    )(parts)


def on_diagonal(size):
    shape = (size, size)
    return lax.broadcasted_iota(jnp.int32, shape, 0) == lax.broadcasted_iota(jnp.int32, shape, 1)


def turned_down(across, diagonal):
    return jnp.sum(jnp.where(diagonal, across, 0.0), 1, keepdims=True)


def inverse_kernel(devices, totals, one_ref, one_scale_ref, two_ref, two_scale_ref, out_ref, held_ref):
    size = held_ref.shape[0]
    diagonal = on_diagonal(size)
    system = None
    for total, gram_ref, scale_ref in zip(totals, (one_ref, two_ref), (one_scale_ref, two_scale_ref)):
        inverse_scale = 1.0 / scale_ref[...]
        gram = unpack_gram(gram_ref, devices) * (inverse_scale / total) * turned_down(inverse_scale, diagonal)
        system = gram if system is None else system * gram
    across = lax.rsqrt(jnp.sum(jnp.where(diagonal, system, 0.0), 0, keepdims=True))
    down = turned_down(across, diagonal)
    held_ref[...] = system * across * down
    here = lax.broadcasted_iota(jnp.int32, (1, size), 1) < PANEL
    rest = size - PANEL

    def eliminate(step, carry):
        pivot = panel_inverse([held_ref[8 * g : 8 * g + 8, :PANEL] for g in range(PANEL // 8)])
        rows = held_ref[:PANEL, :]
        scaled = exact_dot(pivot, rows, ((1,), (0,)))
        minus = jnp.concatenate([-pivot, jnp.zeros((PANEL, rest), F32)], 1)
        scaled = jnp.where(here, minus, scaled)
        others = jnp.where(here, 0.0, held_ref[PANEL:, :]) - exact_dot(
            rows[:, PANEL:], scaled, ((0,), (0,))
        )
        held_ref[:rest, :] = pltpu.roll(others, rest, 1)
        held_ref[rest:, :] = pltpu.roll(scaled, rest, 1)
        return carry

    lax.fori_loop(0, size // PANEL, eliminate, 0)
    out_ref[...] = -held_ref[...] * across * down


def product_inverse(one, two, devices):
    rank = one[2].shape[1]
    return pl.pallas_call(
        functools.partial(inverse_kernel, devices, (one[1], two[1])),
        out_shape=jax.ShapeDtypeStruct((rank, rank), F32),
        scratch_shapes=[pltpu.VMEM((rank, rank), F32)],
        compiler_params=pltpu.CompilerParams(vmem_limit_bytes=10 << 20),
        cost_estimate=pl.CostEstimate(flops=10**10, bytes_accessed=3 << 18, transcendentals=0),
    )(one[0], one[2], two[0], two[2])


def solve_kernel(devices, stacked, parts, *refs):
    inverse_ref, outs = refs[parts], refs[parts + 1 :]
    if stacked:
        terms = [refs[0][part] for part in range(refs[0].shape[0])]
    else:
        terms = [ref[...] for ref in refs[:parts]]
    raw = exact_dot(functools.reduce(jnp.add, terms), inverse_ref[...], ((1,), (0,)))
    outs[0][...] = raw
    if len(outs) > 1:
        squares = jnp.sum(raw * raw, 0, keepdims=True)
        pack_gram(outs[1], exact_dot(raw, raw, ((0,), (0,))), squares, devices)


def solve_swapped(own, others, inverse, devices):
    rows, rank = others[0].shape
    whole = pl.BlockSpec((rows, rank), lambda step: (0, 0))
    square = pl.BlockSpec((rank, rank), lambda step: (0, 0))
    messages = message_shape(devices)
    return pl.pallas_call(
        functools.partial(solve_kernel, devices, False, 1 + len(others)),
        grid=(1,),
        in_specs=[whole] * (1 + len(others)) + [square],
        out_specs=[whole, pl.BlockSpec(messages.shape, lambda step: (0, 0))],
        out_shape=[jax.ShapeDtypeStruct((rows, rank), F32), messages],
        compiler_params=pltpu.CompilerParams(vmem_limit_bytes=12 << 20),
    )(own, *others, inverse)


def solve_stacked(parts, inverse, devices, with_gram):
    out_shape = [jax.ShapeDtypeStruct(parts.shape[1:], F32)]
    if with_gram:
        out_shape.append(message_shape(devices))
    return pl.pallas_call(
        functools.partial(solve_kernel, devices, True, 1),
        out_shape=out_shape,
        compiler_params=pltpu.CompilerParams(vmem_limit_bytes=10 << 20),
    )(parts, inverse)


def scale_kernel(devices, row_total, parts_ref, raw_ref, factor_ref, rounded_ref, scale_ref):
    own, rows = message_rows(devices)
    total = functools.reduce(jnp.add, [parts_ref[rows * d + own : rows * d + own + 2, :] for d in range(devices)])
    squares = jnp.concatenate([total[:1], total[1:2]], 1)
    scale = jnp.sqrt(squares / row_total + EPS)
    scale_ref[...] = scale
    factor = raw_ref[...] / scale
    factor_ref[...] = factor
    rounded_ref[...] = factor.astype(BF16)


def scale_rows(messages, raw, row_total, devices):
    return pl.pallas_call(
        functools.partial(scale_kernel, devices, row_total),
        out_shape=[
            jax.ShapeDtypeStruct(raw.shape, F32),
            jax.ShapeDtypeStruct(raw.shape, BF16),
            jax.ShapeDtypeStruct((1, raw.shape[1]), F32),
        ],
        compiler_params=pltpu.CompilerParams(vmem_limit_bytes=10 << 20),
    )(messages, raw)


def on_device(blocks, coords, counts, b_init, c_init):
    slab_count = lax.axis_size("slab")
    grid_count = lax.axis_size("grid")
    local_blocks = blocks[0, 0]
    doc_rows = IBP * W
    term_rows = JBP * W
    doc_total = doc_rows * slab_count
    term_total = term_rows * grid_count
    month_total = c_init.shape[0]
    devices = slab_count * grid_count
    ones = jnp.ones((1, c_init.shape[1]), F32)
    b_rounded, b_held = lax.optimization_barrier((b_init.astype(BF16), b_init))
    term_panel = swap_gather(b_rounded, "slab")
    held_blocks, term_panel = lax.optimization_barrier((local_blocks, term_panel))
    terms_one = turned_blocks(1, held_blocks, counts, 0)
    messages_b, terms_one = lax.optimization_barrier((swap_all(gram_message(b_held, devices)), terms_one))
    spread_b, term_panel = lax.optimization_barrier((fold(messages_b, devices), term_panel))
    gram_b = (swap_all(spread_b), term_total, ones)
    moments_a = block_moments(
        0, (TERM_ORDER, None, DOC_ORDER), [local_blocks], coords, counts, term_panel, c_init, doc_rows
    )
    others_a = swap_pieces(moments_a, "grid")
    c_held, _ = lax.optimization_barrier((c_init, moments_a))
    gram_c = (gram_local(c_held), month_total, ones)
    inverse_a = product_inverse(gram_b, gram_c, devices)
    held_blocks, inverse_a = lax.optimization_barrier((local_blocks, inverse_a))
    terms_two = turned_blocks(1, held_blocks, counts, 1)
    inverse_a, terms_two = lax.optimization_barrier((inverse_a, terms_two))
    raw_a, messages_a = solve_swapped(moments_a, others_a, inverse_a, devices)
    held_blocks, messages_a = lax.optimization_barrier((local_blocks, messages_a))
    months_one = turned_blocks(2, held_blocks, counts, 0)
    messages_a, months_one = lax.optimization_barrier((swap_all(messages_a), months_one))
    factor_a, rounded_a, scale_a = scale_rows(messages_a, raw_a, doc_total, devices)
    pieces = [rounded_a] + [swap(rounded_a, "grid", k) for k in range(1, grid_count)]
    messages_a, pieces[1] = lax.optimization_barrier((messages_a, pieces[1]))
    doc_panel = jnp.concatenate(pieces, 0)
    spread_a = fold(messages_a, devices)
    gram_a = (swap_all(spread_a), doc_total, scale_a)

    moments_b = block_moments(
        1, (DOC_ORDER, None, None), [terms_one, terms_two], coords, counts, doc_panel, c_init, term_rows
    )
    parts_b = exchange(moments_b, "slab")
    inverse_b = product_inverse(gram_a, gram_c, devices)
    raw_b, messages_n = solve_stacked(parts_b, inverse_b, devices, True)
    held_blocks, messages_n = lax.optimization_barrier((local_blocks, messages_n))
    months_two = turned_blocks(2, held_blocks, counts, 1)
    messages_n, months_two = lax.optimization_barrier((swap_all(messages_n), months_two))
    factor_b, rounded_b, scale_b = scale_rows(messages_n, raw_b, term_total, devices)
    term_panel_new = swap_gather(rounded_b, "slab")
    messages_n, _ = lax.optimization_barrier((messages_n, rounded_b))
    spread_n = fold(messages_n, devices)
    gram_bn = (swap_all(spread_n), term_total, scale_b)

    moments_c = block_moments(
        2, (TERM_ORDER, DOC_ORDER, None), [months_one, months_two], coords, counts, term_panel_new, doc_panel, month_total
    )
    parts_c = exchange(moments_c, BOTH)
    inverse_c = product_inverse(gram_a, gram_bn, devices)
    (raw_own,) = solve_stacked(parts_c, inverse_c, devices, False)
    raw_c = spread_rows(raw_own, BOTH)
    column_scale = jnp.sqrt(jnp.mean(raw_c * raw_c, axis=0) + EPS)
    return (factor_a, factor_b, raw_c / column_scale)


def solution(mesh):
    in_specs = (
        P("slab", "grid", None, None, None),
        P("slab", "grid", None, None),
        P("slab", "grid"),
        P(("slab", "grid"), None),
        P(),
    )
    out_specs = (P(("slab", "grid"), None), P(("slab", "grid"), None), P())
    return jax.shard_map(
        on_device, mesh=mesh, in_specs=in_specs, out_specs=out_specs, check_vma=False
    )
```

```python
import functools

import jax
import jax.numpy as jnp
from jax import lax
from jax.experimental import pallas as pl
from jax.experimental.pallas import tpu as pltpu
from jax.sharding import PartitionSpec as P

W = 64
IBP = 16
JBP = 16
LANES = 128
STRIDE = 40
PANEL = 128
GROUP = 4

HIGH = lax.Precision.HIGHEST
EPS = 1e-05
BOTH = ("slab", "grid")
TERM_ORDER, DOC_ORDER = ("slab", True), ("grid", False)
F32 = jnp.float32
BF16 = jnp.bfloat16


def product_rows(first, second, start):
    rank = first.shape[1]
    pieces = []
    for row in range(start, start + GROUP):
        spread = jnp.broadcast_to(first[row : row + 1, :], (16, rank)).astype(BF16)
        pieces.append((second * spread[None]).reshape(W, rank))
    return jnp.concatenate(pieces, 0)


def slot_rows(coords_ref, slot, mode, order):
    block = coords_ref[0, 0, slot, mode]
    if order is not None:
        axis, paired = order
        devices = lax.axis_size(axis)
        each = IBP // devices
        place = (block // each) ^ lax.axis_index(axis)
        if paired:
            place = place // 2 + place % 2 * (devices // 2)
        block = place * each + block % each
    return pl.multiple_of(block * W, W)


def fetch(source_ref, source, held_ref, sems, slot):
    return pltpu.make_async_copy(source_ref.at[source], held_ref.at[slot], sems.at[slot])


def fetch_all(count, block_refs, first, held_ref, sems):
    each = block_refs[0].shape[0]
    for slot in range(held_ref.shape[0]):

        @pl.when(slot < count)
        def _():
            fetch(block_refs[slot // each], first + slot % each, held_ref, sems, slot).start()


def moments_kernel(mode, orders, arrays, count_ref, coords_ref, *refs):
    block_refs, refs = refs[:arrays], refs[arrays:]
    first_ref, second_ref, out_ref, held_ref, sems, order_ref = refs
    rank = out_ref.shape[1]
    count = count_ref[0, 0]
    fetch_all(count, block_refs, 0, held_ref, sems)
    out_ref[...] = jnp.zeros_like(out_ref)
    spread_mode, tile_mode = ((1, 2), (0, 2), (1, 0))[mode]

    def add_block(slot, carry):
        first = first_ref[pl.ds(slot_rows(coords_ref, slot, spread_mode, orders[0]), W), :].astype(F32)
        second = second_ref[pl.ds(slot_rows(coords_ref, slot, tile_mode, orders[1]), W), :].astype(BF16).reshape(4, 16, rank)
        target = slot_rows(coords_ref, slot, mode, orders[2])
        fetch(block_refs[0], 0, held_ref, sems, slot).wait()
        total = jnp.zeros((W, rank), F32)
        for step in range(W // GROUP):
            left = held_ref[slot, :, step * GROUP * W : (step + 1) * GROUP * W]
            right = product_rows(first, second, step * GROUP)
            total = total + jnp.dot(left, right, preferred_element_type=F32)
        if mode == 1:
            halves = []
            for part in range(rank // LANES):
                for parity in range(2):
                    order_ref[part, pl.ds(parity, W // 2, stride=2), :] = total[
                        parity * W // 2 : (parity + 1) * W // 2, part * LANES : (part + 1) * LANES
                    ]
                halves.append(order_ref[part])
            total = jnp.concatenate(halves, 1)
        out_ref[pl.ds(target, W), :] += total
        return carry

    lax.fori_loop(0, count, add_block, 0)


SMEM_SPEC = pl.BlockSpec(memory_space=pltpu.SMEM)
HBM_SPEC = pl.BlockSpec(memory_space=pltpu.HBM)
VMEM_SPEC = pl.BlockSpec(memory_space=pltpu.VMEM)


def block_moments(mode, orders, blocks, coords, count, first, second, out_rows):
    slots = sum(part.shape[0] for part in blocks)
    shape = (slots, *blocks[0].shape[1:])
    rank = first.shape[1]
    in_hbm = lambda array: pltpu.with_memory_space_constraint(array, pltpu.HBM)
    scratch = [
        pltpu.VMEM(shape, BF16),
        pltpu.SemaphoreType.DMA((slots,)),
        pltpu.VMEM((rank // LANES, W, LANES), F32),
    ]
    return pl.pallas_call(
        functools.partial(moments_kernel, mode, orders, len(blocks)),
        in_specs=[SMEM_SPEC, SMEM_SPEC] + [HBM_SPEC] * len(blocks) + [VMEM_SPEC, VMEM_SPEC],
        out_specs=VMEM_SPEC,
        out_shape=jax.ShapeDtypeStruct((out_rows, rank), F32),
        scratch_shapes=scratch,
        compiler_params=pltpu.CompilerParams(vmem_limit_bytes=18 << 20),
        cost_estimate=pl.CostEstimate(
            flops=2 * slots * W**3 * rank, bytes_accessed=slots * W**3 * 2, transcendentals=0
        ),
    )(count, coords, *[in_hbm(part) for part in blocks], first, second)


def turn_kernel(mode, first, count_ref, blocks_ref, out_ref, held_ref, turned_ref, in_sems, out_sems, lanes_ref):
    count = jnp.clip(count_ref[0, 0] - first, 0, held_ref.shape[0])
    fetch_all(count, [blocks_ref], first, held_ref, in_sems)
    columns = W * W // LANES

    def turn(slot, carry):
        fetch(blocks_ref, 0, held_ref, in_sems, slot).wait()
        if mode == 1:
            for column in range(columns):
                lanes_ref[pl.ds(column, W, stride=STRIDE), :] = held_ref[
                    slot, :, column * LANES : (column + 1) * LANES
                ].astype(F32)
            low = lax.broadcasted_iota(jnp.int32, (columns, LANES), 1) < W
            for pair in range(W // 2):
                one = lanes_ref[2 * pair * STRIDE : 2 * pair * STRIDE + columns, :]
                two = lanes_ref[(2 * pair + 1) * STRIDE : (2 * pair + 1) * STRIDE + columns, :]
                even = jnp.where(low, one, pltpu.roll(two, W, 1)).astype(BF16)
                odd = jnp.where(low, pltpu.roll(one, W, 1), two).astype(BF16)
                turned_ref[slot, :, pair * LANES : (pair + 1) * LANES] = jnp.concatenate([even, odd], 0)
        else:
            for pair in range(W // 2):
                turned = held_ref[slot, :, pair * LANES : (pair + 1) * LANES].T
                turned_ref[slot, :, pair * LANES : (pair + 1) * LANES] = jnp.concatenate(
                    [turned[:W], turned[W:]], 1
                )
        fetch(turned_ref, slot, out_ref, out_sems, slot).start()
        return carry

    lax.fori_loop(0, count, turn, 0)

    def finish(slot, carry):
        fetch(turned_ref, slot, out_ref, out_sems, slot).wait()
        return carry

    lax.fori_loop(0, count, finish, 0)


def turned_blocks(mode, blocks, count, half):
    slots = blocks.shape[0] // 2
    shape = (slots, *blocks.shape[1:])
    return pl.pallas_call(
        functools.partial(turn_kernel, mode, half * slots),
        in_specs=[SMEM_SPEC, HBM_SPEC],
        out_specs=HBM_SPEC,
        out_shape=pltpu.HBM(shape, blocks.dtype),
        scratch_shapes=[
            pltpu.VMEM(shape, BF16),
            pltpu.VMEM(shape, BF16),
            pltpu.SemaphoreType.DMA((slots,)),
            pltpu.SemaphoreType.DMA((slots,)),
            pltpu.VMEM((W * STRIDE, LANES), F32),
        ],
        compiler_params=pltpu.CompilerParams(vmem_limit_bytes=14 << 20),
        cost_estimate=pl.CostEstimate(flops=0, bytes_accessed=blocks.size * 4, transcendentals=0),
    )(count, pltpu.with_memory_space_constraint(blocks, pltpu.HBM))


def exchange(rows, axes):
    devices = lax.axis_size(axes)
    parts = lax.all_to_all(rows, axes, split_axis=0, concat_axis=0, tiled=True)
    return parts.reshape(devices, rows.shape[0] // devices, rows.shape[1])


def spread_rows(rows, axes):
    devices = lax.axis_size(axes)
    return lax.all_to_all(jnp.tile(rows, (devices, 1)), axes, split_axis=0, concat_axis=0, tiled=True)


def swap(rows, axis, step):
    return lax.ppermute(rows, axis, [(i, i ^ step) for i in range(lax.axis_size(axis))])


def swap_pieces(rows, axis):
    devices = lax.axis_size(axis)
    each = rows.shape[0] // devices
    return [swap(rows[k * each : (k + 1) * each], axis, k) for k in range(1, devices)]


def swap_gather(rows, axis):
    even = [rows] + [swap(rows, axis, k) for k in range(2, lax.axis_size(axis), 2)]
    rows = jnp.concatenate(even, 0)
    return jnp.concatenate([rows, swap(rows, axis, 1)], 0)


def gram_local(factor):
    return jnp.dot(factor.T, factor, precision=HIGH, preferred_element_type=F32)


def exact_dot(left, right, contract):
    return lax.dot_general(left, right, (contract, ((), ())), precision=HIGH, preferred_element_type=F32)


def across_lanes(tile, lane):
    return jnp.broadcast_to(tile[:, lane : lane + 1], tile.shape)


def across_rows(tile, row):
    return jnp.broadcast_to(tile[row : row + 1, :], tile.shape)


def tree_sum(terms):
    while len(terms) > 1:
        terms = [a + b for a, b in zip(terms[::2], terms[1::2])]
    return terms[0]


def sweep_corner(entries):
    for k in range(0, 8, 2):
        at = lambda i, j: entries[(min(i, j), max(i, j))]
        a, o, d = at(k, k), at(k, k + 1), at(k + 1, k + 1)
        inverse = 1.0 / (a * d - o * o)
        w00, w01, w11 = d * inverse, -(o * inverse), a * inverse
        rest = [j for j in range(8) if j not in (k, k + 1)]
        top = {j: w00 * at(k, j) + w01 * at(k + 1, j) for j in rest}
        low = {j: w01 * at(k, j) + w11 * at(k + 1, j) for j in rest}
        swept = {(k, k): -w00, (k, k + 1): -w01, (k + 1, k + 1): -w11}
        for i in rest:
            swept[(min(k, i), max(k, i))] = top[i]
            swept[(min(k + 1, i), max(k + 1, i))] = low[i]
            for j in rest:
                if i <= j:
                    swept[(i, j)] = at(i, j) - (at(k, i) * top[j] + at(k + 1, i) * low[j])
        entries = swept
    return entries


def panel_inverse(tiles):
    shape = tiles[0].shape
    lane = lax.broadcasted_iota(jnp.int32, shape, 1)
    row = lax.broadcasted_iota(jnp.int32, shape, 0)
    for pivot in range(len(tiles)):
        tile = tiles[pivot]
        first = 8 * pivot
        columns = [across_lanes(tile, first + j) for j in range(8)]
        corner = sweep_corner({(i, j): across_rows(columns[j], i) for j in range(8) for i in range(j + 1)})
        here = (lane >= first) & (lane < first + 8)
        turned = jnp.where(here, jnp.where(lane - first == row, 1.0, 0.0), -tile)
        rows = [across_rows(turned, i) for i in range(8)]
        scaled = [tree_sum([corner[(min(i, j), max(i, j))] * rows[j] for j in range(8)]) for i in range(8)]
        swept = []
        for other, held in enumerate(tiles):
            if other == pivot:
                mine = scaled[0]
                for i in range(1, 8):
                    mine = jnp.where(row == i, scaled[i], mine)
            else:
                change = tree_sum([across_lanes(held, first + j) * scaled[j] for j in range(8)])
                mine = jnp.where(here, 0.0, held) - change
            swept.append(mine)
        tiles = swept
    return -jnp.concatenate(tiles, 0)


def on_diagonal(size):
    shape = (size, size)
    return lax.broadcasted_iota(jnp.int32, shape, 0) == lax.broadcasted_iota(jnp.int32, shape, 1)


def turned_down(across, diagonal):
    return jnp.sum(jnp.where(diagonal, across, 0.0), 1, keepdims=True)


def message_rows(devices):
    own = -(-3 * LANES // devices)
    return own, -(-(own + 2) // 8) * 8


def pack_gram(message_ref, gram, squares, devices):
    own, rows = message_rows(devices)
    packed = jnp.concatenate([gram[:LANES, :LANES], gram[:LANES, LANES:], gram[LANES:, LANES:]], 0)
    if devices * own > 3 * LANES or rows > own + 2:
        message_ref[...] = jnp.zeros_like(message_ref)
    for e in range(own):
        held = min(devices, 3 * LANES - devices * e)
        message_ref[pl.ds(e, held, stride=rows), :] = packed[devices * e : devices * e + held]
    for half in range(2):
        part = squares[:, half * LANES : (half + 1) * LANES]
        message_ref[pl.ds(own + half, devices, stride=rows), :] = jnp.broadcast_to(part, (devices, LANES))


def fold_messages(parts_ref, spread_ref, devices):
    rows = message_rows(devices)[1]
    terms = [parts_ref[rows * d : rows * (d + 1), :] for d in range(devices)]
    total = functools.reduce(jnp.add, terms)
    for d in range(devices):
        spread_ref[rows * d : rows * (d + 1), :] = total


def unpack_gram(ref, devices):
    if ref.shape[1] != LANES:
        return ref[...]
    own, rows = message_rows(devices)
    pieces = []
    for e in range(own):
        held = min(devices, 3 * LANES - devices * e)
        pieces.append(ref[pl.ds(e, held, stride=rows), :])
    packed = jnp.concatenate(pieces, 0)
    first, corner, last = packed[:LANES], packed[LANES : 2 * LANES], packed[2 * LANES :]
    return jnp.concatenate(
        [jnp.concatenate([first, corner], 1), jnp.concatenate([corner.T, last], 1)], 0
    )


def swap_all(messages):
    return lax.all_to_all(messages, BOTH, split_axis=0, concat_axis=0, tiled=True)


def gram_message_kernel(devices, factor_ref, message_ref):
    factor = factor_ref[...]
    squares = jnp.sum(factor * factor, 0, keepdims=True)
    pack_gram(message_ref, exact_dot(factor, factor, ((0,), (0,))), squares, devices)


def fold_kernel(devices, parts_ref, spread_ref):
    fold_messages(parts_ref, spread_ref, devices)


def message_shape(devices):
    return jax.ShapeDtypeStruct((devices * message_rows(devices)[1], LANES), F32)


def gram_message(factor, devices):
    return pl.pallas_call(
        functools.partial(gram_message_kernel, devices),
        out_shape=message_shape(devices),
        compiler_params=pltpu.CompilerParams(vmem_limit_bytes=10 << 20),
    )(factor)


def fold(parts, devices):
    return pl.pallas_call(
        functools.partial(fold_kernel, devices),
        out_shape=message_shape(devices),
        compiler_params=pltpu.CompilerParams(vmem_limit_bytes=10 << 20),
    )(parts)


def on_diagonal(size):
    shape = (size, size)
    return lax.broadcasted_iota(jnp.int32, shape, 0) == lax.broadcasted_iota(jnp.int32, shape, 1)


def turned_down(across, diagonal):
    return jnp.sum(jnp.where(diagonal, across, 0.0), 1, keepdims=True)


def inverse_kernel(devices, totals, one_ref, one_scale_ref, two_ref, two_scale_ref, out_ref, held_ref):
    size = held_ref.shape[0]
    diagonal = on_diagonal(size)
    system = None
    for total, gram_ref, scale_ref in zip(totals, (one_ref, two_ref), (one_scale_ref, two_scale_ref)):
        inverse_scale = 1.0 / scale_ref[...]
        gram = unpack_gram(gram_ref, devices) * (inverse_scale / total) * turned_down(inverse_scale, diagonal)
        system = gram if system is None else system * gram
    across = lax.rsqrt(jnp.sum(jnp.where(diagonal, system, 0.0), 0, keepdims=True))
    down = turned_down(across, diagonal)
    held_ref[...] = system * across * down
    here = lax.broadcasted_iota(jnp.int32, (1, size), 1) < PANEL
    rest = size - PANEL

    def eliminate(step, carry):
        pivot = panel_inverse([held_ref[8 * g : 8 * g + 8, :PANEL] for g in range(PANEL // 8)])
        rows = held_ref[:PANEL, :]
        scaled = exact_dot(pivot, rows, ((1,), (0,)))
        minus = jnp.concatenate([-pivot, jnp.zeros((PANEL, rest), F32)], 1)
        scaled = jnp.where(here, minus, scaled)
        others = jnp.where(here, 0.0, held_ref[PANEL:, :]) - exact_dot(
            rows[:, PANEL:], scaled, ((0,), (0,))
        )
        held_ref[:rest, :] = pltpu.roll(others, rest, 1)
        held_ref[rest:, :] = pltpu.roll(scaled, rest, 1)
        return carry

    lax.fori_loop(0, size // PANEL, eliminate, 0)
    out_ref[...] = -held_ref[...] * across * down


def product_inverse(one, two, devices):
    rank = one[2].shape[1]
    return pl.pallas_call(
        functools.partial(inverse_kernel, devices, (one[1], two[1])),
        out_shape=jax.ShapeDtypeStruct((rank, rank), F32),
        scratch_shapes=[pltpu.VMEM((rank, rank), F32)],
        compiler_params=pltpu.CompilerParams(vmem_limit_bytes=10 << 20),
        cost_estimate=pl.CostEstimate(flops=10**10, bytes_accessed=3 << 18, transcendentals=0),
    )(one[0], one[2], two[0], two[2])


def solve_kernel(devices, stacked, parts, *refs):
    inverse_ref, outs = refs[parts], refs[parts + 1 :]
    if stacked:
        terms = [refs[0][part] for part in range(refs[0].shape[0])]
    else:
        terms = [ref[...] for ref in refs[:parts]]
    raw = exact_dot(functools.reduce(jnp.add, terms), inverse_ref[...], ((1,), (0,)))
    outs[0][...] = raw
    if len(outs) > 1:
        squares = jnp.sum(raw * raw, 0, keepdims=True)
        pack_gram(outs[1], exact_dot(raw, raw, ((0,), (0,))), squares, devices)


def solve_swapped(own, others, inverse, devices):
    rows, rank = others[0].shape
    whole = pl.BlockSpec((rows, rank), lambda step: (0, 0))
    square = pl.BlockSpec((rank, rank), lambda step: (0, 0))
    messages = message_shape(devices)
    return pl.pallas_call(
        functools.partial(solve_kernel, devices, False, 1 + len(others)),
        grid=(1,),
        in_specs=[whole] * (1 + len(others)) + [square],
        out_specs=[whole, pl.BlockSpec(messages.shape, lambda step: (0, 0))],
        out_shape=[jax.ShapeDtypeStruct((rows, rank), F32), messages],
        compiler_params=pltpu.CompilerParams(vmem_limit_bytes=12 << 20),
    )(own, *others, inverse)


def solve_stacked(parts, inverse, devices, with_gram):
    out_shape = [jax.ShapeDtypeStruct(parts.shape[1:], F32)]
    if with_gram:
        out_shape.append(message_shape(devices))
    return pl.pallas_call(
        functools.partial(solve_kernel, devices, True, 1),
        out_shape=out_shape,
        compiler_params=pltpu.CompilerParams(vmem_limit_bytes=10 << 20),
    )(parts, inverse)


def scale_kernel(devices, row_total, parts_ref, raw_ref, factor_ref, rounded_ref, scale_ref):
    own, rows = message_rows(devices)
    total = functools.reduce(jnp.add, [parts_ref[rows * d + own : rows * d + own + 2, :] for d in range(devices)])
    squares = jnp.concatenate([total[:1], total[1:2]], 1)
    scale = jnp.sqrt(squares / row_total + EPS)
    scale_ref[...] = scale
    factor = raw_ref[...] / scale
    factor_ref[...] = factor
    rounded_ref[...] = factor.astype(BF16)


def scale_rows(messages, raw, row_total, devices):
    return pl.pallas_call(
        functools.partial(scale_kernel, devices, row_total),
        out_shape=[
            jax.ShapeDtypeStruct(raw.shape, F32),
            jax.ShapeDtypeStruct(raw.shape, BF16),
            jax.ShapeDtypeStruct((1, raw.shape[1]), F32),
        ],
        compiler_params=pltpu.CompilerParams(vmem_limit_bytes=10 << 20),
    )(messages, raw)


def on_device(blocks, coords, counts, b_init, c_init):
    slab_count = lax.axis_size("slab")
    grid_count = lax.axis_size("grid")
    local_blocks = blocks[0, 0]
    doc_rows = IBP * W
    term_rows = JBP * W
    doc_total = doc_rows * slab_count
    term_total = term_rows * grid_count
    month_total = c_init.shape[0]
    devices = slab_count * grid_count
    ones = jnp.ones((1, c_init.shape[1]), F32)
    messages_b, b_rounded = lax.optimization_barrier((gram_message(b_init, devices), b_init.astype(BF16)))
    messages_b = swap_all(messages_b)
    even = [b_rounded] + [swap(b_rounded, "slab", k) for k in range(2, slab_count, 2)]
    held_blocks, even[-1] = lax.optimization_barrier((local_blocks, even[-1]))
    terms_one = turned_blocks(1, held_blocks, counts, 0)
    messages_b, terms_one = lax.optimization_barrier((messages_b, terms_one))
    even = jnp.concatenate(even, 0)
    term_panel = jnp.concatenate([even, swap(even, "slab", 1)], 0)
    spread_b, term_panel = lax.optimization_barrier((fold(messages_b, devices), term_panel))
    gram_b = (swap_all(spread_b), term_total, ones)
    moments_a = block_moments(
        0, (TERM_ORDER, None, DOC_ORDER), [local_blocks], coords, counts, term_panel, c_init, doc_rows
    )
    others_a = swap_pieces(moments_a, "grid")
    c_held, _ = lax.optimization_barrier((c_init, moments_a))
    gram_c = (gram_local(c_held), month_total, ones)
    inverse_a = product_inverse(gram_b, gram_c, devices)
    held_blocks, inverse_a = lax.optimization_barrier((local_blocks, inverse_a))
    terms_two = turned_blocks(1, held_blocks, counts, 1)
    inverse_a, terms_two = lax.optimization_barrier((inverse_a, terms_two))
    raw_a, messages_a = solve_swapped(moments_a, others_a, inverse_a, devices)
    held_blocks, messages_a = lax.optimization_barrier((local_blocks, messages_a))
    months_one = turned_blocks(2, held_blocks, counts, 0)
    messages_a, months_one = lax.optimization_barrier((swap_all(messages_a), months_one))
    factor_a, rounded_a, scale_a = scale_rows(messages_a, raw_a, doc_total, devices)
    pieces = [rounded_a] + [swap(rounded_a, "grid", k) for k in range(1, grid_count)]
    messages_a, pieces[1] = lax.optimization_barrier((messages_a, pieces[1]))
    doc_panel = jnp.concatenate(pieces, 0)
    spread_a = fold(messages_a, devices)
    gram_a = (swap_all(spread_a), doc_total, scale_a)

    moments_b = block_moments(
        1, (DOC_ORDER, None, None), [terms_one, terms_two], coords, counts, doc_panel, c_init, term_rows
    )
    parts_b = exchange(moments_b, "slab")
    inverse_b = product_inverse(gram_a, gram_c, devices)
    raw_b, messages_n = solve_stacked(parts_b, inverse_b, devices, True)
    held_blocks, messages_n = lax.optimization_barrier((local_blocks, messages_n))
    months_two = turned_blocks(2, held_blocks, counts, 1)
    messages_n, months_two = lax.optimization_barrier((swap_all(messages_n), months_two))
    factor_b, rounded_b, scale_b = scale_rows(messages_n, raw_b, term_total, devices)
    term_panel_new = swap_gather(rounded_b, "slab")
    messages_n, _ = lax.optimization_barrier((messages_n, rounded_b))
    spread_n = fold(messages_n, devices)
    gram_bn = (swap_all(spread_n), term_total, scale_b)

    moments_c = block_moments(
        2, (TERM_ORDER, DOC_ORDER, None), [months_one, months_two], coords, counts, term_panel_new, doc_panel, month_total
    )
    parts_c = exchange(moments_c, BOTH)
    inverse_c = product_inverse(gram_a, gram_bn, devices)
    (raw_own,) = solve_stacked(parts_c, inverse_c, devices, False)
    raw_c = spread_rows(raw_own, BOTH)
    column_scale = jnp.sqrt(jnp.mean(raw_c * raw_c, axis=0) + EPS)
    return (factor_a, factor_b, raw_c / column_scale)


def solution(mesh):
    in_specs = (
        P("slab", "grid", None, None, None),
        P("slab", "grid", None, None),
        P("slab", "grid"),
        P(("slab", "grid"), None),
        P(),
    )
    out_specs = (P(("slab", "grid"), None), P(("slab", "grid"), None), P())
    return jax.shard_map(
        on_device, mesh=mesh, in_specs=in_specs, out_specs=out_specs, check_vma=False
    )
```

```python
import functools

import jax
import jax.numpy as jnp
from jax import lax
from jax.experimental import pallas as pl
from jax.experimental.pallas import tpu as pltpu
from jax.sharding import PartitionSpec as P

W = 64
IBP = 16
JBP = 16
LANES = 128
STRIDE = 40
PANEL = 128
GROUP = 4

HIGH = lax.Precision.HIGHEST
EPS = 1e-05
BOTH = ("slab", "grid")
TERM_ORDER, DOC_ORDER = ("slab", True), ("grid", False)
F32 = jnp.float32
BF16 = jnp.bfloat16


def product_rows(first, second, start):
    rank = first.shape[1]
    pieces = []
    for row in range(start, start + GROUP):
        spread = jnp.broadcast_to(first[row : row + 1, :], (16, rank)).astype(BF16)
        pieces.append((second * spread[None]).reshape(W, rank))
    return jnp.concatenate(pieces, 0)


def slot_rows(coords_ref, slot, mode, order):
    block = coords_ref[0, 0, slot, mode]
    if order is not None:
        axis, paired = order
        devices = lax.axis_size(axis)
        each = IBP // devices
        place = (block // each) ^ lax.axis_index(axis)
        if paired:
            place = place // 2 + place % 2 * (devices // 2)
        block = place * each + block % each
    return pl.multiple_of(block * W, W)


def fetch(source_ref, source, held_ref, sems, slot):
    return pltpu.make_async_copy(source_ref.at[source], held_ref.at[slot], sems.at[slot])


def fetch_all(count, block_refs, first, held_ref, sems):
    each = block_refs[0].shape[0]
    for slot in range(held_ref.shape[0]):

        @pl.when(slot < count)
        def _():
            fetch(block_refs[slot // each], first + slot % each, held_ref, sems, slot).start()


def moments_kernel(mode, orders, arrays, count_ref, coords_ref, *refs):
    block_refs, refs = refs[:arrays], refs[arrays:]
    first_ref, second_ref, out_ref, held_ref, sems, order_ref = refs
    rank = out_ref.shape[1]
    count = count_ref[0, 0]
    fetch_all(count, block_refs, 0, held_ref, sems)
    out_ref[...] = jnp.zeros_like(out_ref)
    spread_mode, tile_mode = ((1, 2), (0, 2), (1, 0))[mode]

    def add_block(slot, carry):
        first = first_ref[pl.ds(slot_rows(coords_ref, slot, spread_mode, orders[0]), W), :].astype(BF16).astype(F32)
        second = second_ref[pl.ds(slot_rows(coords_ref, slot, tile_mode, orders[1]), W), :].astype(BF16).reshape(4, 16, rank)
        target = slot_rows(coords_ref, slot, mode, orders[2])
        fetch(block_refs[0], 0, held_ref, sems, slot).wait()
        total = jnp.zeros((W, rank), F32)
        for step in range(W // GROUP):
            left = held_ref[slot, :, step * GROUP * W : (step + 1) * GROUP * W]
            right = product_rows(first, second, step * GROUP)
            total = total + jnp.dot(left, right, preferred_element_type=F32)
        if mode == 1:
            halves = []
            for part in range(rank // LANES):
                for parity in range(2):
                    order_ref[part, pl.ds(parity, W // 2, stride=2), :] = total[
                        parity * W // 2 : (parity + 1) * W // 2, part * LANES : (part + 1) * LANES
                    ]
                halves.append(order_ref[part])
            total = jnp.concatenate(halves, 1)
        out_ref[pl.ds(target, W), :] += total
        return carry

    lax.fori_loop(0, count, add_block, 0)


SMEM_SPEC = pl.BlockSpec(memory_space=pltpu.SMEM)
HBM_SPEC = pl.BlockSpec(memory_space=pltpu.HBM)
VMEM_SPEC = pl.BlockSpec(memory_space=pltpu.VMEM)


def block_moments(mode, orders, blocks, coords, count, first, second, out_rows):
    slots = sum(part.shape[0] for part in blocks)
    shape = (slots, *blocks[0].shape[1:])
    rank = first.shape[1]
    in_hbm = lambda array: pltpu.with_memory_space_constraint(array, pltpu.HBM)
    scratch = [
        pltpu.VMEM(shape, BF16),
        pltpu.SemaphoreType.DMA((slots,)),
        pltpu.VMEM((rank // LANES, W, LANES), F32),
    ]
    return pl.pallas_call(
        functools.partial(moments_kernel, mode, orders, len(blocks)),
        in_specs=[SMEM_SPEC, SMEM_SPEC] + [HBM_SPEC] * len(blocks) + [VMEM_SPEC, VMEM_SPEC],
        out_specs=VMEM_SPEC,
        out_shape=jax.ShapeDtypeStruct((out_rows, rank), F32),
        scratch_shapes=scratch,
        compiler_params=pltpu.CompilerParams(vmem_limit_bytes=18 << 20),
        cost_estimate=pl.CostEstimate(
            flops=2 * slots * W**3 * rank, bytes_accessed=slots * W**3 * 2, transcendentals=0
        ),
    )(count, coords, *[in_hbm(part) for part in blocks], first, second)


def turn_kernel(mode, first, count_ref, blocks_ref, out_ref, held_ref, turned_ref, in_sems, out_sems, lanes_ref):
    count = jnp.clip(count_ref[0, 0] - first, 0, held_ref.shape[0])
    fetch_all(count, [blocks_ref], first, held_ref, in_sems)
    columns = W * W // LANES

    def turn(slot, carry):
        fetch(blocks_ref, 0, held_ref, in_sems, slot).wait()
        if mode == 1:
            for column in range(columns):
                lanes_ref[pl.ds(column, W, stride=STRIDE), :] = held_ref[
                    slot, :, column * LANES : (column + 1) * LANES
                ].astype(F32)
            low = lax.broadcasted_iota(jnp.int32, (columns, LANES), 1) < W
            for pair in range(W // 2):
                one = lanes_ref[2 * pair * STRIDE : 2 * pair * STRIDE + columns, :]
                two = lanes_ref[(2 * pair + 1) * STRIDE : (2 * pair + 1) * STRIDE + columns, :]
                even = jnp.where(low, one, pltpu.roll(two, W, 1)).astype(BF16)
                odd = jnp.where(low, pltpu.roll(one, W, 1), two).astype(BF16)
                turned_ref[slot, :, pair * LANES : (pair + 1) * LANES] = jnp.concatenate([even, odd], 0)
        else:
            for pair in range(W // 2):
                turned = held_ref[slot, :, pair * LANES : (pair + 1) * LANES].T
                turned_ref[slot, :, pair * LANES : (pair + 1) * LANES] = jnp.concatenate(
                    [turned[:W], turned[W:]], 1
                )
        fetch(turned_ref, slot, out_ref, out_sems, slot).start()
        return carry

    lax.fori_loop(0, count, turn, 0)

    def finish(slot, carry):
        fetch(turned_ref, slot, out_ref, out_sems, slot).wait()
        return carry

    lax.fori_loop(0, count, finish, 0)


def turned_blocks(mode, blocks, count, half):
    slots = blocks.shape[0] // 2
    shape = (slots, *blocks.shape[1:])
    return pl.pallas_call(
        functools.partial(turn_kernel, mode, half * slots),
        in_specs=[SMEM_SPEC, HBM_SPEC],
        out_specs=HBM_SPEC,
        out_shape=pltpu.HBM(shape, blocks.dtype),
        scratch_shapes=[
            pltpu.VMEM(shape, BF16),
            pltpu.VMEM(shape, BF16),
            pltpu.SemaphoreType.DMA((slots,)),
            pltpu.SemaphoreType.DMA((slots,)),
            pltpu.VMEM((W * STRIDE, LANES), F32),
        ],
        compiler_params=pltpu.CompilerParams(vmem_limit_bytes=14 << 20),
        cost_estimate=pl.CostEstimate(flops=0, bytes_accessed=blocks.size * 4, transcendentals=0),
    )(count, pltpu.with_memory_space_constraint(blocks, pltpu.HBM))


def exchange(rows, axes):
    devices = lax.axis_size(axes)
    parts = lax.all_to_all(rows, axes, split_axis=0, concat_axis=0, tiled=True)
    return parts.reshape(devices, rows.shape[0] // devices, rows.shape[1])


def spread_rows(rows, axes):
    devices = lax.axis_size(axes)
    return lax.all_to_all(jnp.tile(rows, (devices, 1)), axes, split_axis=0, concat_axis=0, tiled=True)


def swap(rows, axis, step):
    return lax.ppermute(rows, axis, [(i, i ^ step) for i in range(lax.axis_size(axis))])


def swap_pieces(rows, axis):
    devices = lax.axis_size(axis)
    each = rows.shape[0] // devices
    return [swap(rows[k * each : (k + 1) * each], axis, k) for k in range(1, devices)]


def swap_gather(rows, axis):
    even = [rows] + [swap(rows, axis, k) for k in range(2, lax.axis_size(axis), 2)]
    rows = jnp.concatenate(even, 0)
    return jnp.concatenate([rows, swap(rows, axis, 1)], 0)


def gram_local(factor):
    return jnp.dot(factor.T, factor, precision=HIGH, preferred_element_type=F32)


def exact_dot(left, right, contract):
    return lax.dot_general(left, right, (contract, ((), ())), precision=HIGH, preferred_element_type=F32)


def across_lanes(tile, lane):
    return jnp.broadcast_to(tile[:, lane : lane + 1], tile.shape)


def across_rows(tile, row):
    return jnp.broadcast_to(tile[row : row + 1, :], tile.shape)


def tree_sum(terms):
    while len(terms) > 1:
        terms = [a + b for a, b in zip(terms[::2], terms[1::2])]
    return terms[0]


def sweep_corner(entries):
    for k in range(0, 8, 2):
        at = lambda i, j: entries[(min(i, j), max(i, j))]
        a, o, d = at(k, k), at(k, k + 1), at(k + 1, k + 1)
        inverse = 1.0 / (a * d - o * o)
        w00, w01, w11 = d * inverse, -(o * inverse), a * inverse
        rest = [j for j in range(8) if j not in (k, k + 1)]
        top = {j: w00 * at(k, j) + w01 * at(k + 1, j) for j in rest}
        low = {j: w01 * at(k, j) + w11 * at(k + 1, j) for j in rest}
        swept = {(k, k): -w00, (k, k + 1): -w01, (k + 1, k + 1): -w11}
        for i in rest:
            swept[(min(k, i), max(k, i))] = top[i]
            swept[(min(k + 1, i), max(k + 1, i))] = low[i]
            for j in rest:
                if i <= j:
                    swept[(i, j)] = at(i, j) - (at(k, i) * top[j] + at(k + 1, i) * low[j])
        entries = swept
    return entries


def panel_inverse(tiles):
    shape = tiles[0].shape
    lane = lax.broadcasted_iota(jnp.int32, shape, 1)
    row = lax.broadcasted_iota(jnp.int32, shape, 0)
    for pivot in range(len(tiles)):
        tile = tiles[pivot]
        first = 8 * pivot
        columns = [across_lanes(tile, first + j) for j in range(8)]
        corner = sweep_corner({(i, j): across_rows(columns[j], i) for j in range(8) for i in range(j + 1)})
        here = (lane >= first) & (lane < first + 8)
        turned = jnp.where(here, jnp.where(lane - first == row, 1.0, 0.0), -tile)
        rows = [across_rows(turned, i) for i in range(8)]
        scaled = [tree_sum([corner[(min(i, j), max(i, j))] * rows[j] for j in range(8)]) for i in range(8)]
        swept = []
        for other, held in enumerate(tiles):
            if other == pivot:
                mine = scaled[0]
                for i in range(1, 8):
                    mine = jnp.where(row == i, scaled[i], mine)
            else:
                change = tree_sum([across_lanes(held, first + j) * scaled[j] for j in range(8)])
                mine = jnp.where(here, 0.0, held) - change
            swept.append(mine)
        tiles = swept
    return -jnp.concatenate(tiles, 0)


def on_diagonal(size):
    shape = (size, size)
    return lax.broadcasted_iota(jnp.int32, shape, 0) == lax.broadcasted_iota(jnp.int32, shape, 1)


def turned_down(across, diagonal):
    return jnp.sum(jnp.where(diagonal, across, 0.0), 1, keepdims=True)


def message_rows(devices):
    own = -(-3 * LANES // devices)
    return own, -(-(own + 2) // 8) * 8


def packed_blocks(gram):
    return jnp.concatenate([gram[:LANES, :LANES], gram[:LANES, LANES:], gram[LANES:, LANES:]], 0)


def pack_gram(message_ref, gram, squares, devices):
    own, rows = message_rows(devices)
    packed = packed_blocks(gram)
    if devices * own > 3 * LANES or rows > own + 2:
        message_ref[...] = jnp.zeros_like(message_ref)
    for e in range(own):
        held = min(devices, 3 * LANES - devices * e)
        message_ref[pl.ds(e, held, stride=rows), :] = packed[devices * e : devices * e + held]
    for half in range(2):
        part = squares[:, half * LANES : (half + 1) * LANES]
        message_ref[pl.ds(own + half, devices, stride=rows), :] = jnp.broadcast_to(part, (devices, LANES))


def fold_messages(parts_ref, spread_ref, devices):
    rows = message_rows(devices)[1]
    terms = [parts_ref[rows * d : rows * (d + 1), :] for d in range(devices)]
    total = functools.reduce(jnp.add, terms)
    for d in range(devices):
        spread_ref[rows * d : rows * (d + 1), :] = total


def unpack_gram(ref, devices):
    if ref.shape[1] != LANES:
        return ref[...]
    if ref.shape[0] == 3 * LANES:
        packed = ref[...]
    else:
        own, rows = message_rows(devices)
        pieces = []
        for e in range(own):
            held = min(devices, 3 * LANES - devices * e)
            pieces.append(ref[pl.ds(e, held, stride=rows), :])
        packed = jnp.concatenate(pieces, 0)
    first, corner, last = packed[:LANES], packed[LANES : 2 * LANES], packed[2 * LANES :]
    return jnp.concatenate(
        [jnp.concatenate([first, corner], 1), jnp.concatenate([corner.T, last], 1)], 0
    )


def swap_all(messages):
    return lax.all_to_all(messages, BOTH, split_axis=0, concat_axis=0, tiled=True)


def panel_gram_kernel(panel_ref, packed_ref):
    panel = panel_ref[...]
    packed_ref[...] = packed_blocks(exact_dot(panel, panel, ((0,), (0,))))


def fold_kernel(devices, parts_ref, spread_ref):
    fold_messages(parts_ref, spread_ref, devices)


def message_shape(devices):
    return jax.ShapeDtypeStruct((devices * message_rows(devices)[1], LANES), F32)


def panel_gram(panel):
    return pl.pallas_call(
        panel_gram_kernel,
        out_shape=jax.ShapeDtypeStruct((3 * LANES, LANES), F32),
        compiler_params=pltpu.CompilerParams(vmem_limit_bytes=10 << 20),
    )(panel)


def fold(parts, devices):
    return pl.pallas_call(
        functools.partial(fold_kernel, devices),
        out_shape=message_shape(devices),
        compiler_params=pltpu.CompilerParams(vmem_limit_bytes=10 << 20),
    )(parts)


def on_diagonal(size):
    shape = (size, size)
    return lax.broadcasted_iota(jnp.int32, shape, 0) == lax.broadcasted_iota(jnp.int32, shape, 1)


def turned_down(across, diagonal):
    return jnp.sum(jnp.where(diagonal, across, 0.0), 1, keepdims=True)


def inverse_kernel(devices, totals, one_ref, one_scale_ref, two_ref, two_scale_ref, out_ref, held_ref):
    size = held_ref.shape[0]
    diagonal = on_diagonal(size)
    system = None
    for total, gram_ref, scale_ref in zip(totals, (one_ref, two_ref), (one_scale_ref, two_scale_ref)):
        inverse_scale = 1.0 / scale_ref[...]
        gram = unpack_gram(gram_ref, devices) * (inverse_scale / total) * turned_down(inverse_scale, diagonal)
        system = gram if system is None else system * gram
    across = lax.rsqrt(jnp.sum(jnp.where(diagonal, system, 0.0), 0, keepdims=True))
    down = turned_down(across, diagonal)
    held_ref[...] = system * across * down
    here = lax.broadcasted_iota(jnp.int32, (1, size), 1) < PANEL
    rest = size - PANEL

    def eliminate(step, carry):
        pivot = panel_inverse([held_ref[8 * g : 8 * g + 8, :PANEL] for g in range(PANEL // 8)])
        rows = held_ref[:PANEL, :]
        scaled = exact_dot(pivot, rows, ((1,), (0,)))
        minus = jnp.concatenate([-pivot, jnp.zeros((PANEL, rest), F32)], 1)
        scaled = jnp.where(here, minus, scaled)
        others = jnp.where(here, 0.0, held_ref[PANEL:, :]) - exact_dot(
            rows[:, PANEL:], scaled, ((0,), (0,))
        )
        held_ref[:rest, :] = pltpu.roll(others, rest, 1)
        held_ref[rest:, :] = pltpu.roll(scaled, rest, 1)
        return carry

    lax.fori_loop(0, size // PANEL, eliminate, 0)
    out_ref[...] = -held_ref[...] * across * down


def product_inverse(one, two, devices):
    rank = one[2].shape[1]
    return pl.pallas_call(
        functools.partial(inverse_kernel, devices, (one[1], two[1])),
        out_shape=jax.ShapeDtypeStruct((rank, rank), F32),
        scratch_shapes=[pltpu.VMEM((rank, rank), F32)],
        compiler_params=pltpu.CompilerParams(vmem_limit_bytes=10 << 20),
        cost_estimate=pl.CostEstimate(flops=10**10, bytes_accessed=3 << 18, transcendentals=0),
    )(one[0], one[2], two[0], two[2])


def solve_kernel(devices, stacked, parts, *refs):
    inverse_ref, outs = refs[parts], refs[parts + 1 :]
    if stacked:
        terms = [refs[0][part] for part in range(refs[0].shape[0])]
    else:
        terms = [ref[...] for ref in refs[:parts]]
    raw = exact_dot(functools.reduce(jnp.add, terms), inverse_ref[...], ((1,), (0,)))
    outs[0][...] = raw
    if len(outs) > 1:
        squares = jnp.sum(raw * raw, 0, keepdims=True)
        pack_gram(outs[1], exact_dot(raw, raw, ((0,), (0,))), squares, devices)


def solve_swapped(own, others, inverse, devices):
    rows, rank = others[0].shape
    whole = pl.BlockSpec((rows, rank), lambda step: (0, 0))
    square = pl.BlockSpec((rank, rank), lambda step: (0, 0))
    messages = message_shape(devices)
    return pl.pallas_call(
        functools.partial(solve_kernel, devices, False, 1 + len(others)),
        grid=(1,),
        in_specs=[whole] * (1 + len(others)) + [square],
        out_specs=[whole, pl.BlockSpec(messages.shape, lambda step: (0, 0))],
        out_shape=[jax.ShapeDtypeStruct((rows, rank), F32), messages],
        compiler_params=pltpu.CompilerParams(vmem_limit_bytes=12 << 20),
    )(own, *others, inverse)


def solve_stacked(parts, inverse, devices, with_gram):
    out_shape = [jax.ShapeDtypeStruct(parts.shape[1:], F32)]
    if with_gram:
        out_shape.append(message_shape(devices))
    return pl.pallas_call(
        functools.partial(solve_kernel, devices, True, 1),
        out_shape=out_shape,
        compiler_params=pltpu.CompilerParams(vmem_limit_bytes=10 << 20),
    )(parts, inverse)


def scale_kernel(devices, row_total, parts_ref, raw_ref, factor_ref, rounded_ref, scale_ref):
    own, rows = message_rows(devices)
    total = functools.reduce(jnp.add, [parts_ref[rows * d + own : rows * d + own + 2, :] for d in range(devices)])
    squares = jnp.concatenate([total[:1], total[1:2]], 1)
    scale = jnp.sqrt(squares / row_total + EPS)
    scale_ref[...] = scale
    factor = raw_ref[...] / scale
    factor_ref[...] = factor
    rounded_ref[...] = factor.astype(BF16)


def scale_rows(messages, raw, row_total, devices):
    return pl.pallas_call(
        functools.partial(scale_kernel, devices, row_total),
        out_shape=[
            jax.ShapeDtypeStruct(raw.shape, F32),
            jax.ShapeDtypeStruct(raw.shape, BF16),
            jax.ShapeDtypeStruct((1, raw.shape[1]), F32),
        ],
        compiler_params=pltpu.CompilerParams(vmem_limit_bytes=10 << 20),
    )(messages, raw)


def on_device(blocks, coords, counts, b_init, c_init):
    slab_count = lax.axis_size("slab")
    grid_count = lax.axis_size("grid")
    local_blocks = blocks[0, 0]
    doc_rows = IBP * W
    term_rows = JBP * W
    doc_total = doc_rows * slab_count
    term_total = term_rows * grid_count
    month_total = c_init.shape[0]
    devices = slab_count * grid_count
    ones = jnp.ones((1, c_init.shape[1]), F32)
    even = [b_init] + [swap(b_init, "slab", k) for k in range(2, slab_count, 2)]
    held_blocks, even[1] = lax.optimization_barrier((local_blocks, even[1]))
    terms_one = turned_blocks(1, held_blocks, counts, 0)
    even, terms_one = lax.optimization_barrier((even, terms_one))
    even = jnp.concatenate(even, 0)
    term_panel = jnp.concatenate([even, swap(even, "slab", 1)], 0)
    own_gram_b = panel_gram(term_panel)
    own_gram_b, term_panel = lax.optimization_barrier((own_gram_b, term_panel))
    grams_b = [own_gram_b] + [swap(own_gram_b, "grid", k) for k in range(1, grid_count)]
    moments_a = block_moments(
        0, (TERM_ORDER, None, DOC_ORDER), [local_blocks], coords, counts, term_panel, c_init, doc_rows
    )
    grams_b, moments_a = lax.optimization_barrier((grams_b, moments_a))
    others_a = swap_pieces(moments_a, "grid")
    gram_b = (functools.reduce(jnp.add, grams_b), term_total, ones)
    c_held, _ = lax.optimization_barrier((c_init, moments_a))
    gram_c = (gram_local(c_held), month_total, ones)
    inverse_a = product_inverse(gram_b, gram_c, devices)
    held_blocks, inverse_a = lax.optimization_barrier((local_blocks, inverse_a))
    terms_two = turned_blocks(1, held_blocks, counts, 1)
    inverse_a, terms_two = lax.optimization_barrier((inverse_a, terms_two))
    raw_a, messages_a = solve_swapped(moments_a, others_a, inverse_a, devices)
    held_blocks, messages_a = lax.optimization_barrier((local_blocks, messages_a))
    months_one = turned_blocks(2, held_blocks, counts, 0)
    messages_a, months_one = lax.optimization_barrier((swap_all(messages_a), months_one))
    factor_a, rounded_a, scale_a = scale_rows(messages_a, raw_a, doc_total, devices)
    pieces = [rounded_a] + [swap(rounded_a, "grid", k) for k in range(1, grid_count)]
    messages_a, pieces[1] = lax.optimization_barrier((messages_a, pieces[1]))
    doc_panel = jnp.concatenate(pieces, 0)
    spread_a = fold(messages_a, devices)
    gram_a = (swap_all(spread_a), doc_total, scale_a)

    moments_b = block_moments(
        1, (DOC_ORDER, None, None), [terms_one, terms_two], coords, counts, doc_panel, c_init, term_rows
    )
    parts_b = exchange(moments_b, "slab")
    inverse_b = product_inverse(gram_a, gram_c, devices)
    raw_b, messages_n = solve_stacked(parts_b, inverse_b, devices, True)
    held_blocks, messages_n = lax.optimization_barrier((local_blocks, messages_n))
    months_two = turned_blocks(2, held_blocks, counts, 1)
    messages_n, months_two = lax.optimization_barrier((swap_all(messages_n), months_two))
    factor_b, rounded_b, scale_b = scale_rows(messages_n, raw_b, term_total, devices)
    term_panel_new = swap_gather(rounded_b, "slab")
    messages_n, _ = lax.optimization_barrier((messages_n, rounded_b))
    spread_n = fold(messages_n, devices)
    gram_bn = (swap_all(spread_n), term_total, scale_b)

    moments_c = block_moments(
        2, (TERM_ORDER, DOC_ORDER, None), [months_one, months_two], coords, counts, term_panel_new, doc_panel, month_total
    )
    parts_c = exchange(moments_c, BOTH)
    inverse_c = product_inverse(gram_a, gram_bn, devices)
    (raw_own,) = solve_stacked(parts_c, inverse_c, devices, False)
    raw_c = spread_rows(raw_own, BOTH)
    column_scale = jnp.sqrt(jnp.mean(raw_c * raw_c, axis=0) + EPS)
    return (factor_a, factor_b, raw_c / column_scale)


def solution(mesh):
    in_specs = (
        P("slab", "grid", None, None, None),
        P("slab", "grid", None, None),
        P("slab", "grid"),
        P(("slab", "grid"), None),
        P(),
    )
    out_specs = (P(("slab", "grid"), None), P(("slab", "grid"), None), P())
    return jax.shard_map(
        on_device, mesh=mesh, in_specs=in_specs, out_specs=out_specs, check_vma=False
    )
```

```python
import functools

import jax
import jax.numpy as jnp
from jax import lax
from jax.experimental import pallas as pl
from jax.experimental.pallas import tpu as pltpu
from jax.sharding import PartitionSpec as P

W = 64
IBP = 16
JBP = 16
LANES = 128
STRIDE = 40
PANEL = 128
GROUP = 4

HIGH = lax.Precision.HIGHEST
EPS = 1e-05
BOTH = ("slab", "grid")
TERM_ORDER, DOC_ORDER = ("slab", True), ("grid", False)
F32 = jnp.float32
BF16 = jnp.bfloat16


def product_rows(first, second, start):
    rank = first.shape[1]
    pieces = []
    for row in range(start, start + GROUP):
        spread = jnp.broadcast_to(first[row : row + 1, :], (16, rank)).astype(BF16)
        pieces.append((second * spread[None]).reshape(W, rank))
    return jnp.concatenate(pieces, 0)


def slot_rows(coords_ref, slot, mode, order):
    block = coords_ref[0, 0, slot, mode]
    if order is not None:
        axis, paired = order
        devices = lax.axis_size(axis)
        each = IBP // devices
        place = (block // each) ^ lax.axis_index(axis)
        if paired:
            place = place // 2 + place % 2 * (devices // 2)
        block = place * each + block % each
    return pl.multiple_of(block * W, W)


def fetch(source_ref, source, held_ref, sems, slot):
    return pltpu.make_async_copy(source_ref.at[source], held_ref.at[slot], sems.at[slot])


def fetch_all(count, block_refs, first, held_ref, sems):
    each = block_refs[0].shape[0]
    for slot in range(held_ref.shape[0]):

        @pl.when(slot < count)
        def _():
            fetch(block_refs[slot // each], first + slot % each, held_ref, sems, slot).start()


def moments_kernel(mode, orders, arrays, count_ref, coords_ref, *refs):
    block_refs, refs = refs[:arrays], refs[arrays:]
    first_ref, second_ref, out_ref, held_ref, sems, order_ref = refs
    rank = out_ref.shape[1]
    count = count_ref[0, 0]
    fetch_all(count, block_refs, 0, held_ref, sems)
    out_ref[...] = jnp.zeros_like(out_ref)
    spread_mode, tile_mode = ((1, 2), (0, 2), (1, 0))[mode]

    def add_block(slot, carry):
        first = first_ref[pl.ds(slot_rows(coords_ref, slot, spread_mode, orders[0]), W), :].astype(BF16).astype(F32)
        second = second_ref[pl.ds(slot_rows(coords_ref, slot, tile_mode, orders[1]), W), :].astype(BF16).reshape(4, 16, rank)
        target = slot_rows(coords_ref, slot, mode, orders[2])
        fetch(block_refs[0], 0, held_ref, sems, slot).wait()
        total = jnp.zeros((W, rank), F32)
        for step in range(W // GROUP):
            left = held_ref[slot, :, step * GROUP * W : (step + 1) * GROUP * W]
            right = product_rows(first, second, step * GROUP)
            total = total + jnp.dot(left, right, preferred_element_type=F32)
        if mode == 1:
            halves = []
            for part in range(rank // LANES):
                for parity in range(2):
                    order_ref[part, pl.ds(parity, W // 2, stride=2), :] = total[
                        parity * W // 2 : (parity + 1) * W // 2, part * LANES : (part + 1) * LANES
                    ]
                halves.append(order_ref[part])
            total = jnp.concatenate(halves, 1)
        out_ref[pl.ds(target, W), :] += total
        return carry

    lax.fori_loop(0, count, add_block, 0)


SMEM_SPEC = pl.BlockSpec(memory_space=pltpu.SMEM)
HBM_SPEC = pl.BlockSpec(memory_space=pltpu.HBM)
VMEM_SPEC = pl.BlockSpec(memory_space=pltpu.VMEM)


def block_moments(mode, orders, blocks, coords, count, first, second, out_rows):
    slots = sum(part.shape[0] for part in blocks)
    shape = (slots, *blocks[0].shape[1:])
    rank = first.shape[1]
    in_hbm = lambda array: pltpu.with_memory_space_constraint(array, pltpu.HBM)
    scratch = [
        pltpu.VMEM(shape, BF16),
        pltpu.SemaphoreType.DMA((slots,)),
        pltpu.VMEM((rank // LANES, W, LANES), F32),
    ]
    return pl.pallas_call(
        functools.partial(moments_kernel, mode, orders, len(blocks)),
        in_specs=[SMEM_SPEC, SMEM_SPEC] + [HBM_SPEC] * len(blocks) + [VMEM_SPEC, VMEM_SPEC],
        out_specs=VMEM_SPEC,
        out_shape=jax.ShapeDtypeStruct((out_rows, rank), F32),
        scratch_shapes=scratch,
        compiler_params=pltpu.CompilerParams(vmem_limit_bytes=18 << 20),
        cost_estimate=pl.CostEstimate(
            flops=2 * slots * W**3 * rank, bytes_accessed=slots * W**3 * 2, transcendentals=0
        ),
    )(count, coords, *[in_hbm(part) for part in blocks], first, second)


def turn_kernel(mode, first, count_ref, blocks_ref, out_ref, held_ref, turned_ref, in_sems, out_sems, lanes_ref):
    count = jnp.clip(count_ref[0, 0] - first, 0, held_ref.shape[0])
    fetch_all(count, [blocks_ref], first, held_ref, in_sems)
    columns = W * W // LANES

    def turn(slot, carry):
        fetch(blocks_ref, 0, held_ref, in_sems, slot).wait()
        if mode == 1:
            for column in range(columns):
                lanes_ref[pl.ds(column, W, stride=STRIDE), :] = held_ref[
                    slot, :, column * LANES : (column + 1) * LANES
                ].astype(F32)
            low = lax.broadcasted_iota(jnp.int32, (columns, LANES), 1) < W
            for pair in range(W // 2):
                one = lanes_ref[2 * pair * STRIDE : 2 * pair * STRIDE + columns, :]
                two = lanes_ref[(2 * pair + 1) * STRIDE : (2 * pair + 1) * STRIDE + columns, :]
                even = jnp.where(low, one, pltpu.roll(two, W, 1)).astype(BF16)
                odd = jnp.where(low, pltpu.roll(one, W, 1), two).astype(BF16)
                turned_ref[slot, :, pair * LANES : (pair + 1) * LANES] = jnp.concatenate([even, odd], 0)
        else:
            for pair in range(W // 2):
                turned = held_ref[slot, :, pair * LANES : (pair + 1) * LANES].T
                turned_ref[slot, :, pair * LANES : (pair + 1) * LANES] = jnp.concatenate(
                    [turned[:W], turned[W:]], 1
                )
        fetch(turned_ref, slot, out_ref, out_sems, slot).start()
        return carry

    lax.fori_loop(0, count, turn, 0)

    def finish(slot, carry):
        fetch(turned_ref, slot, out_ref, out_sems, slot).wait()
        return carry

    lax.fori_loop(0, count, finish, 0)


def turned_blocks(mode, blocks, count, half):
    slots = blocks.shape[0] // 2
    shape = (slots, *blocks.shape[1:])
    return pl.pallas_call(
        functools.partial(turn_kernel, mode, half * slots),
        in_specs=[SMEM_SPEC, HBM_SPEC],
        out_specs=HBM_SPEC,
        out_shape=pltpu.HBM(shape, blocks.dtype),
        scratch_shapes=[
            pltpu.VMEM(shape, BF16),
            pltpu.VMEM(shape, BF16),
            pltpu.SemaphoreType.DMA((slots,)),
            pltpu.SemaphoreType.DMA((slots,)),
            pltpu.VMEM((W * STRIDE, LANES), F32),
        ],
        compiler_params=pltpu.CompilerParams(vmem_limit_bytes=14 << 20),
        cost_estimate=pl.CostEstimate(flops=0, bytes_accessed=blocks.size * 4, transcendentals=0),
    )(count, pltpu.with_memory_space_constraint(blocks, pltpu.HBM))


def exchange(rows, axes):
    devices = lax.axis_size(axes)
    parts = lax.all_to_all(rows, axes, split_axis=0, concat_axis=0, tiled=True)
    return parts.reshape(devices, rows.shape[0] // devices, rows.shape[1])


def spread_rows(rows, axes):
    devices = lax.axis_size(axes)
    return lax.all_to_all(jnp.tile(rows, (devices, 1)), axes, split_axis=0, concat_axis=0, tiled=True)


def swap(rows, axis, step):
    return lax.ppermute(rows, axis, [(i, i ^ step) for i in range(lax.axis_size(axis))])


def swap_pieces(rows, axis):
    devices = lax.axis_size(axis)
    each = rows.shape[0] // devices
    return [swap(rows[k * each : (k + 1) * each], axis, k) for k in range(1, devices)]


def swap_gather(rows, axis):
    even = [rows] + [swap(rows, axis, k) for k in range(2, lax.axis_size(axis), 2)]
    rows = jnp.concatenate(even, 0)
    return jnp.concatenate([rows, swap(rows, axis, 1)], 0)


def gram_local(factor):
    return jnp.dot(factor.T, factor, precision=HIGH, preferred_element_type=F32)


def exact_dot(left, right, contract):
    return lax.dot_general(left, right, (contract, ((), ())), precision=HIGH, preferred_element_type=F32)


def across_lanes(tile, lane):
    return jnp.broadcast_to(tile[:, lane : lane + 1], tile.shape)


def across_rows(tile, row):
    return jnp.broadcast_to(tile[row : row + 1, :], tile.shape)


def tree_sum(terms):
    while len(terms) > 1:
        terms = [a + b for a, b in zip(terms[::2], terms[1::2])]
    return terms[0]


def sweep_corner(entries):
    for k in range(0, 8, 2):
        at = lambda i, j: entries[(min(i, j), max(i, j))]
        a, o, d = at(k, k), at(k, k + 1), at(k + 1, k + 1)
        inverse = 1.0 / (a * d - o * o)
        w00, w01, w11 = d * inverse, -(o * inverse), a * inverse
        rest = [j for j in range(8) if j not in (k, k + 1)]
        top = {j: w00 * at(k, j) + w01 * at(k + 1, j) for j in rest}
        low = {j: w01 * at(k, j) + w11 * at(k + 1, j) for j in rest}
        swept = {(k, k): -w00, (k, k + 1): -w01, (k + 1, k + 1): -w11}
        for i in rest:
            swept[(min(k, i), max(k, i))] = top[i]
            swept[(min(k + 1, i), max(k + 1, i))] = low[i]
            for j in rest:
                if i <= j:
                    swept[(i, j)] = at(i, j) - (at(k, i) * top[j] + at(k + 1, i) * low[j])
        entries = swept
    return entries


def panel_inverse(tiles):
    shape = tiles[0].shape
    lane = lax.broadcasted_iota(jnp.int32, shape, 1)
    row = lax.broadcasted_iota(jnp.int32, shape, 0)
    for pivot in range(len(tiles)):
        tile = tiles[pivot]
        first = 8 * pivot
        columns = [across_lanes(tile, first + j) for j in range(8)]
        corner = sweep_corner({(i, j): across_rows(columns[j], i) for j in range(8) for i in range(j + 1)})
        here = (lane >= first) & (lane < first + 8)
        turned = jnp.where(here, jnp.where(lane - first == row, 1.0, 0.0), -tile)
        rows = [across_rows(turned, i) for i in range(8)]
        scaled = [tree_sum([corner[(min(i, j), max(i, j))] * rows[j] for j in range(8)]) for i in range(8)]
        swept = []
        for other, held in enumerate(tiles):
            if other == pivot:
                mine = scaled[0]
                for i in range(1, 8):
                    mine = jnp.where(row == i, scaled[i], mine)
            else:
                change = tree_sum([across_lanes(held, first + j) * scaled[j] for j in range(8)])
                mine = jnp.where(here, 0.0, held) - change
            swept.append(mine)
        tiles = swept
    return -jnp.concatenate(tiles, 0)


def on_diagonal(size):
    shape = (size, size)
    return lax.broadcasted_iota(jnp.int32, shape, 0) == lax.broadcasted_iota(jnp.int32, shape, 1)


def turned_down(across, diagonal):
    return jnp.sum(jnp.where(diagonal, across, 0.0), 1, keepdims=True)


def message_rows(devices):
    own = -(-3 * LANES // devices)
    return own, -(-(own + 2) // 8) * 8


def packed_blocks(gram):
    return jnp.concatenate([gram[:LANES, :LANES], gram[:LANES, LANES:], gram[LANES:, LANES:]], 0)


def pack_gram(message_ref, gram, squares, devices):
    own, rows = message_rows(devices)
    packed = packed_blocks(gram)
    if devices * own > 3 * LANES or rows > own + 2:
        message_ref[...] = jnp.zeros_like(message_ref)
    for e in range(own):
        held = min(devices, 3 * LANES - devices * e)
        message_ref[pl.ds(e, held, stride=rows), :] = packed[devices * e : devices * e + held]
    for half in range(2):
        part = squares[:, half * LANES : (half + 1) * LANES]
        message_ref[pl.ds(own + half, devices, stride=rows), :] = jnp.broadcast_to(part, (devices, LANES))


def fold_messages(parts_ref, spread_ref, devices):
    rows = message_rows(devices)[1]
    terms = [parts_ref[rows * d : rows * (d + 1), :] for d in range(devices)]
    total = functools.reduce(jnp.add, terms)
    for d in range(devices):
        spread_ref[rows * d : rows * (d + 1), :] = total


def unpack_gram(ref, devices):
    if ref.shape[1] != LANES:
        return ref[...]
    if ref.shape[0] == 3 * LANES:
        packed = ref[...]
    else:
        own, rows = message_rows(devices)
        pieces = []
        for e in range(own):
            held = min(devices, 3 * LANES - devices * e)
            pieces.append(ref[pl.ds(e, held, stride=rows), :])
        packed = jnp.concatenate(pieces, 0)
    first, corner, last = packed[:LANES], packed[LANES : 2 * LANES], packed[2 * LANES :]
    return jnp.concatenate(
        [jnp.concatenate([first, corner], 1), jnp.concatenate([corner.T, last], 1)], 0
    )


def swap_all(messages):
    return lax.all_to_all(messages, BOTH, split_axis=0, concat_axis=0, tiled=True)


def panel_gram_kernel(panel_ref, packed_ref):
    panel = panel_ref[...]
    packed = packed_blocks(exact_dot(panel, panel, ((0,), (0,))))
    rows = packed_ref.shape[0]
    packed_ref[...] = jnp.where(lax.axis_index("slab") % 2 == 0, packed[:rows], packed[rows:])


def fold_kernel(devices, parts_ref, spread_ref):
    fold_messages(parts_ref, spread_ref, devices)


def message_shape(devices):
    return jax.ShapeDtypeStruct((devices * message_rows(devices)[1], LANES), F32)


def panel_gram(panel):
    return pl.pallas_call(
        panel_gram_kernel,
        out_shape=jax.ShapeDtypeStruct((3 * LANES // 2, LANES), F32),
        compiler_params=pltpu.CompilerParams(vmem_limit_bytes=10 << 20),
    )(panel)


def fold(parts, devices):
    return pl.pallas_call(
        functools.partial(fold_kernel, devices),
        out_shape=message_shape(devices),
        compiler_params=pltpu.CompilerParams(vmem_limit_bytes=10 << 20),
    )(parts)


def on_diagonal(size):
    shape = (size, size)
    return lax.broadcasted_iota(jnp.int32, shape, 0) == lax.broadcasted_iota(jnp.int32, shape, 1)


def turned_down(across, diagonal):
    return jnp.sum(jnp.where(diagonal, across, 0.0), 1, keepdims=True)


def inverse_kernel(devices, totals, one_ref, one_scale_ref, two_ref, two_scale_ref, out_ref, held_ref):
    size = held_ref.shape[0]
    diagonal = on_diagonal(size)
    system = None
    for total, gram_ref, scale_ref in zip(totals, (one_ref, two_ref), (one_scale_ref, two_scale_ref)):
        inverse_scale = 1.0 / scale_ref[...]
        gram = unpack_gram(gram_ref, devices) * (inverse_scale / total) * turned_down(inverse_scale, diagonal)
        system = gram if system is None else system * gram
    across = lax.rsqrt(jnp.sum(jnp.where(diagonal, system, 0.0), 0, keepdims=True))
    down = turned_down(across, diagonal)
    held_ref[...] = system * across * down
    here = lax.broadcasted_iota(jnp.int32, (1, size), 1) < PANEL
    rest = size - PANEL

    def eliminate(step, carry):
        pivot = panel_inverse([held_ref[8 * g : 8 * g + 8, :PANEL] for g in range(PANEL // 8)])
        rows = held_ref[:PANEL, :]
        scaled = exact_dot(pivot, rows, ((1,), (0,)))
        minus = jnp.concatenate([-pivot, jnp.zeros((PANEL, rest), F32)], 1)
        scaled = jnp.where(here, minus, scaled)
        others = jnp.where(here, 0.0, held_ref[PANEL:, :]) - exact_dot(
            rows[:, PANEL:], scaled, ((0,), (0,))
        )
        held_ref[:rest, :] = pltpu.roll(others, rest, 1)
        held_ref[rest:, :] = pltpu.roll(scaled, rest, 1)
        return carry

    lax.fori_loop(0, size // PANEL, eliminate, 0)
    out_ref[...] = -held_ref[...] * across * down


def product_inverse(one, two, devices):
    rank = one[2].shape[1]
    return pl.pallas_call(
        functools.partial(inverse_kernel, devices, (one[1], two[1])),
        out_shape=jax.ShapeDtypeStruct((rank, rank), F32),
        scratch_shapes=[pltpu.VMEM((rank, rank), F32)],
        compiler_params=pltpu.CompilerParams(vmem_limit_bytes=10 << 20),
        cost_estimate=pl.CostEstimate(flops=10**10, bytes_accessed=3 << 18, transcendentals=0),
    )(one[0], one[2], two[0], two[2])


def solve_kernel(devices, stacked, parts, *refs):
    inverse_ref, outs = refs[parts], refs[parts + 1 :]
    if stacked:
        terms = [refs[0][part] for part in range(refs[0].shape[0])]
    else:
        terms = [ref[...] for ref in refs[:parts]]
    raw = exact_dot(functools.reduce(jnp.add, terms), inverse_ref[...], ((1,), (0,)))
    outs[0][...] = raw
    if len(outs) > 1:
        squares = jnp.sum(raw * raw, 0, keepdims=True)
        pack_gram(outs[1], exact_dot(raw, raw, ((0,), (0,))), squares, devices)


def solve_swapped(own, others, inverse, devices):
    rows, rank = others[0].shape
    whole = pl.BlockSpec((rows, rank), lambda step: (0, 0))
    square = pl.BlockSpec((rank, rank), lambda step: (0, 0))
    messages = message_shape(devices)
    return pl.pallas_call(
        functools.partial(solve_kernel, devices, False, 1 + len(others)),
        grid=(1,),
        in_specs=[whole] * (1 + len(others)) + [square],
        out_specs=[whole, pl.BlockSpec(messages.shape, lambda step: (0, 0))],
        out_shape=[jax.ShapeDtypeStruct((rows, rank), F32), messages],
        compiler_params=pltpu.CompilerParams(vmem_limit_bytes=12 << 20),
    )(own, *others, inverse)


def solve_stacked(parts, inverse, devices, with_gram):
    out_shape = [jax.ShapeDtypeStruct(parts.shape[1:], F32)]
    if with_gram:
        out_shape.append(message_shape(devices))
    return pl.pallas_call(
        functools.partial(solve_kernel, devices, True, 1),
        out_shape=out_shape,
        compiler_params=pltpu.CompilerParams(vmem_limit_bytes=10 << 20),
    )(parts, inverse)


def scale_kernel(devices, row_total, parts_ref, raw_ref, factor_ref, rounded_ref, scale_ref):
    own, rows = message_rows(devices)
    total = functools.reduce(jnp.add, [parts_ref[rows * d + own : rows * d + own + 2, :] for d in range(devices)])
    squares = jnp.concatenate([total[:1], total[1:2]], 1)
    scale = jnp.sqrt(squares / row_total + EPS)
    scale_ref[...] = scale
    factor = raw_ref[...] / scale
    factor_ref[...] = factor
    rounded_ref[...] = factor.astype(BF16)


def scale_rows(messages, raw, row_total, devices):
    return pl.pallas_call(
        functools.partial(scale_kernel, devices, row_total),
        out_shape=[
            jax.ShapeDtypeStruct(raw.shape, F32),
            jax.ShapeDtypeStruct(raw.shape, BF16),
            jax.ShapeDtypeStruct((1, raw.shape[1]), F32),
        ],
        compiler_params=pltpu.CompilerParams(vmem_limit_bytes=10 << 20),
    )(messages, raw)


def on_device(blocks, coords, counts, b_init, c_init):
    slab_count = lax.axis_size("slab")
    grid_count = lax.axis_size("grid")
    local_blocks = blocks[0, 0]
    doc_rows = IBP * W
    term_rows = JBP * W
    doc_total = doc_rows * slab_count
    term_total = term_rows * grid_count
    month_total = c_init.shape[0]
    devices = slab_count * grid_count
    ones = jnp.ones((1, c_init.shape[1]), F32)
    even = [b_init] + [swap(b_init, "slab", k) for k in range(2, slab_count, 2)]
    held_blocks, even[1] = lax.optimization_barrier((local_blocks, even[1]))
    terms_one = turned_blocks(1, held_blocks, counts, 0)
    even, terms_one = lax.optimization_barrier((even, terms_one))
    even = jnp.concatenate(even, 0)
    term_panel = jnp.concatenate([even, swap(even, "slab", 1)], 0)
    own_gram_b = panel_gram(term_panel)
    own_gram_b, term_panel = lax.optimization_barrier((own_gram_b, term_panel))
    grams_b = [own_gram_b] + [swap(own_gram_b, "grid", k) for k in range(1, grid_count)]
    moments_a = block_moments(
        0, (TERM_ORDER, None, DOC_ORDER), [local_blocks], coords, counts, term_panel, c_init, doc_rows
    )
    grams_b, moments_a = lax.optimization_barrier((grams_b, moments_a))
    others_a = swap_pieces(moments_a, "grid")
    half_b = functools.reduce(jnp.add, grams_b)
    other_b = swap(half_b, "slab", 1)
    even_device = lax.axis_index("slab") % 2 == 0
    packed_b = jnp.concatenate(
        [jnp.where(even_device, half_b, other_b), jnp.where(even_device, other_b, half_b)], 0
    )
    gram_b = (packed_b, term_total, ones)
    c_held, _ = lax.optimization_barrier((c_init, moments_a))
    gram_c = (gram_local(c_held), month_total, ones)
    inverse_a = product_inverse(gram_b, gram_c, devices)
    held_blocks, inverse_a = lax.optimization_barrier((local_blocks, inverse_a))
    terms_two = turned_blocks(1, held_blocks, counts, 1)
    inverse_a, terms_two = lax.optimization_barrier((inverse_a, terms_two))
    raw_a, messages_a = solve_swapped(moments_a, others_a, inverse_a, devices)
    held_blocks, messages_a = lax.optimization_barrier((local_blocks, messages_a))
    months_one = turned_blocks(2, held_blocks, counts, 0)
    messages_a, months_one = lax.optimization_barrier((swap_all(messages_a), months_one))
    factor_a, rounded_a, scale_a = scale_rows(messages_a, raw_a, doc_total, devices)
    pieces = [rounded_a] + [swap(rounded_a, "grid", k) for k in range(1, grid_count)]
    messages_a, pieces[1] = lax.optimization_barrier((messages_a, pieces[1]))
    doc_panel = jnp.concatenate(pieces, 0)
    spread_a = fold(messages_a, devices)
    gram_a = (swap_all(spread_a), doc_total, scale_a)

    moments_b = block_moments(
        1, (DOC_ORDER, None, None), [terms_one, terms_two], coords, counts, doc_panel, c_init, term_rows
    )
    parts_b = exchange(moments_b, "slab")
    inverse_b = product_inverse(gram_a, gram_c, devices)
    raw_b, messages_n = solve_stacked(parts_b, inverse_b, devices, True)
    held_blocks, messages_n = lax.optimization_barrier((local_blocks, messages_n))
    months_two = turned_blocks(2, held_blocks, counts, 1)
    messages_n, months_two = lax.optimization_barrier((swap_all(messages_n), months_two))
    factor_b, rounded_b, scale_b = scale_rows(messages_n, raw_b, term_total, devices)
    term_panel_new = swap_gather(rounded_b, "slab")
    messages_n, _ = lax.optimization_barrier((messages_n, rounded_b))
    spread_n = fold(messages_n, devices)
    gram_bn = (swap_all(spread_n), term_total, scale_b)

    moments_c = block_moments(
        2, (TERM_ORDER, DOC_ORDER, None), [months_one, months_two], coords, counts, term_panel_new, doc_panel, month_total
    )
    parts_c = exchange(moments_c, BOTH)
    inverse_c = product_inverse(gram_a, gram_bn, devices)
    (raw_own,) = solve_stacked(parts_c, inverse_c, devices, False)
    raw_c = spread_rows(raw_own, BOTH)
    column_scale = jnp.sqrt(jnp.mean(raw_c * raw_c, axis=0) + EPS)
    return (factor_a, factor_b, raw_c / column_scale)


def solution(mesh):
    in_specs = (
        P("slab", "grid", None, None, None),
        P("slab", "grid", None, None),
        P("slab", "grid"),
        P(("slab", "grid"), None),
        P(),
    )
    out_specs = (P(("slab", "grid"), None), P(("slab", "grid"), None), P())
    return jax.shard_map(
        on_device, mesh=mesh, in_specs=in_specs, out_specs=out_specs, check_vma=False
    )
```

```python
import functools

import jax
import jax.numpy as jnp
from jax import lax
from jax.experimental import pallas as pl
from jax.experimental.pallas import tpu as pltpu
from jax.sharding import PartitionSpec as P

W = 64
IBP = 16
JBP = 16
LANES = 128
STRIDE = 40
PANEL = 128
GROUP = 4

HIGH = lax.Precision.HIGHEST
EPS = 1e-05
BOTH = ("slab", "grid")
TERM_ORDER, DOC_ORDER = ("slab", True), ("grid", False)
F32 = jnp.float32
BF16 = jnp.bfloat16


def product_rows(first, second, start):
    rank = first.shape[1]
    pieces = []
    for row in range(start, start + GROUP):
        spread = jnp.broadcast_to(first[row : row + 1, :], (16, rank)).astype(BF16)
        pieces.append((second * spread[None]).reshape(W, rank))
    return jnp.concatenate(pieces, 0)


def slot_rows(coords_ref, slot, mode, order):
    block = coords_ref[0, 0, slot, mode]
    if order is not None:
        axis, paired = order
        devices = lax.axis_size(axis)
        each = IBP // devices
        place = (block // each) ^ lax.axis_index(axis)
        if paired:
            place = place // 2 + place % 2 * (devices // 2)
        block = place * each + block % each
    return pl.multiple_of(block * W, W)


def fetch(source_ref, source, held_ref, sems, slot):
    return pltpu.make_async_copy(source_ref.at[source], held_ref.at[slot], sems.at[slot])


def fetch_all(count, block_refs, first, held_ref, sems):
    each = block_refs[0].shape[0]
    for slot in range(held_ref.shape[0]):

        @pl.when(slot < count)
        def _():
            fetch(block_refs[slot // each], first + slot % each, held_ref, sems, slot).start()


def moments_kernel(mode, orders, arrays, count_ref, coords_ref, *refs):
    block_refs, refs = refs[:arrays], refs[arrays:]
    first_ref, second_ref, out_ref, held_ref, sems, order_ref = refs
    rank = out_ref.shape[1]
    count = count_ref[0, 0]
    fetch_all(count, block_refs, 0, held_ref, sems)
    out_ref[...] = jnp.zeros_like(out_ref)
    spread_mode, tile_mode = ((1, 2), (0, 2), (1, 0))[mode]

    def add_block(slot, carry):
        first = first_ref[pl.ds(slot_rows(coords_ref, slot, spread_mode, orders[0]), W), :].astype(BF16).astype(F32)
        second = second_ref[pl.ds(slot_rows(coords_ref, slot, tile_mode, orders[1]), W), :].astype(BF16).reshape(4, 16, rank)
        target = slot_rows(coords_ref, slot, mode, orders[2])
        fetch(block_refs[0], 0, held_ref, sems, slot).wait()
        total = jnp.zeros((W, rank), F32)
        for step in range(W // GROUP):
            left = held_ref[slot, :, step * GROUP * W : (step + 1) * GROUP * W]
            right = product_rows(first, second, step * GROUP)
            total = total + jnp.dot(left, right, preferred_element_type=F32)
        if mode == 1:
            halves = []
            for part in range(rank // LANES):
                for parity in range(2):
                    order_ref[part, pl.ds(parity, W // 2, stride=2), :] = total[
                        parity * W // 2 : (parity + 1) * W // 2, part * LANES : (part + 1) * LANES
                    ]
                halves.append(order_ref[part])
            total = jnp.concatenate(halves, 1)
        out_ref[pl.ds(target, W), :] += total
        return carry

    lax.fori_loop(0, count, add_block, 0)


SMEM_SPEC = pl.BlockSpec(memory_space=pltpu.SMEM)
HBM_SPEC = pl.BlockSpec(memory_space=pltpu.HBM)
VMEM_SPEC = pl.BlockSpec(memory_space=pltpu.VMEM)


def block_moments(mode, orders, blocks, coords, count, first, second, out_rows):
    slots = sum(part.shape[0] for part in blocks)
    shape = (slots, *blocks[0].shape[1:])
    rank = first.shape[1]
    in_hbm = lambda array: pltpu.with_memory_space_constraint(array, pltpu.HBM)
    scratch = [
        pltpu.VMEM(shape, BF16),
        pltpu.SemaphoreType.DMA((slots,)),
        pltpu.VMEM((rank // LANES, W, LANES), F32),
    ]
    return pl.pallas_call(
        functools.partial(moments_kernel, mode, orders, len(blocks)),
        in_specs=[SMEM_SPEC, SMEM_SPEC] + [HBM_SPEC] * len(blocks) + [VMEM_SPEC, VMEM_SPEC],
        out_specs=VMEM_SPEC,
        out_shape=jax.ShapeDtypeStruct((out_rows, rank), F32),
        scratch_shapes=scratch,
        compiler_params=pltpu.CompilerParams(vmem_limit_bytes=18 << 20),
        cost_estimate=pl.CostEstimate(
            flops=2 * slots * W**3 * rank, bytes_accessed=slots * W**3 * 2, transcendentals=0
        ),
    )(count, coords, *[in_hbm(part) for part in blocks], first, second)


def turn_kernel(mode, first, count_ref, blocks_ref, out_ref, held_ref, turned_ref, in_sems, out_sems, lanes_ref):
    count = jnp.clip(count_ref[0, 0] - first, 0, held_ref.shape[0])
    fetch_all(count, [blocks_ref], first, held_ref, in_sems)
    columns = W * W // LANES

    def turn(slot, carry):
        fetch(blocks_ref, 0, held_ref, in_sems, slot).wait()
        if mode == 1:
            for column in range(columns):
                lanes_ref[pl.ds(column, W, stride=STRIDE), :] = held_ref[
                    slot, :, column * LANES : (column + 1) * LANES
                ].astype(F32)
            low = lax.broadcasted_iota(jnp.int32, (columns, LANES), 1) < W
            for pair in range(W // 2):
                one = lanes_ref[2 * pair * STRIDE : 2 * pair * STRIDE + columns, :]
                two = lanes_ref[(2 * pair + 1) * STRIDE : (2 * pair + 1) * STRIDE + columns, :]
                even = jnp.where(low, one, pltpu.roll(two, W, 1)).astype(BF16)
                odd = jnp.where(low, pltpu.roll(one, W, 1), two).astype(BF16)
                turned_ref[slot, :, pair * LANES : (pair + 1) * LANES] = jnp.concatenate([even, odd], 0)
        else:
            for pair in range(W // 2):
                turned = held_ref[slot, :, pair * LANES : (pair + 1) * LANES].T
                turned_ref[slot, :, pair * LANES : (pair + 1) * LANES] = jnp.concatenate(
                    [turned[:W], turned[W:]], 1
                )
        fetch(turned_ref, slot, out_ref, out_sems, slot).start()
        return carry

    lax.fori_loop(0, count, turn, 0)

    def finish(slot, carry):
        fetch(turned_ref, slot, out_ref, out_sems, slot).wait()
        return carry

    lax.fori_loop(0, count, finish, 0)


def turned_blocks(mode, blocks, count, half):
    slots = blocks.shape[0] // 2
    shape = (slots, *blocks.shape[1:])
    return pl.pallas_call(
        functools.partial(turn_kernel, mode, half * slots),
        in_specs=[SMEM_SPEC, HBM_SPEC],
        out_specs=HBM_SPEC,
        out_shape=pltpu.HBM(shape, blocks.dtype),
        scratch_shapes=[
            pltpu.VMEM(shape, BF16),
            pltpu.VMEM(shape, BF16),
            pltpu.SemaphoreType.DMA((slots,)),
            pltpu.SemaphoreType.DMA((slots,)),
            pltpu.VMEM((W * STRIDE, LANES), F32),
        ],
        compiler_params=pltpu.CompilerParams(vmem_limit_bytes=14 << 20),
        cost_estimate=pl.CostEstimate(flops=0, bytes_accessed=blocks.size * 4, transcendentals=0),
    )(count, pltpu.with_memory_space_constraint(blocks, pltpu.HBM))


def exchange(rows, axes):
    devices = lax.axis_size(axes)
    parts = lax.all_to_all(rows, axes, split_axis=0, concat_axis=0, tiled=True)
    return parts.reshape(devices, rows.shape[0] // devices, rows.shape[1])


def spread_rows(rows, axes):
    devices = lax.axis_size(axes)
    return lax.all_to_all(jnp.tile(rows, (devices, 1)), axes, split_axis=0, concat_axis=0, tiled=True)


def swap(rows, axis, step):
    return lax.ppermute(rows, axis, [(i, i ^ step) for i in range(lax.axis_size(axis))])


def swap_pieces(rows, axis):
    devices = lax.axis_size(axis)
    each = rows.shape[0] // devices
    return [swap(rows[k * each : (k + 1) * each], axis, k) for k in range(1, devices)]


def swap_gather(rows, axis):
    even = [rows] + [swap(rows, axis, k) for k in range(2, lax.axis_size(axis), 2)]
    rows = jnp.concatenate(even, 0)
    return jnp.concatenate([rows, swap(rows, axis, 1)], 0)


def gram_local(factor):
    return jnp.dot(factor.T, factor, precision=HIGH, preferred_element_type=F32)


def exact_dot(left, right, contract):
    return lax.dot_general(left, right, (contract, ((), ())), precision=HIGH, preferred_element_type=F32)


def across_lanes(tile, lane):
    return jnp.broadcast_to(tile[:, lane : lane + 1], tile.shape)


def across_rows(tile, row):
    return jnp.broadcast_to(tile[row : row + 1, :], tile.shape)


def tree_sum(terms):
    while len(terms) > 1:
        terms = [a + b for a, b in zip(terms[::2], terms[1::2])]
    return terms[0]


def sweep_corner(entries):
    for k in range(0, 8, 2):
        at = lambda i, j: entries[(min(i, j), max(i, j))]
        a, o, d = at(k, k), at(k, k + 1), at(k + 1, k + 1)
        inverse = 1.0 / (a * d - o * o)
        w00, w01, w11 = d * inverse, -(o * inverse), a * inverse
        rest = [j for j in range(8) if j not in (k, k + 1)]
        top = {j: w00 * at(k, j) + w01 * at(k + 1, j) for j in rest}
        low = {j: w01 * at(k, j) + w11 * at(k + 1, j) for j in rest}
        swept = {(k, k): -w00, (k, k + 1): -w01, (k + 1, k + 1): -w11}
        for i in rest:
            swept[(min(k, i), max(k, i))] = top[i]
            swept[(min(k + 1, i), max(k + 1, i))] = low[i]
            for j in rest:
                if i <= j:
                    swept[(i, j)] = at(i, j) - (at(k, i) * top[j] + at(k + 1, i) * low[j])
        entries = swept
    return entries


def panel_inverse(tiles):
    shape = tiles[0].shape
    lane = lax.broadcasted_iota(jnp.int32, shape, 1)
    row = lax.broadcasted_iota(jnp.int32, shape, 0)
    for pivot in range(len(tiles)):
        tile = tiles[pivot]
        first = 8 * pivot
        columns = [across_lanes(tile, first + j) for j in range(8)]
        corner = sweep_corner({(i, j): across_rows(columns[j], i) for j in range(8) for i in range(j + 1)})
        here = (lane >= first) & (lane < first + 8)
        turned = jnp.where(here, jnp.where(lane - first == row, 1.0, 0.0), -tile)
        rows = [across_rows(turned, i) for i in range(8)]
        scaled = [tree_sum([corner[(min(i, j), max(i, j))] * rows[j] for j in range(8)]) for i in range(8)]
        swept = []
        for other, held in enumerate(tiles):
            if other == pivot:
                mine = scaled[0]
                for i in range(1, 8):
                    mine = jnp.where(row == i, scaled[i], mine)
            else:
                change = tree_sum([across_lanes(held, first + j) * scaled[j] for j in range(8)])
                mine = jnp.where(here, 0.0, held) - change
            swept.append(mine)
        tiles = swept
    return -jnp.concatenate(tiles, 0)


def on_diagonal(size):
    shape = (size, size)
    return lax.broadcasted_iota(jnp.int32, shape, 0) == lax.broadcasted_iota(jnp.int32, shape, 1)


def turned_down(across, diagonal):
    return jnp.sum(jnp.where(diagonal, across, 0.0), 1, keepdims=True)


def message_rows(devices):
    own = -(-3 * LANES // devices)
    return own, -(-(own + 2) // 8) * 8


def packed_blocks(gram):
    return jnp.concatenate([gram[:LANES, :LANES], gram[:LANES, LANES:], gram[LANES:, LANES:]], 0)


def pack_gram(message_ref, gram, squares, devices):
    own, rows = message_rows(devices)
    packed = packed_blocks(gram)
    if devices * own > 3 * LANES or rows > own + 2:
        message_ref[...] = jnp.zeros_like(message_ref)
    for e in range(own):
        held = min(devices, 3 * LANES - devices * e)
        message_ref[pl.ds(e, held, stride=rows), :] = packed[devices * e : devices * e + held]
    for half in range(2):
        part = squares[:, half * LANES : (half + 1) * LANES]
        message_ref[pl.ds(own + half, devices, stride=rows), :] = jnp.broadcast_to(part, (devices, LANES))


def fold_messages(parts_ref, spread_ref, devices):
    rows = message_rows(devices)[1]
    terms = [parts_ref[rows * d : rows * (d + 1), :] for d in range(devices)]
    total = functools.reduce(jnp.add, terms)
    for d in range(devices):
        spread_ref[rows * d : rows * (d + 1), :] = total


def unpack_gram(ref, devices):
    if ref.shape[1] != LANES:
        return ref[...]
    if ref.shape[0] == 3 * LANES:
        packed = ref[...]
    else:
        own, rows = message_rows(devices)
        pieces = []
        for e in range(own):
            held = min(devices, 3 * LANES - devices * e)
            pieces.append(ref[pl.ds(e, held, stride=rows), :])
        packed = jnp.concatenate(pieces, 0)
    first, corner, last = packed[:LANES], packed[LANES : 2 * LANES], packed[2 * LANES :]
    return jnp.concatenate(
        [jnp.concatenate([first, corner], 1), jnp.concatenate([corner.T, last], 1)], 0
    )


def swap_all(messages):
    return lax.all_to_all(messages, BOTH, split_axis=0, concat_axis=0, tiled=True)


def panel_gram_kernel(panel_ref, packed_ref):
    panel = panel_ref[...]
    packed = packed_blocks(exact_dot(panel, panel, ((0,), (0,))))
    rows = packed_ref.shape[0]
    packed_ref[...] = jnp.where(lax.axis_index("slab") % 2 == 0, packed[:rows], packed[rows:])


def fold_kernel(devices, parts_ref, spread_ref):
    fold_messages(parts_ref, spread_ref, devices)


def message_shape(devices):
    return jax.ShapeDtypeStruct((devices * message_rows(devices)[1], LANES), F32)


def panel_gram(panel):
    return pl.pallas_call(
        panel_gram_kernel,
        out_shape=jax.ShapeDtypeStruct((3 * LANES // 2, LANES), F32),
        compiler_params=pltpu.CompilerParams(vmem_limit_bytes=10 << 20),
    )(panel)


def fold(parts, devices):
    return pl.pallas_call(
        functools.partial(fold_kernel, devices),
        out_shape=message_shape(devices),
        compiler_params=pltpu.CompilerParams(vmem_limit_bytes=10 << 20),
    )(parts)


def on_diagonal(size):
    shape = (size, size)
    return lax.broadcasted_iota(jnp.int32, shape, 0) == lax.broadcasted_iota(jnp.int32, shape, 1)


def turned_down(across, diagonal):
    return jnp.sum(jnp.where(diagonal, across, 0.0), 1, keepdims=True)


def inverse_kernel(devices, totals, one_ref, one_scale_ref, two_ref, two_scale_ref, out_ref, held_ref):
    size = held_ref.shape[0]
    diagonal = on_diagonal(size)
    system = None
    for total, gram_ref, scale_ref in zip(totals, (one_ref, two_ref), (one_scale_ref, two_scale_ref)):
        inverse_scale = 1.0 / scale_ref[...]
        gram = unpack_gram(gram_ref, devices) * (inverse_scale / total) * turned_down(inverse_scale, diagonal)
        system = gram if system is None else system * gram
    across = lax.rsqrt(jnp.sum(jnp.where(diagonal, system, 0.0), 0, keepdims=True))
    down = turned_down(across, diagonal)
    held_ref[...] = system * across * down
    here = lax.broadcasted_iota(jnp.int32, (1, size), 1) < PANEL
    rest = size - PANEL

    def eliminate(step, carry):
        pivot = panel_inverse([held_ref[8 * g : 8 * g + 8, :PANEL] for g in range(PANEL // 8)])
        rows = held_ref[:PANEL, :]
        scaled = exact_dot(pivot, rows, ((1,), (0,)))
        minus = jnp.concatenate([-pivot, jnp.zeros((PANEL, rest), F32)], 1)
        scaled = jnp.where(here, minus, scaled)
        others = jnp.where(here, 0.0, held_ref[PANEL:, :]) - exact_dot(
            rows[:, PANEL:], scaled, ((0,), (0,))
        )
        held_ref[:rest, :] = pltpu.roll(others, rest, 1)
        held_ref[rest:, :] = pltpu.roll(scaled, rest, 1)
        return carry

    lax.fori_loop(0, size // PANEL, eliminate, 0)
    out_ref[...] = -held_ref[...] * across * down


def product_inverse(one, two, devices):
    rank = one[2].shape[1]
    return pl.pallas_call(
        functools.partial(inverse_kernel, devices, (one[1], two[1])),
        out_shape=jax.ShapeDtypeStruct((rank, rank), F32),
        scratch_shapes=[pltpu.VMEM((rank, rank), F32)],
        compiler_params=pltpu.CompilerParams(vmem_limit_bytes=10 << 20),
        cost_estimate=pl.CostEstimate(flops=10**10, bytes_accessed=3 << 18, transcendentals=0),
    )(one[0], one[2], two[0], two[2])


def solve_kernel(devices, stacked, parts, *refs):
    inverse_ref, outs = refs[parts], refs[parts + 1 :]
    if stacked:
        terms = [refs[0][part] for part in range(refs[0].shape[0])]
    else:
        terms = [ref[...] for ref in refs[:parts]]
    raw = exact_dot(functools.reduce(jnp.add, terms), inverse_ref[...], ((1,), (0,)))
    outs[0][...] = raw
    if len(outs) > 1:
        squares = jnp.sum(raw * raw, 0, keepdims=True)
        pack_gram(outs[1], exact_dot(raw, raw, ((0,), (0,))), squares, devices)


def solve_swapped(own, others, inverse, devices):
    rows, rank = others[0].shape
    whole = pl.BlockSpec((rows, rank), lambda step: (0, 0))
    square = pl.BlockSpec((rank, rank), lambda step: (0, 0))
    messages = message_shape(devices)
    return pl.pallas_call(
        functools.partial(solve_kernel, devices, False, 1 + len(others)),
        grid=(1,),
        in_specs=[whole] * (1 + len(others)) + [square],
        out_specs=[whole, pl.BlockSpec(messages.shape, lambda step: (0, 0))],
        out_shape=[jax.ShapeDtypeStruct((rows, rank), F32), messages],
        compiler_params=pltpu.CompilerParams(vmem_limit_bytes=12 << 20),
    )(own, *others, inverse)


def solve_stacked(parts, inverse, devices, with_gram):
    out_shape = [jax.ShapeDtypeStruct(parts.shape[1:], F32)]
    if with_gram:
        out_shape.append(message_shape(devices))
    return pl.pallas_call(
        functools.partial(solve_kernel, devices, True, 1),
        out_shape=out_shape,
        compiler_params=pltpu.CompilerParams(vmem_limit_bytes=10 << 20),
    )(parts, inverse)


def scale_kernel(devices, row_total, parts_ref, raw_ref, factor_ref, rounded_ref, scale_ref):
    own, rows = message_rows(devices)
    total = functools.reduce(jnp.add, [parts_ref[rows * d + own : rows * d + own + 2, :] for d in range(devices)])
    squares = jnp.concatenate([total[:1], total[1:2]], 1)
    scale = jnp.sqrt(squares / row_total + EPS)
    scale_ref[...] = scale
    factor = raw_ref[...] / scale
    factor_ref[...] = factor
    rounded_ref[...] = factor.astype(BF16)


def scale_rows(messages, raw, row_total, devices):
    return pl.pallas_call(
        functools.partial(scale_kernel, devices, row_total),
        out_shape=[
            jax.ShapeDtypeStruct(raw.shape, F32),
            jax.ShapeDtypeStruct(raw.shape, BF16),
            jax.ShapeDtypeStruct((1, raw.shape[1]), F32),
        ],
        compiler_params=pltpu.CompilerParams(vmem_limit_bytes=10 << 20),
    )(messages, raw)


def on_device(blocks, coords, counts, b_init, c_init):
    slab_count = lax.axis_size("slab")
    grid_count = lax.axis_size("grid")
    local_blocks = blocks[0, 0]
    doc_rows = IBP * W
    term_rows = JBP * W
    doc_total = doc_rows * slab_count
    term_total = term_rows * grid_count
    month_total = c_init.shape[0]
    devices = slab_count * grid_count
    ones = jnp.ones((1, c_init.shape[1]), F32)
    even = [b_init] + [swap(b_init, "slab", k) for k in range(2, slab_count, 2)]
    held_blocks, even[1] = lax.optimization_barrier((local_blocks, even[1]))
    terms_one = turned_blocks(1, held_blocks, counts, 0)
    even, terms_one = lax.optimization_barrier((even, terms_one))
    even = jnp.concatenate(even, 0)
    term_panel = jnp.concatenate([even, swap(even, "slab", 1)], 0)
    own_gram_b = panel_gram(term_panel)
    own_gram_b, term_panel = lax.optimization_barrier((own_gram_b, term_panel))
    grams_b = [own_gram_b] + [swap(own_gram_b, "grid", k) for k in range(1, grid_count)]
    moments_a = block_moments(
        0, (TERM_ORDER, None, DOC_ORDER), [local_blocks], coords, counts, term_panel, c_init, doc_rows
    )
    grams_b, moments_a = lax.optimization_barrier((grams_b, moments_a))
    others_a = swap_pieces(moments_a, "grid")
    half_b = functools.reduce(jnp.add, grams_b)
    c_held, other_b = lax.optimization_barrier((c_init, swap(half_b, "slab", 1)))
    even_device = lax.axis_index("slab") % 2 == 0
    packed_b = jnp.concatenate(
        [jnp.where(even_device, half_b, other_b), jnp.where(even_device, other_b, half_b)], 0
    )
    gram_b = (packed_b, term_total, ones)
    gram_c = (gram_local(c_held), month_total, ones)
    inverse_a = product_inverse(gram_b, gram_c, devices)
    held_blocks, inverse_a = lax.optimization_barrier((local_blocks, inverse_a))
    terms_two = turned_blocks(1, held_blocks, counts, 1)
    inverse_a, terms_two = lax.optimization_barrier((inverse_a, terms_two))
    raw_a, messages_a = solve_swapped(moments_a, others_a, inverse_a, devices)
    held_blocks, messages_a = lax.optimization_barrier((local_blocks, messages_a))
    months_one = turned_blocks(2, held_blocks, counts, 0)
    messages_a, months_one = lax.optimization_barrier((swap_all(messages_a), months_one))
    factor_a, rounded_a, scale_a = scale_rows(messages_a, raw_a, doc_total, devices)
    pieces = [rounded_a] + [swap(rounded_a, "grid", k) for k in range(1, grid_count)]
    messages_a, pieces[1] = lax.optimization_barrier((messages_a, pieces[1]))
    doc_panel = jnp.concatenate(pieces, 0)
    spread_a = fold(messages_a, devices)
    gram_a = (swap_all(spread_a), doc_total, scale_a)

    moments_b = block_moments(
        1, (DOC_ORDER, None, None), [terms_one, terms_two], coords, counts, doc_panel, c_init, term_rows
    )
    parts_b = exchange(moments_b, "slab")
    inverse_b = product_inverse(gram_a, gram_c, devices)
    raw_b, messages_n = solve_stacked(parts_b, inverse_b, devices, True)
    held_blocks, messages_n = lax.optimization_barrier((local_blocks, messages_n))
    months_two = turned_blocks(2, held_blocks, counts, 1)
    messages_n, months_two = lax.optimization_barrier((swap_all(messages_n), months_two))
    factor_b, rounded_b, scale_b = scale_rows(messages_n, raw_b, term_total, devices)
    term_panel_new = swap_gather(rounded_b, "slab")
    messages_n, _ = lax.optimization_barrier((messages_n, rounded_b))
    spread_n = fold(messages_n, devices)
    gram_bn = (swap_all(spread_n), term_total, scale_b)

    moments_c = block_moments(
        2, (TERM_ORDER, DOC_ORDER, None), [months_one, months_two], coords, counts, term_panel_new, doc_panel, month_total
    )
    parts_c = exchange(moments_c, BOTH)
    inverse_c = product_inverse(gram_a, gram_bn, devices)
    (raw_own,) = solve_stacked(parts_c, inverse_c, devices, False)
    raw_c = spread_rows(raw_own, BOTH)
    column_scale = jnp.sqrt(jnp.mean(raw_c * raw_c, axis=0) + EPS)
    return (factor_a, factor_b, raw_c / column_scale)


def solution(mesh):
    in_specs = (
        P("slab", "grid", None, None, None),
        P("slab", "grid", None, None),
        P("slab", "grid"),
        P(("slab", "grid"), None),
        P(),
    )
    out_specs = (P(("slab", "grid"), None), P(("slab", "grid"), None), P())
    return jax.shard_map(
        on_device, mesh=mesh, in_specs=in_specs, out_specs=out_specs, check_vma=False
    )
```
